256 devices in a mesh: img: 32 (over z_hi, x, core), fou: 8 (over z_lo, y).
Axes of the slice: x: 4, y: 4, z: 8 (z_hi: 4, z_lo: 2; z = z_hi * 2 + z_lo), core: 2. Of those that a mesh axis runs over, the one named last changes fastest.
Arguments:
- sky_estimate: float32 [4, 2048, 2048], P(None, 'img', 'fou'), may hold values from 0 to 2
- dual_coeffs: bfloat16 [4, 9, 2048, 2048], P(None, None, 'img', 'fou'), may hold values from -2 to 2
- dirty_image: float32 [4, 2048, 2048], P(None, 'img', 'fou'), may hold values from -4 to 4
- filters: float32 [8, 17], replicated, may hold values from -1.5 to 1.5
- thresholds: float32 [9], replicated, may hold values from 0.2 to 1.2
- facet_rows: int32 [32], P('img'), may hold values from 16 to 64, as said below
- tile_slots: int32 [4, 32, 6], P(None, 'img'), may hold values from 0 to 31, as said below
- tile_count: int32 [4, 32], P(None, 'img'), may hold values from 1 to 6, as said below
- gram_tiles: bfloat16 [4, 32, 6, 64, 64], P(None, 'img'), may hold values from -4 to 4
Outputs:
- image_next: float32 [4, 2048, 2048], P(None, 'img', 'fou')
- dual_next: bfloat16 [4, 9, 2048, 2048], P(None, None, 'img', 'fou')
The draws below stay inside these ranges and needn't reach their ends.
Inputs may be any that keep to these rules, and one draw needn't show every extreme that they name: `facet_rows`: facet f covers image rows f * 64 to (f + 1) * 64 - 1; some facet is full. `tile_slots`: the 6 entries of one channel and v-tile are distinct. `tile_count`: slots at or beyond the count hold no tile; in each channel some v-tile uses all 6 slots.
All inputs are finite; a program needn't handle non-finite values.
Results may differ from the reference program's by a relative error of at most 0.005.
Values may be sent and summed in bfloat16 or wider, within the bound.
No kernel may reach another device: no remote copies, remote signals or barrier semaphores. Data moves between devices by JAX's collectives and lax.ppermute only.
A program may use at most 64 MiB of HBM per device.

```python
import math
import jax
import jax.numpy as jnp
from jax import lax

PIXELS = 2048
CHANNELS = 4
FRAMES = 9
RADIUS = 8
BLOCK = 64
SLOTS = 6
BLOCKS = 32
FACETS = 32
ROWS_IMG = 64


def draw_facet_rows(key, part):
    first, second = jax.random.split(jax.random.fold_in(key, 11))
    counts = jax.random.randint(first, (FACETS,), ROWS_IMG // 4, ROWS_IMG + 1)
    chosen = jax.random.randint(second, (), 0, FACETS)
    return jnp.where(jnp.arange(FACETS) == chosen, ROWS_IMG, counts).astype(jnp.int32)


def draw_tile_slots(key, part):
    scores = jax.random.randint(jax.random.fold_in(key, 23), (CHANNELS, BLOCKS, BLOCKS), 0, 1 << 20)
    scores = scores * BLOCKS + jnp.arange(BLOCKS, dtype=jnp.int32)[None, None, :]
    ordering = jnp.argsort(scores, axis=-1)
    return ordering[:, :, :SLOTS].astype(jnp.int32)


def draw_tile_count(key, part):
    first, second = jax.random.split(jax.random.fold_in(key, 37))
    counts = jax.random.randint(first, (CHANNELS, BLOCKS), 1, SLOTS + 1)
    chosen = jax.random.randint(second, (CHANNELS, 1), 0, BLOCKS)
    return jnp.where(jnp.arange(BLOCKS)[None, :] == chosen, SLOTS, counts).astype(jnp.int32)


def draw_gram_tiles(key, part):
    first, second = jax.random.split(jax.random.fold_in(key, 53))
    shape = (CHANNELS, BLOCKS, SLOTS, BLOCK, BLOCK)
    diagonal = jax.random.uniform(first, shape[:-1], jnp.float32, 0.5, 2.0)
    noise = jax.random.normal(second, shape, jnp.float32)
    noise = (noise + jnp.swapaxes(noise, -1, -2)) * (0.5 / BLOCK ** 0.5)
    identity = jnp.eye(BLOCK, dtype=jnp.float32)
    return (noise + identity * diagonal[..., None]).astype(jnp.bfloat16)


def level_of(key, shape, cuts, smallest, high):
    def one(axis_at, shards_of):
        heights = jax.random.uniform(jax.random.fold_in(jax.random.fold_in(key, 6), axis_at), (shards_of,), jnp.float32, smallest / len(cuts), high / len(cuts))
        return jnp.repeat(jnp.exp(heights), shape[axis_at] // shards_of).reshape((-1,) + (1,) * (len(shape) - axis_at - 1))

    loudness = one(*cuts[0])
    for cut in cuts[1:]:
        loudness = loudness * one(*cut)
    return loudness


def gaussian(stream_key, dims, spread, reach, pieces=(), kind=jnp.bfloat16):
    gain = level_of(stream_key, dims, pieces, -0.22, 0.18) if pieces else 1.0
    array = jax.random.normal(stream_key, dims, jnp.float32) * spread * gain
    return jnp.minimum(jnp.maximum(array, -reach), reach).astype(kind)


def setup_inputs(seed: int = 0) -> dict:
    keys = jax.random.split(jax.random.key(seed), 10)
    sky_estimate = jnp.clip(2.0 * jax.random.uniform(keys[0], (CHANNELS, PIXELS, PIXELS), jnp.float32) ** level_of(keys[0], (CHANNELS, PIXELS, PIXELS), ((1, 32), (2, 8)), -0.2, 0.2), 0.0, 2.0)
    dual_coeffs = gaussian(keys[1], (CHANNELS, FRAMES, PIXELS, PIXELS), 0.3, 2.0, ((2, 32), (3, 8)))
    dirty_image = gaussian(keys[2], (CHANNELS, PIXELS, PIXELS), 0.5, 4.0, ((1, 32), (2, 8)), jnp.float32)
    filters = gaussian(keys[3], (FRAMES - 1, 2 * RADIUS + 1), (2 * RADIUS + 1) ** -0.5, 1.5, (), jnp.float32)
    thresholds = jnp.clip(jnp.exp(jax.random.uniform(keys[4], (FRAMES,), jnp.float32, math.log(0.2), math.log(1.2))), 0.2, 1.2)
    facet_rows = draw_facet_rows(jax.random.fold_in(keys[9], 71), 0)
    tile_slots = draw_tile_slots(jax.random.fold_in(keys[9], 71), 0)
    tile_count = draw_tile_count(jax.random.fold_in(keys[9], 71), 0)
    gram_tiles = draw_gram_tiles(jax.random.fold_in(keys[9], 71), 0)
    return dict(sky_estimate=sky_estimate, dual_coeffs=dual_coeffs, dirty_image=dirty_image, filters=filters, thresholds=thresholds, facet_rows=facet_rows, tile_slots=tile_slots, tile_count=tile_count, gram_tiles=gram_tiles)


STEP_PRIMAL = 0.5
STEP_DUAL = 0.5
PRECISE = lax.Precision.HIGHEST

def correlate(planes, filter_taps):
    groups = filter_taps.shape[0]
    radius = (filter_taps.shape[1] - 1) // 2
    layout = ('NCHW', 'OIHW', 'NCHW')
    rowwise = lax.conv_general_dilated(planes, filter_taps[:, None, :, None], (1, 1), ((radius, radius), (0, 0)), dimension_numbers=layout, feature_group_count=groups, precision=PRECISE)
    return lax.conv_general_dilated(rowwise, filter_taps[:, None, None, :], (1, 1), ((0, 0), (radius, radius)), dimension_numbers=layout, feature_group_count=groups, precision=PRECISE)

def reference(sky_estimate, dual_coeffs, dirty_image, filters, thresholds, facet_rows, tile_slots, tile_count, gram_tiles):
    taps_len = 2 * RADIUS + 1
    identity_tap = (jnp.arange(taps_len, dtype=jnp.int32) == RADIUS).astype(jnp.float32)
    all_taps = jnp.concatenate([identity_tap[None, :], filters], axis=0)
    flipped = all_taps[:, ::-1]

    def synth_channel(frames_one):
        return lax.optimization_barrier(jnp.sum(correlate(frames_one[None], flipped)[0], axis=0))
    synthesis = lax.map(synth_channel, dual_coeffs.astype(jnp.float32))
    spectrum = jnp.fft.fft2(sky_estimate)
    by_tile = jnp.swapaxes(spectrum, 1, 2).reshape(CHANNELS, BLOCKS, BLOCK, BLOCKS, BLOCK)
    positions = jnp.broadcast_to(tile_slots[:, :, None, :, None], (CHANNELS, BLOCKS, BLOCK, SLOTS, BLOCK))
    picked = jnp.take_along_axis(by_tile, positions, axis=3)
    in_use = (jnp.arange(SLOTS, dtype=jnp.int32)[None, None, :] < tile_count[:, :, None]).astype(jnp.float32)
    masked = gram_tiles.astype(jnp.float32) * in_use[:, :, :, None, None]
    selector = (tile_slots[:, :, :, None] == jnp.arange(BLOCKS, dtype=jnp.int32)[None, None, None, :]).astype(jnp.float32) * in_use[:, :, :, None]

    def weigh_part(plane_part):
        product = jnp.einsum('cqvsa,cqsab->cqvsb', plane_part, masked, precision=PRECISE)
        placed = jnp.einsum('cqvsb,cqst->cqvtb', product, selector, precision=PRECISE)
        return jnp.swapaxes(placed.reshape(CHANNELS, PIXELS, PIXELS), 1, 2)
    weighted = lax.complex(weigh_part(jnp.real(picked).astype(jnp.float32)), weigh_part(jnp.imag(picked).astype(jnp.float32)))
    gram_image = jnp.real(jnp.fft.ifft2(weighted)).astype(jnp.float32)
    counter = jnp.arange(PIXELS, dtype=jnp.int32)
    live_rows = (counter % ROWS_IMG < facet_rows[counter // ROWS_IMG]).astype(jnp.float32)
    image_next = jnp.maximum(sky_estimate - STEP_PRIMAL * (gram_image - dirty_image + synthesis), 0.0) * live_rows[None, :, None]
    probe = 2.0 * image_next - sky_estimate

    def update_frame(item):
        frame_taps, bound, current = item
        coeffs = correlate(probe[:, None], frame_taps[None, :])[:, 0]
        candidate = current.astype(jnp.float32) + STEP_DUAL * coeffs
        magnitude = jnp.sqrt(lax.optimization_barrier(jnp.sum(candidate * candidate, axis=0)))
        return (candidate * (bound / jnp.maximum(magnitude, bound))).astype(jnp.bfloat16)
    dual_next = jnp.swapaxes(lax.map(update_frame, (all_taps, thresholds, jnp.swapaxes(dual_coeffs, 0, 1))), 0, 1)
    return (image_next, dual_next)
```

```python
import math

import jax
import jax.numpy as jnp
import numpy as np
from jax import lax
from jax.experimental import pallas as pl
from jax.experimental.pallas import tpu as pltpu
from jax.sharding import PartitionSpec as P

PIXELS = 2048
RADIUS = 8
SLOTS = 6
ROWS = 64
COLS = 256
FRAMES = 8
PEERS_IMG = 32
STEP_PRIMAL = 0.5
STEP_DUAL = 0.5
BF = jnp.bfloat16
F32 = jnp.float32
VMEM_LIMIT = 48 << 20


def two_terms_np(table):
    high = table.astype(jnp.bfloat16)
    low = (table - high.astype(np.float64)).astype(jnp.bfloat16)
    return high, low


def two_terms(table):
    high = table.astype(BF)
    return high, (table - high.astype(F32)).astype(BF)


def dot(a, b, dims=((1,), (0,))):
    return lax.dot_general(a, b, (dims, ((), ())), preferred_element_type=F32)


def angle_np(a, b, period):
    return 2.0 * np.pi * ((a[:, None] * b[None, :]) % period) / period


def line_table():
    ang = angle_np(np.arange(256), np.arange(256), 256)
    return np.concatenate([-np.sin(ang), np.cos(ang), np.sin(ang)], axis=1)


def block_table():
    ang = angle_np(np.arange(32), np.arange(32), 32)
    c, s = np.cos(ang), np.sin(ang)
    return np.block([[c, s], [-s, c]])


def turn_table():
    ang = angle_np(np.arange(64), np.arange(64), 2048)
    ang = np.concatenate([ang, ang], axis=1)
    return np.stack([np.cos(ang), np.sin(ang)]).astype(np.float32)


def fold_tables(parity, scale):
    cls = jnp.arange(4, dtype=jnp.int32)
    freq = parity + 2 * cls
    pos = jnp.arange(4 * COLS, dtype=jnp.int32).reshape(4, COLS)
    ang = (freq[:, None, None] * pos[None] % PIXELS).astype(F32) * (2.0 * math.pi / PIXELS)
    return jnp.stack([jnp.cos(ang), jnp.sin(ang)]) * scale


def forward_kernel(x_ref, fold_ref, sign_ref, whi_ref, wlo_ref, o_ref):
    sign = sign_ref[0:1, :]
    xe = [x_ref[f].astype(F32) + sign * x_ref[f + 4].astype(F32) for f in range(4)]
    whi = whi_ref[:, 256:768]
    wlo = wlo_ref[:, 256:768]
    parts = [[], []]
    for chi in range(2):
        rows_re, rows_im = [], []
        for clo in range(2):
            cls = 2 * chi + clo
            yr = xe[0] * fold_ref[0, cls, 0:1, :]
            yi = xe[0] * fold_ref[1, cls, 0:1, :]
            for f in range(1, 4):
                yr = yr + xe[f] * fold_ref[0, cls, f : f + 1, :]
                yi = yi + xe[f] * fold_ref[1, cls, f : f + 1, :]
            yi = -yi
            rows_re.append(jnp.concatenate([yr, yi], axis=1))
            rows_im.append(jnp.concatenate([yi, -yr], axis=1))
        for part, rows in enumerate((rows_re, rows_im)):
            r = jnp.concatenate(rows, axis=0).astype(BF)
            out = dot(whi, r, ((1,), (1,))) + dot(wlo, r, ((1,), (1,)))
            parts[part].append(out.reshape(32, 8, 128))
    for part in range(2):
        both = jnp.concatenate(parts[part], axis=1)
        o_ref[:, part * 16 : (part + 1) * 16, :] = both.astype(BF)


def inverse_kernel(t_ref, fold_ref, sign_ref, whi_ref, wlo_ref, o_ref):
    sign = sign_ref[0:1, :]
    re = t_ref[:, 0:16, :].astype(F32)
    im = t_ref[:, 16:32, :].astype(F32)
    total = [None] * 4
    for chi in range(2):
        a = re[:, chi * 8 : chi * 8 + 8, :].reshape(256, 128).astype(BF)
        b = im[:, chi * 8 : chi * 8 + 8, :].reshape(256, 128).astype(BF)
        u = None
        for ref in (whi_ref, wlo_ref):
            term = dot(a, ref[:, 256:768], ((0,), (0,))) + dot(b, ref[:, 0:512], ((0,), (0,)))
            u = term if u is None else u + term
        for clo in range(2):
            cls = 2 * chi + clo
            ur = u[clo * 64 : clo * 64 + 64, 0:256]
            ui = u[clo * 64 : clo * 64 + 64, 256:512]
            for f in range(4):
                g = ur * fold_ref[0, cls, f : f + 1, :] - ui * fold_ref[1, cls, f : f + 1, :]
                total[f] = g if total[f] is None else total[f] + g
    for f in range(4):
        o_ref[f] = total[f].astype(BF)
        o_ref[f + 4] = (sign * total[f]).astype(BF)


def gram_kernel(
    d_ref, turn_ref, chi_ref, clo_ref, ehi_ref, elo_ref, gram_ref, o_ref, rows, rhs, mid
):
    rows[...] = d_ref[...].reshape(1024, 128).astype(F32)
    for vp in range(16):
        lanes = slice(vp * 128, vp * 128 + 128)
        rhs[0:32, lanes] = rows[pl.ds(vp, 32, stride=32), :].astype(BF)
        rhs[32:64, lanes] = rows[pl.ds(16 + vp, 32, stride=32), :].astype(BF)
    first = dot(chi_ref[...], rhs[...]) + dot(clo_ref[...], rhs[...])
    tc = turn_ref[0]
    ts = turn_ref[1]
    for vp in range(16):
        g = first[:, vp * 128 : vp * 128 + 128]
        gr = jnp.concatenate([g[0:32], g[0:32]], axis=0)
        gi = jnp.concatenate([g[32:64], g[32:64]], axis=0)
        mid[:, vp * 256 : vp * 256 + 128] = (gr * tc + gi * ts).astype(BF)
        mid[:, vp * 256 + 128 : vp * 256 + 256] = (gi * tc - gr * ts).astype(BF)
    pieces = []
    for g in range(4):
        m = mid[:, g * 1024 : (g + 1) * 1024]
        pieces.append((dot(m, ehi_ref[...]) + dot(m, elo_ref[...])).astype(BF))
    spec = jnp.concatenate(pieces, axis=1)
    mixed = dot(gram_ref[...], spec)
    lane_slot = (lax.broadcasted_iota(jnp.int32, (64, 512), 1) % 32) // 4
    weighted = jnp.where(lane_slot == 0, mixed[0:64], 0.0)
    for k in range(1, SLOTS):
        weighted = jnp.where(lane_slot == k, mixed[k * 64 : k * 64 + 64], weighted)
    weighted = weighted.astype(BF)
    for g in range(4):
        w = weighted[:, g * 128 : g * 128 + 128]
        z = dot(w, ehi_ref[...], ((1,), (1,))) + dot(w, elo_ref[...], ((1,), (1,)))
        for v in range(4):
            vp = g * 4 + v
            zr = z[:, v * 256 : v * 256 + 128]
            zi = z[:, v * 256 + 128 : v * 256 + 256]
            hr = zr * tc - zi * ts
            hi = zi * tc + zr * ts
            rhs[0:32, vp * 128 : vp * 128 + 128] = (hr[0:32] + hr[32:64]).astype(BF)
            rhs[32:64, vp * 128 : vp * 128 + 128] = (hi[0:32] + hi[32:64]).astype(BF)
    last = dot(chi_ref[...], rhs[...], ((0,), (0,))) + dot(clo_ref[...], rhs[...], ((0,), (0,)))
    for vp in range(16):
        lanes = slice(vp * 128, vp * 128 + 128)
        rows[pl.ds(vp, 32, stride=32), :] = last[0:32, lanes]
        rows[pl.ds(16 + vp, 32, stride=32), :] = last[32:64, lanes]
    o_ref[...] = rows[...].reshape(32, 32, 128).astype(BF)


def synth_kernel(dual_ref, strip_ref, o_ref, across):
    channels = o_ref.shape[0]
    for k in range(FRAMES):
        p = dual_ref[:, k].reshape(channels * ROWS, COLS)
        both = jnp.concatenate([p[:, 0:128], p[:, 128:256]], axis=0)
        a = dot(both, strip_ref[0, k]) + dot(both, strip_ref[1, k])
        a0 = a[0 : channels * ROWS]
        a1 = a[channels * ROWS :]
        out = jnp.concatenate([a0[:, 0:128], a0[:, 128:256] + a1[:, 0:128], a1[:, 128:256]], axis=1)
        for c in range(channels):
            across[c, k * ROWS : (k + 1) * ROWS, :] = out[c * ROWS : (c + 1) * ROWS].astype(BF)
    for c in range(channels):
        total = None
        for t in range(2):
            for k in range(FRAMES):
                term = dot(
                    strip_ref[t, k][0:64, 0:128],
                    across[c, k * ROWS : (k + 1) * ROWS, :],
                    ((0,), (0,)),
                )
                total = term if total is None else total + term
        o_ref[c] = total[0:80, 0:272]


def frames_kernel(bound_ref, probe_ref, dual_ref, strip_ref, o_ref, wide):
    step = pl.program_id(0)
    channels = probe_ref.shape[0]
    bound = bound_ref[step]

    @pl.when(step == 0)
    def _():
        wide[...] = jnp.zeros_like(wide)
        for c in range(channels):
            wide[c * 80 : c * 80 + 80, 0:272] = probe_ref[c].astype(BF)

    def finish(analysis):
        cand = [dual_ref[c, 0].astype(F32) + STEP_DUAL * analysis(c) for c in range(channels)]
        square = cand[0] * cand[0]
        for c in range(1, channels):
            square = square + cand[c] * cand[c]
        magnitude = jnp.sqrt(square)
        factor = bound / jnp.maximum(magnitude, bound)
        for c in range(channels):
            o_ref[c, 0] = (cand[c] * factor).astype(BF)

    @pl.when(step == 0)
    def _():
        finish(lambda c: probe_ref[c, 8:72, 8:264])

    @pl.when(step > 0)
    def _():
        down = []
        for c in range(channels):
            w = wide[c * 80 : c * 80 + 80, :]
            term = dot(strip_ref[0, 0][0:64, 0:80], w) + dot(strip_ref[1, 0][0:64, 0:80], w)
            down.append(term.astype(BF))
        down = jnp.concatenate(down, axis=0)
        both = jnp.concatenate([down[:, 0:256], down[:, 128:384]], axis=0)
        dims = ((1,), (1,))
        a = dot(both, strip_ref[0, 0], dims) + dot(both, strip_ref[1, 0], dims)
        rows = channels * ROWS
        finish(
            lambda c: jnp.concatenate(
                [a[c * ROWS : c * ROWS + ROWS], a[rows + c * ROWS : rows + c * ROWS + ROWS]], axis=1
            )
        )


def call(kernel, out_shape, scratch, flops, moved, *args):
    return pl.pallas_call(
        kernel,
        out_shape=out_shape,
        in_specs=[pl.BlockSpec(memory_space=pltpu.VMEM)] * len(args),
        out_specs=pl.BlockSpec(memory_space=pltpu.VMEM),
        scratch_shapes=scratch,
        compiler_params=pltpu.CompilerParams(vmem_limit_bytes=VMEM_LIMIT),
        cost_estimate=pl.CostEstimate(flops=flops, bytes_accessed=moved, transcendentals=0),
    )(*args)


def padded_2(cells, sides, width):
    for axis, dim in sides:
        count = lax.axis_size(axis)
        ends = count - 1
        head = lax.slice_in_dim(cells, 0, width, axis=dim)
        tail = lax.slice_in_dim(cells, cells.shape[dim] - width, cells.shape[dim], axis=dim)
        cells = jnp.concatenate(
            [
                lax.ppermute(tail, axis, [(i, (i + 1) % count) for i in range(ends)]),
                cells,
                lax.ppermute(head, axis, [((i + 1) % count, i) for i in range(ends)]),
            ],
            axis=dim,
        )
    return cells


def body(
    sky_estimate,
    dual_coeffs,
    dirty_image,
    filters,
    thresholds,
    facet_rows,
    tile_slots,
    tile_count,
    gram_tiles,
):
    channels, tile_rows, tile_cols = sky_estimate.shape
    place = lax.axis_index("fou")
    channel = place // 2
    parity = place % 2

    sent = jnp.repeat(sky_estimate.astype(BF), 2, axis=0)
    lines = lax.all_to_all(sent, "fou", split_axis=0, concat_axis=0, tiled=True)

    line_hi, line_lo = two_terms_np(line_table())
    fold = fold_tables(parity, 1.0)
    fold_back = fold_tables(parity, 1.0 / (PIXELS * PIXELS))
    sign = jnp.full((8, COLS), 1.0, F32) * (1 - 2 * parity).astype(F32)
    slab = jax.ShapeDtypeStruct((PEERS_IMG, 32, 128), BF)
    packed = call(
        forward_kernel, slab, [], 1 << 29, 1 << 20, lines, fold, sign, line_hi, line_lo
    )
    received = lax.all_to_all(packed, "img", split_axis=0, concat_axis=0, tiled=True)

    slots = lax.dynamic_index_in_dim(tile_slots[:, 0], channel, 0, keepdims=False)
    count = lax.dynamic_index_in_dim(tile_count[:, 0], channel, 0, keepdims=False)
    tiles = lax.dynamic_index_in_dim(gram_tiles[:, 0], channel, 0, keepdims=False)
    live_slot = (jnp.arange(SLOTS, dtype=jnp.int32) < count).astype(F32)
    r1 = jnp.arange(64, dtype=jnp.int32)
    ang = (r1[:, None] * slots[None, :] % 32).astype(F32) * (2.0 * math.pi / 32.0)
    ec = jnp.cos(ang) * live_slot
    es = jnp.sin(ang) * live_slot
    pad = ((0, 0), (0, 2))
    ec, es = jnp.pad(ec, pad), jnp.pad(es, pad)
    quad = jnp.stack([jnp.stack([ec, -es], -1), jnp.stack([es, ec], -1)])
    eye2 = jnp.eye(2, dtype=F32)
    one = quad[:, None, :, :, None, :] * eye2[None, :, None, None, :, None]
    one = one.reshape(256, 32)
    eye4 = jnp.eye(4, dtype=F32)
    four = (eye4[:, None, :, None] * one[None, :, None, :]).reshape(1024, 128)
    ehi, elo = two_terms(four)
    gram = jnp.swapaxes(tiles, 1, 2).reshape(SLOTS * 64, 64)

    block_hi, block_lo = two_terms_np(block_table())
    scratch = [
        pltpu.VMEM((1024, 128), F32),
        pltpu.VMEM((64, 2048), BF),
        pltpu.VMEM((64, 4096), BF),
    ]
    weighted = call(
        gram_kernel,
        slab,
        scratch,
        1 << 29,
        1 << 20,
        received,
        turn_table(),
        block_hi,
        block_lo,
        ehi,
        elo,
        gram,
    )
    returned = lax.all_to_all(weighted, "img", split_axis=0, concat_axis=0, tiled=True)
    blocks = call(
        inverse_kernel,
        jax.ShapeDtypeStruct((8, tile_rows, tile_cols), BF),
        [],
        1 << 29,
        1 << 20,
        returned,
        fold_back,
        sign,
        line_hi,
        line_lo,
    )
    halves = lax.all_to_all(blocks, "fou", split_axis=0, concat_axis=0, tiled=True)
    halves = halves.reshape(channels, 2, tile_rows, tile_cols).astype(F32)
    gram_image = halves[:, 0] + halves[:, 1]

    diff = (
        jnp.arange(256, dtype=jnp.int32)[None, :] - jnp.arange(128, dtype=jnp.int32)[:, None]
    )[None]
    strip = jnp.zeros((FRAMES, 128, 256), F32)
    for tap in range(2 * RADIUS + 1):
        strip = jnp.where(diff == tap, filters[:, tap][:, None, None], strip)
    strip = jnp.stack(two_terms(strip))

    spilled = call(
        synth_kernel,
        jax.ShapeDtypeStruct((channels, tile_rows + 16, tile_cols + 16), F32),
        [pltpu.VMEM((channels, FRAMES * ROWS, 384), BF)],
        1 << 31,
        4 << 20,
        dual_coeffs[:, 1:],
        strip,
    )
    double_rad = 2 * RADIUS
    edged = padded_2(spilled, (("img", 1), ("fou", 2)), RADIUS)
    upper_portion = jnp.pad(edged[:, :RADIUS, :], ((0, 0), (0, tile_rows - RADIUS), (0, 0)))
    lower_part = jnp.pad(
        edged[:, tile_rows + 3 * RADIUS :, :], ((0, 0), (tile_rows - RADIUS, 0), (0, 0))
    )
    row_folded = edged[:, double_rad : double_rad + tile_rows, :] + upper_portion + lower_part
    left_part = jnp.pad(row_folded[:, :, :RADIUS], ((0, 0), (0, 0), (0, tile_cols - RADIUS)))
    right_part = jnp.pad(
        row_folded[:, :, tile_cols + 3 * RADIUS :], ((0, 0), (0, 0), (tile_cols - RADIUS, 0))
    )
    folded = row_folded[:, :, double_rad : double_rad + tile_cols] + left_part + right_part
    synthesis = dual_coeffs[:, 0].astype(F32) + folded

    live_rows = (jnp.arange(tile_rows, dtype=jnp.int32) < facet_rows[0]).astype(F32)
    image_next = (
        jnp.maximum(sky_estimate - STEP_PRIMAL * (gram_image - dirty_image + synthesis), 0.0)
        * live_rows[None, :, None]
    )
    probe = 2.0 * image_next - sky_estimate
    beside_all = padded_2(probe, (("img", 1), ("fou", 2)), RADIUS)

    dual_spec = pl.BlockSpec((channels, 1, tile_rows, tile_cols), lambda f: (0, f, 0, 0))
    dual_next = pl.pallas_call(
        frames_kernel,
        out_shape=jax.ShapeDtypeStruct(dual_coeffs.shape, BF),
        grid=(FRAMES + 1,),
        in_specs=[
            pl.BlockSpec(memory_space=pltpu.SMEM),
            pl.BlockSpec(beside_all.shape, lambda f: (0, 0, 0)),
            dual_spec,
            pl.BlockSpec((2, 1, 128, 256), lambda f: (0, jnp.maximum(f - 1, 0), 0, 0)),
        ],
        out_specs=dual_spec,
        scratch_shapes=[pltpu.VMEM((channels * 80, 384), BF)],
        compiler_params=pltpu.CompilerParams(vmem_limit_bytes=VMEM_LIMIT),
        cost_estimate=pl.CostEstimate(flops=1 << 31, bytes_accessed=3 << 20, transcendentals=0),
    )(thresholds, beside_all, dual_coeffs, strip)
    return (image_next, dual_next)


def solution(mesh):
    in_specs = (
        P(None, "img", "fou"),
        P(None, None, "img", "fou"),
        P(None, "img", "fou"),
        P(),
        P(),
        P("img"),
        P(None, "img", None),
        P(None, "img"),
        P(None, "img", None, None, None),
    )
    out_specs = (P(None, "img", "fou"), P(None, None, "img", "fou"))
    return jax.shard_map(body, mesh=mesh, in_specs=in_specs, out_specs=out_specs, check_vma=False)
```

```python
import math

import jax
import jax.numpy as jnp
import numpy as np
from jax import lax
from jax.experimental import pallas as pl
from jax.experimental.pallas import tpu as pltpu
from jax.sharding import PartitionSpec as P

PIXELS = 2048
RADIUS = 8
SLOTS = 6
ROWS = 64
COLS = 256
FRAMES = 8
PEERS_IMG = 32
STEP_PRIMAL = 0.5
STEP_DUAL = 0.5
BF = jnp.bfloat16
F32 = jnp.float32
VMEM_LIMIT = 48 << 20
OUTSIDE = -1.0e30
LAST = ((1,), (1,))
FIRST = ((0,), (0,))


def two_terms_np(table):
    high = table.astype(jnp.bfloat16)
    low = (table - high.astype(np.float64)).astype(jnp.bfloat16)
    return high, low


def two_terms(table):
    high = table.astype(BF)
    return high, (table - high.astype(F32)).astype(BF)


def dot(a, b, dims=((1,), (0,))):
    return lax.dot_general(a, b, (dims, ((), ())), preferred_element_type=F32)


def angle_np(a, b, period):
    return 2.0 * np.pi * ((a[:, None] * b[None, :]) % period) / period


def line_table():
    ang = angle_np(np.arange(256), np.arange(256), 256)
    return two_terms_np(np.concatenate([-np.sin(ang), np.cos(ang), np.sin(ang)], axis=1))


def block_table():
    ang = angle_np(np.arange(32), np.arange(32), 32)
    c, s = np.cos(ang), np.sin(ang)
    return two_terms_np(np.block([[c, s], [-s, c]]))


HALO = np.concatenate([np.arange(-8, 0), np.arange(64, 72)])


def turn_table():
    main = np.tile(np.arange(64), 2)
    halo = np.tile(HALO, 8)
    ang = [angle_np(np.arange(64), r, 2048) for r in (main, halo)]
    return np.stack([np.cos(ang[0]), np.sin(ang[0]), np.cos(ang[1]), np.sin(ang[1])]).astype(np.float32)


def tile_table():
    t = np.arange(32)
    ang = angle_np(t, np.arange(64), 32)
    c, s = np.cos(ang), np.sin(ang)
    main = np.zeros((32, 2, 2, 2, 2, 64))
    for p in range(2):
        main[:, p, 0, 0, p] = c
        main[:, p, 1, 0, p] = -s
        main[:, p, 0, 1, p] = s
        main[:, p, 1, 1, p] = c
    ang = angle_np(t, HALO, 32)
    c, s = np.cos(ang), np.sin(ang)
    halo = np.zeros((32, 2, 2, 2, 2, 2, 2, 2, 16))
    for p in range(2):
        for x in range(2):
            halo[:, p, 0, x, 0, 0, x, p] = c
            halo[:, p, 1, x, 0, 0, x, p] = -s
            halo[:, p, 0, x, 1, 0, x, p] = s
            halo[:, p, 1, x, 1, 0, x, p] = c
            halo[:, p, 0, x, 0, 1, x, p] = s
            halo[:, p, 1, x, 0, 1, x, p] = c
            halo[:, p, 0, x, 1, 1, x, p] = -c
            halo[:, p, 1, x, 1, 1, x, p] = s
    table = np.concatenate([main.reshape(128, 256), halo.reshape(128, 512)], axis=1)
    return two_terms_np(table)


def fold_table():
    freq = np.arange(2)[:, None] + 2 * np.arange(4)[None]
    pos = np.arange(4 * COLS).reshape(4, COLS)
    ang = 2.0 * np.pi * ((freq[:, :, None, None] * pos) % PIXELS) / PIXELS
    return np.stack([np.cos(ang), np.sin(ang)], axis=1).astype(np.float32)


def forward_kernel(par_ref, x_ref, fold_ref, line_ref, o_ref):
    par = par_ref[1]
    sign = (1 - 2 * par).astype(F32)
    xe = [x_ref[f].astype(F32) + sign * x_ref[f + 4].astype(F32) for f in range(4)]
    parts = [[], []]
    for chi in range(2):
        rows_re, rows_im = [], []
        for clo in range(2):
            cos = fold_ref[par, 0, 2 * chi + clo]
            sin = fold_ref[par, 1, 2 * chi + clo]
            yr = xe[0] * cos[0:1]
            yi = xe[0] * sin[0:1]
            for f in range(1, 4):
                yr = yr + xe[f] * cos[f : f + 1]
                yi = yi + xe[f] * sin[f : f + 1]
            yi = -yi
            rows_re.append(jnp.concatenate([yr, yi], axis=1))
            rows_im.append(jnp.concatenate([yi, -yr], axis=1))
        for part, rows in enumerate((rows_re, rows_im)):
            r = jnp.concatenate(rows, axis=0).astype(BF)
            out = dot(line_ref[0, :, 256:768], r, LAST) + dot(line_ref[1, :, 256:768], r, LAST)
            parts[part].append(out.reshape(32, 8, 128))
    for part in range(2):
        both = jnp.concatenate(parts[part], axis=1)
        o_ref[:, part * 16 : (part + 1) * 16, :] = both.astype(BF)


def inverse_kernel(par_ref, t_ref, fold_ref, line_ref, o_ref):
    par = par_ref[1]
    sign = (1 - 2 * par).astype(F32)
    re = t_ref[:, 0:16, :].astype(F32)
    im = t_ref[:, 16:32, :].astype(F32)
    edge = t_ref[:, 32:40, :].astype(F32).reshape(256, 128).astype(BF)
    h = dot(edge, line_ref[0], FIRST) + dot(edge, line_ref[1], FIRST)
    h = h[0:64, 256:768] + h[64:128, 0:512]
    total = [None] * 4
    for chi in range(2):
        a = re[:, chi * 8 : chi * 8 + 8, :].reshape(256, 128).astype(BF)
        b = im[:, chi * 8 : chi * 8 + 8, :].reshape(256, 128).astype(BF)
        u = None
        for t in range(2):
            term = dot(a, line_ref[t, :, 256:768], FIRST) + dot(b, line_ref[t, :, 0:512], FIRST)
            u = term if u is None else u + term
        for clo in range(2):
            cls = 2 * chi + clo
            e = h[cls * 16 : cls * 16 + 16]
            whole = jnp.concatenate([e[0:8], u[clo * 64 : clo * 64 + 64], e[8:16]], axis=0)
            ur = whole[:, 0:256]
            ui = whole[:, 256:512]
            cos = fold_ref[par, 0, cls]
            sin = fold_ref[par, 1, cls]
            for f in range(4):
                g = ur * cos[f : f + 1] - ui * sin[f : f + 1]
                total[f] = g if total[f] is None else total[f] + g
    scale = 1.0 / (PIXELS * PIXELS)
    total = [g * scale for g in total]
    total = total + [sign * g for g in total]
    none = jnp.zeros((80, 128), F32)
    for f in range(8):
        before = total[f - 1][:, 128:256] if f > 0 else none
        after = total[f + 1][:, 0:128] if f < 7 else none
        line = jnp.concatenate([before, total[f], after], axis=1)
        o_ref[f] = pltpu.roll(line, 512 - 120, 1)[:, 0:384].astype(BF)


def tiles_kernel(where_ref, slots_ref, count_ref, tiles_ref, table_ref, o_ref, gram_ref):
    channel = where_ref[0]
    left = lax.broadcasted_iota(jnp.int32, (32, 128), 0)
    right = lax.broadcasted_iota(jnp.int32, (32, 128), 1)
    tile = jnp.full((32, 128), -1, jnp.int32)
    for k in range(SLOTS):
        slot = jnp.where(k < count_ref[channel, 0], slots_ref[channel, 0, k], -1)
        tile = jnp.where(left // 4 == k, slot, tile)
    pick = (tile == right // 4) & (left % 4 == right % 4)
    pick = jnp.where(pick, 1.0, 0.0).astype(BF)
    for k in range(SLOTS):
        gram_ref[k * 64 : k * 64 + 64, :] = tiles_ref[channel, 0, k].astype(F32).T.astype(BF)
    o_ref[...] = jnp.zeros_like(o_ref)
    for t in range(2):
        row = dot(pick, table_ref[t]).astype(BF)
        for j in range(2):
            for chi in range(2):
                p = 2 * j + chi
                rows = slice(p * 32, p * 32 + 32)
                o_ref[t, rows, p * 256 : p * 256 + 256] = row[:, 0:256]
                for comp in range(2):
                    at = 256 + chi * 256 + comp * 128
                    to = 1024 + comp * 256 + j * 128
                    o_ref[t, rows, to : to + 128] = row[:, at : at + 128]


def gram_kernel(d_ref, turn_ref, block_ref, e_ref, gram_ref, o_ref, rows, rhs, mid, edge):
    rows[0:1024, :] = d_ref[...].reshape(1024, 128).astype(F32)
    for p in range(16):
        lanes = slice(p * 128, p * 128 + 128)
        at = (p % 2) * 8 + p // 2
        rhs[0:32, lanes] = rows[pl.ds(at, 32, stride=32), :].astype(BF)
        rhs[32:64, lanes] = rows[pl.ds(16 + at, 32, stride=32), :].astype(BF)
    first = dot(block_ref[0], rhs[...]) + dot(block_ref[1], rhs[...])
    tc, ts, ec, es = turn_ref[0], turn_ref[1], turn_ref[2], turn_ref[3]
    for p in range(16):
        g = first[:, p * 128 : p * 128 + 128]
        gr = jnp.concatenate([g[0:32], g[0:32]], axis=0)
        gi = jnp.concatenate([g[32:64], g[32:64]], axis=0)
        mid[:, p * 256 : p * 256 + 128] = (gr * tc + gi * ts).astype(BF)
        mid[:, p * 256 + 128 : p * 256 + 256] = (gi * tc - gr * ts).astype(BF)
    pieces = []
    for g in range(4):
        m = mid[:, g * 1024 : (g + 1) * 1024]
        pieces.append((dot(m, e_ref[0, :, 0:1024], LAST) + dot(m, e_ref[1, :, 0:1024], LAST)).astype(BF))
    spec = jnp.concatenate(pieces, axis=1)
    mixed = dot(gram_ref[...], spec)
    lane_slot = (lax.broadcasted_iota(jnp.int32, (64, 512), 1) % 32) // 4
    weighted = jnp.where(lane_slot == 0, mixed[0:64], 0.0)
    for k in range(1, SLOTS):
        weighted = jnp.where(lane_slot == k, mixed[k * 64 : k * 64 + 64], weighted)
    weighted = weighted.astype(BF)
    for g in range(4):
        w = weighted[:, g * 128 : g * 128 + 128]
        z = dot(w, e_ref[0]) + dot(w, e_ref[1])
        for v in range(4):
            p = g * 4 + v
            zr = z[:, v * 256 : v * 256 + 128]
            zi = z[:, v * 256 + 128 : v * 256 + 256]
            hr = zr * tc - zi * ts
            hi = zi * tc + zr * ts
            rhs[0:32, p * 128 : p * 128 + 128] = (hr[0:32] + hr[32:64]).astype(BF)
            rhs[32:64, p * 128 : p * 128 + 128] = (hi[0:32] + hi[32:64]).astype(BF)
        for j in range(2):
            zr = z[:, 1024 + j * 128 : 1152 + j * 128]
            zi = z[:, 1280 + j * 128 : 1408 + j * 128]
            hr = zr * ec - zi * es
            hi = zi * ec + zr * es
            lanes = slice((2 * g + j) * 128, (2 * g + j) * 128 + 128)
            edge[0:32, lanes] = (hr[0:32] + hr[32:64]).astype(BF)
            edge[32:64, lanes] = (hi[0:32] + hi[32:64]).astype(BF)
    last = dot(block_ref[0], rhs[...], FIRST) + dot(block_ref[1], rhs[...], FIRST)
    outer = dot(block_ref[0, :, 0:32], edge[...], FIRST) + dot(block_ref[1, :, 0:32], edge[...], FIRST)
    for p in range(16):
        lanes = slice(p * 128, p * 128 + 128)
        at = (p % 2) * 8 + p // 2
        rows[pl.ds(at, 32, stride=40), :] = last[0:32, lanes]
        rows[pl.ds(16 + at, 32, stride=40), :] = last[32:64, lanes]
    for v in range(8):
        rows[pl.ds(32 + v, 32, stride=40), :] = outer[:, v * 128 : v * 128 + 128]
    o_ref[...] = rows[...].reshape(32, 40, 128).astype(BF)


def band_kernel(taps_ref, strip_ref, down_ref):
    lane = lax.broadcasted_iota(jnp.int32, (64, 256), 1)
    for k in range(FRAMES):
        wide = jnp.broadcast_to(taps_ref[k : k + 1, :], (128, 256))
        band = pltpu.roll(wide, 0, 1, stride=1, stride_axis=0)
        high = band.astype(BF)
        low = band - high.astype(F32)
        strip_ref[0, k] = high
        strip_ref[1, k] = low.astype(BF)
        high = jnp.where(lane < 80, high[0:64].astype(F32), 0.0)
        low = jnp.where(lane < 80, low[0:64], 0.0)
        row = high + pltpu.roll(high, 80, 1) + pltpu.roll(low, 160, 1)
        down_ref[k * 64 : k * 64 + 64, :] = row.astype(BF)


def synth_kernel(
    where_ref, live_ref, dual_ref, sky_ref, dirty_ref, strip_ref, o_ref, head_ref, tail_ref, across
):
    channels = sky_ref.shape[0]
    row = lax.broadcasted_iota(jnp.int32, (80, 272), 0) + where_ref[2] * ROWS - RADIUS
    col = lax.broadcasted_iota(jnp.int32, (80, 272), 1) + where_ref[3] * COLS - RADIUS
    inside = (row >= 0) & (row < PIXELS) & (col >= 0) & (col < PIXELS)
    for k in range(FRAMES):
        p = dual_ref[:, k + 1].reshape(channels * ROWS, COLS)
        both = jnp.concatenate([p[:, 0:128], p[:, 128:256]], axis=0)
        a = dot(both, strip_ref[0, k]) + dot(both, strip_ref[1, k])
        a0 = a[0 : channels * ROWS]
        a1 = a[channels * ROWS :]
        out = jnp.concatenate([a0[:, 0:128], a0[:, 128:256] + a1[:, 0:128], a1[:, 128:256]], axis=1)
        for c in range(channels):
            across[c, k * ROWS : (k + 1) * ROWS, :] = out[c * ROWS : (c + 1) * ROWS].astype(BF)
    live = lax.broadcasted_iota(jnp.int32, (ROWS, COLS), 0) < live_ref[0]
    none = jnp.zeros((ROWS, 128), F32)
    edge = jnp.zeros((8, 272), F32)
    for c in range(channels):
        total = None
        for t in range(2):
            for k in range(FRAMES):
                term = dot(
                    strip_ref[t, k][0:64, 0:128],
                    across[c, k * ROWS : (k + 1) * ROWS, :],
                    FIRST,
                )
                total = term if total is None else total + term
        sky = sky_ref[c]
        own = sky + STEP_PRIMAL * dirty_ref[c] - STEP_PRIMAL * dual_ref[c, 0].astype(F32)
        own = jnp.where(live, own, OUTSIDE)
        own = pltpu.roll(jnp.concatenate([own, none], axis=1), 8, 1)[:, 0:272]
        sky = pltpu.roll(jnp.concatenate([sky, none], axis=1), 8, 1)[:, 0:272]
        total = total[0:80, 0:272] * (-STEP_PRIMAL)
        total = total + jnp.concatenate([edge, own, edge], axis=0)
        total = jnp.where(inside, total, OUTSIDE)
        sky = jnp.concatenate([edge, sky, edge], axis=0)
        for at, cells in ((c, total), (channels + c, sky)):
            o_ref[at] = cells
            head_ref[at] = cells[0:16].astype(BF)
            tail_ref[at] = cells[64:80].astype(BF)


def frames_kernel(bound_ref, half_ref, base_ref, dual_ref, strip_ref, down_ref, image_ref, o_ref, probes, wide, down):
    step = pl.program_id(0)
    channels = image_ref.shape[0]
    bound = bound_ref[step]

    def finish(analysis):
        cand = [dual_ref[c, 0].astype(F32) + STEP_DUAL * analysis(c) for c in range(channels)]
        square = cand[0] * cand[0]
        for c in range(1, channels):
            square = square + cand[c] * cand[c]
        factor = bound * lax.rsqrt(jnp.maximum(square, bound * bound))
        for c in range(channels):
            o_ref[c, 0] = (cand[c] * factor).astype(BF)

    @pl.when(step == 0)
    def _():
        wide[...] = jnp.zeros_like(wide)
        for c in range(channels):
            gram = half_ref[2 * c, :, 0:272].astype(F32) + half_ref[2 * c + 1, :, 0:272].astype(F32)
            image = jnp.maximum(base_ref[c] - STEP_PRIMAL * gram, 0.0)
            probe = 2.0 * image - base_ref[channels + c]
            image_ref[c] = image[8:72, 8:264]
            probes[c] = probe[8:72, 8:264]
            high = probe.astype(BF)
            low = (probe - high.astype(F32)).astype(BF)
            wide[0:80, 0:272] = high
            wide[80:160, 0:272] = low
            wide[160:240, 0:272] = high
            d = dot(down_ref[...], wide[...])
            high = d.astype(BF)
            down[0, c] = high
            down[1, c] = (d - high.astype(F32)).astype(BF)
        finish(lambda c: probes[c])

    @pl.when(step > 0)
    def _():
        at = pl.multiple_of((step - 1) * ROWS, ROWS)
        a = None
        for t in range(2):
            d = jnp.concatenate([down[t, c, pl.ds(at, ROWS), :] for c in range(channels)], axis=0)
            both = jnp.concatenate([d[:, 0:256], d[:, 128:384]], axis=0)
            term = dot(both, strip_ref[0, 0], LAST)
            a = term if a is None else a + term
            if t == 0:
                a = a + dot(both, strip_ref[1, 0], LAST)
        rows = channels * ROWS
        finish(
            lambda c: jnp.concatenate(
                [a[c * ROWS : c * ROWS + ROWS], a[rows + c * ROWS : rows + c * ROWS + ROWS]], axis=1
            )
        )


VM = pl.BlockSpec(memory_space=pltpu.VMEM)
SM = pl.BlockSpec(memory_space=pltpu.SMEM)


def call(kernel, out_shape, scratch, flops, moved, *args, scalars=0):
    return pl.pallas_call(
        kernel,
        out_shape=out_shape,
        in_specs=[SM] * scalars + [VM] * (len(args) - scalars),
        out_specs=jax.tree.map(lambda _: VM, out_shape),
        scratch_shapes=scratch,
        compiler_params=pltpu.CompilerParams(vmem_limit_bytes=VMEM_LIMIT),
        cost_estimate=pl.CostEstimate(flops=flops, bytes_accessed=moved, transcendentals=0),
    )(*args)


def overlap_add(cells, head, tail, axis, dim):
    count = lax.axis_size(axis)
    room = cells.shape[dim] - 2 * RADIUS
    from_before = lax.ppermute(tail, axis, [(i, i + 1) for i in range(count - 1)])
    from_after = lax.ppermute(head, axis, [(i + 1, i) for i in range(count - 1)])
    width = [(0, 0)] * cells.ndim
    width[dim] = (0, room)
    cells = cells + jnp.pad(from_before, width).astype(F32)
    width[dim] = (room, 0)
    return cells + jnp.pad(from_after, width).astype(F32)


def after(values, event):
    return lax.optimization_barrier((*values, event))[:-1]


def body(
    sky_estimate,
    dual_coeffs,
    dirty_image,
    filters,
    thresholds,
    facet_rows,
    tile_slots,
    tile_count,
    gram_tiles,
):
    channels, tile_rows, tile_cols = sky_estimate.shape
    place = lax.axis_index("fou")
    where = jnp.stack([place >> 1, place & 1, lax.axis_index("img"), place]).astype(jnp.int32)

    sent = jnp.repeat(sky_estimate.astype(BF), 2, axis=0)
    lines = lax.all_to_all(sent, "fou", split_axis=0, concat_axis=0, tiled=True)

    line = np.stack(line_table())
    fold = fold_table()
    packed = call(
        forward_kernel,
        jax.ShapeDtypeStruct((PEERS_IMG, 32, 128), BF),
        [],
        1 << 29,
        1 << 20,
        where,
        lines,
        fold,
        line,
        scalars=1,
    )
    received = lax.all_to_all(packed, "img", split_axis=0, concat_axis=0, tiled=True)

    spread, gram = call(
        tiles_kernel,
        (jax.ShapeDtypeStruct((2, 128, 1536), BF), jax.ShapeDtypeStruct((SLOTS * 64, 64), BF)),
        [],
        1 << 23,
        1 << 20,
        where,
        tile_slots,
        tile_count,
        gram_tiles,
        np.stack(tile_table()),
        scalars=3,
    )

    scratch = [
        pltpu.VMEM((1280, 128), F32),
        pltpu.VMEM((64, 2048), BF),
        pltpu.VMEM((64, 4096), BF),
        pltpu.VMEM((64, 1024), BF),
    ]
    weighted = call(
        gram_kernel,
        jax.ShapeDtypeStruct((PEERS_IMG, 40, 128), BF),
        scratch,
        1 << 29,
        1 << 20,
        received,
        turn_table(),
        np.stack(block_table()),
        spread,
        gram,
    )
    returned = lax.all_to_all(weighted, "img", split_axis=0, concat_axis=0, tiled=True)
    blocks = call(
        inverse_kernel,
        jax.ShapeDtypeStruct((8, tile_rows + 16, 384), BF),
        [],
        1 << 29,
        1 << 20,
        where,
        returned,
        fold,
        line,
        scalars=1,
    )
    halves = lax.all_to_all(blocks, "fou", split_axis=0, concat_axis=0, tiled=True)

    strip, down = call(
        band_kernel,
        (
            jax.ShapeDtypeStruct((2, FRAMES, 128, 256), BF),
            jax.ShapeDtypeStruct((FRAMES * ROWS, 256), BF),
        ),
        [],
        1 << 20,
        1 << 20,
        jnp.pad(filters, ((0, 0), (0, 256 - filters.shape[1]))),
    )
    ends = jax.ShapeDtypeStruct((2 * channels, 16, tile_cols + 16), BF)
    base, head, tail = call(
        synth_kernel,
        (jax.ShapeDtypeStruct((2 * channels, tile_rows + 16, tile_cols + 16), F32), ends, ends),
        [pltpu.VMEM((channels, FRAMES * ROWS, 384), BF)],
        1 << 31,
        4 << 20,
        where,
        facet_rows,
        dual_coeffs,
        sky_estimate,
        dirty_image,
        strip,
        scalars=2,
    )
    head, tail = after((head, tail), packed)
    base = overlap_add(base, head, tail, "img", 1)
    head, tail = base[:, :, 0:16].astype(BF), base[:, :, tile_cols : tile_cols + 16].astype(BF)
    head, tail = after((head, tail), weighted)
    base = overlap_add(base, head, tail, "fou", 2)

    dual_spec = pl.BlockSpec((channels, 1, tile_rows, tile_cols), lambda f: (0, f, 0, 0))
    whole = lambda a: pl.BlockSpec(a.shape, lambda f: (0,) * a.ndim)
    return pl.pallas_call(
        frames_kernel,
        out_shape=(
            jax.ShapeDtypeStruct(sky_estimate.shape, F32),
            jax.ShapeDtypeStruct(dual_coeffs.shape, BF),
        ),
        grid=(FRAMES + 1,),
        in_specs=[
            SM,
            whole(halves),
            whole(base),
            dual_spec,
            pl.BlockSpec((2, 1, 128, 256), lambda f: (0, jnp.maximum(f - 1, 0), 0, 0)),
            whole(down),
        ],
        out_specs=(pl.BlockSpec(sky_estimate.shape, lambda f: (0, 0, 0)), dual_spec),
        scratch_shapes=[
            pltpu.VMEM(sky_estimate.shape, F32),
            pltpu.VMEM((256, 384), BF),
            pltpu.VMEM((2, channels, FRAMES * ROWS, 384), BF),
        ],
        compiler_params=pltpu.CompilerParams(vmem_limit_bytes=VMEM_LIMIT),
        cost_estimate=pl.CostEstimate(flops=1 << 31, bytes_accessed=3 << 20, transcendentals=0),
    )(thresholds, halves, base, dual_coeffs, strip, down)


def solution(mesh):
    in_specs = (
        P(None, "img", "fou"),
        P(None, None, "img", "fou"),
        P(None, "img", "fou"),
        P(),
        P(),
        P("img"),
        P(None, "img", None),
        P(None, "img"),
        P(None, "img", None, None, None),
    )
    out_specs = (P(None, "img", "fou"), P(None, None, "img", "fou"))
    return jax.shard_map(body, mesh=mesh, in_specs=in_specs, out_specs=out_specs, check_vma=False)
```

```python
import math

import jax
import jax.numpy as jnp
import numpy as np
from jax import lax
from jax.experimental import pallas as pl
from jax.experimental.pallas import tpu as pltpu
from jax.sharding import PartitionSpec as P

PIXELS = 2048
RADIUS = 8
SLOTS = 6
ROWS = 64
COLS = 256
FRAMES = 8
PEERS_IMG = 32
STEP_PRIMAL = 0.5
STEP_DUAL = 0.5
BF = jnp.bfloat16
F32 = jnp.float32
VMEM_LIMIT = 20 << 20
WIDE = 384
OUTSIDE = -1.0e30
LAST = ((1,), (1,))
FIRST = ((0,), (0,))


def two_terms_np(table):
    high = table.astype(jnp.bfloat16)
    low = (table - high.astype(np.float64)).astype(jnp.bfloat16)
    return high, low


def two_terms(table):
    high = table.astype(BF)
    return high, (table - high.astype(F32)).astype(BF)


def dot(a, b, dims=((1,), (0,))):
    return lax.dot_general(a, b, (dims, ((), ())), preferred_element_type=F32)


def angle_np(a, b, period):
    return 2.0 * np.pi * ((a[:, None] * b[None, :]) % period) / period


def line_table():
    ang = angle_np(np.arange(256), np.arange(256), 256)
    return two_terms_np(np.concatenate([np.cos(ang), np.sin(ang)], axis=1))


def block_table():
    ang = angle_np(np.arange(32), np.arange(32), 32)
    c, s = np.cos(ang), np.sin(ang)
    return two_terms_np(np.block([[c, s], [-s, c]]))


HALO = np.concatenate([np.arange(-8, 0), np.arange(64, 72)])


def turn_table():
    main = np.tile(np.arange(64), 2)
    halo = np.tile(HALO, 8)
    ang = [angle_np(np.arange(64), r, 2048) for r in (main, halo)]
    return two_terms_np(
        np.concatenate([np.cos(ang[0]), np.sin(ang[0]), np.cos(ang[1]), np.sin(ang[1])])
    )


def fixed_table():
    table = np.zeros((256, 512), jnp.bfloat16)
    for t in range(2):
        table[:, t * 128 : t * 128 + 128] = turn_table()[t]
        table[0:64, 256 + t * 128 : 320 + t * 128] = block_table()[t]
    return table


def tile_table():
    t = np.arange(32)
    ang = angle_np(t, np.arange(64), 32)
    c, s = np.cos(ang), np.sin(ang)
    main = np.zeros((32, 2, 2, 2, 2, 64))
    for p in range(2):
        main[:, p, 0, 0, p] = c
        main[:, p, 1, 0, p] = -s
        main[:, p, 0, 1, p] = s
        main[:, p, 1, 1, p] = c
    ang = angle_np(t, HALO, 32)
    c, s = np.cos(ang), np.sin(ang)
    halo = np.zeros((32, 2, 2, 2, 2, 2, 2, 2, 16))
    for p in range(2):
        for x in range(2):
            halo[:, p, 0, x, 0, 0, x, p] = c
            halo[:, p, 1, x, 0, 0, x, p] = -s
            halo[:, p, 0, x, 1, 0, x, p] = s
            halo[:, p, 1, x, 1, 0, x, p] = c
            halo[:, p, 0, x, 0, 1, x, p] = s
            halo[:, p, 1, x, 0, 1, x, p] = c
            halo[:, p, 0, x, 1, 1, x, p] = -c
            halo[:, p, 1, x, 1, 1, x, p] = s
    table = np.concatenate([main.reshape(128, 256), halo.reshape(128, 512)], axis=1)
    return two_terms_np(table)


def fold_table():
    freq = np.arange(2)[:, None] + 2 * np.arange(4)[None]
    pos = np.arange(4 * COLS).reshape(4, COLS)
    ang = 2.0 * np.pi * ((freq[:, :, None, None] * pos) % PIXELS) / PIXELS
    return np.stack([np.cos(ang), np.sin(ang)], axis=1).astype(np.float32)


def forward_kernel(par_ref, x_ref, fold_ref, line_ref, o_ref):
    par = par_ref[1]
    sign = (1 - 2 * par).astype(F32)
    xe = [x_ref[f].astype(F32) + sign * x_ref[f + 4].astype(F32) for f in range(4)]
    parts = [[], []]
    for chi in range(2):
        rows_re, rows_im = [], []
        for clo in range(2):
            cos = fold_ref[par, 0, 2 * chi + clo]
            sin = fold_ref[par, 1, 2 * chi + clo]
            yr = xe[0] * cos[0:1]
            yi = xe[0] * sin[0:1]
            for f in range(1, 4):
                yr = yr + xe[f] * cos[f : f + 1]
                yi = yi + xe[f] * sin[f : f + 1]
            yi = -yi
            rows_re.append(jnp.concatenate([yr, yi], axis=1))
            rows_im.append(jnp.concatenate([yi, -yr], axis=1))
        for part, rows in enumerate((rows_re, rows_im)):
            r = jnp.concatenate(rows, axis=0).astype(BF)
            out = dot(line_ref[0], r, LAST) + dot(line_ref[1], r, LAST)
            parts[part].append(out.reshape(32, 8, 128))
    for part in range(2):
        both = jnp.concatenate(parts[part], axis=1)
        o_ref[:, part * 16 : (part + 1) * 16, :] = both.astype(BF)


def inverse_kernel(par_ref, t_ref, fold_ref, line_ref, base_ref, o_ref):
    par = par_ref[1]
    me = par_ref[3]
    sign = (1 - 2 * par).astype(F32)
    re = t_ref[:, 0:16, :].astype(F32)
    im = t_ref[:, 16:32, :].astype(F32)
    edge = t_ref[:, 32:40, :].astype(F32).reshape(256, 128).astype(BF)
    h = dot(edge, line_ref[0], FIRST) + dot(edge, line_ref[1], FIRST)
    h = jnp.concatenate(
        [h[0:64, 0:256] - h[64:128, 256:512], h[0:64, 256:512] + h[64:128, 0:256]], axis=1
    )
    total = [None] * 4
    for chi in range(2):
        a = re[:, chi * 8 : chi * 8 + 8, :].reshape(256, 128).astype(BF)
        b = im[:, chi * 8 : chi * 8 + 8, :].reshape(256, 128).astype(BF)
        a = dot(a, line_ref[0], FIRST) + dot(a, line_ref[1], FIRST)
        b = dot(b, line_ref[0], FIRST) + dot(b, line_ref[1], FIRST)
        u = jnp.concatenate([a[:, 0:256] - b[:, 256:512], a[:, 256:512] + b[:, 0:256]], axis=1)
        for clo in range(2):
            cls = 2 * chi + clo
            e = h[cls * 16 : cls * 16 + 16]
            whole = jnp.concatenate([e[0:8], u[clo * 64 : clo * 64 + 64], e[8:16]], axis=0)
            ur = whole[:, 0:256]
            ui = whole[:, 256:512]
            cos = fold_ref[par, 0, cls]
            sin = fold_ref[par, 1, cls]
            for f in range(4):
                g = ur * cos[f : f + 1] - ui * sin[f : f + 1]
                total[f] = g if total[f] is None else total[f] + g
    scale = 1.0 / (PIXELS * PIXELS)
    total = [g * scale for g in total]
    total = total + [sign * g for g in total]
    none = jnp.zeros((80, 128), F32)
    lane = lax.broadcasted_iota(jnp.int32, (80, 128), 1)
    for f in range(8):
        before = total[f - 1][:, 128:256] if f > 0 else none
        after = total[f + 1][:, 0:128] if f < 7 else none
        line = jnp.concatenate([before, total[f], after], axis=1)
        line = pltpu.roll(line, 512 - 120, 1)
        pack = jnp.where(f == me - 1, base_ref[0, :, WIDE:], 0.0)
        pack = pack + jnp.where(f == me + 1, base_ref[1, :, WIDE:], 0.0)
        o_ref[f, :, 0:256] = line[:, 0:256].astype(BF)
        o_ref[f, :, 256:384] = (jnp.where(lane < 16, line[:, 256:384], 0.0) + pack).astype(BF)


def tiles_kernel(where_ref, slots_ref, count_ref, tiles_ref, table_ref, fixed_ref, o_ref):
    channel = where_ref[0]
    left = lax.broadcasted_iota(jnp.int32, (32, 128), 0)
    right = lax.broadcasted_iota(jnp.int32, (32, 128), 1)
    tile = jnp.full((32, 128), -1, jnp.int32)
    for k in range(SLOTS):
        slot = jnp.where(k < count_ref[channel, 0], slots_ref[channel, 0, k], -1)
        tile = jnp.where(left // 4 == k, slot, tile)
    pick = (tile == right // 4) & (left % 4 == right % 4)
    pick = jnp.where(pick, 1.0, 0.0).astype(BF)
    o_ref[...] = jnp.zeros_like(o_ref)
    for k in range(SLOTS):
        o_ref[256 + k * 64 : 320 + k * 64, 0:64] = tiles_ref[channel, 0, k].astype(F32).T.astype(BF)
    o_ref[256:512, 128:640] = fixed_ref[...]
    for t in range(2):
        row = dot(pick, table_ref[t]).astype(BF)
        for j in range(2):
            for chi in range(2):
                p = 2 * j + chi
                rows = slice(t * 128 + p * 32, t * 128 + p * 32 + 32)
                o_ref[rows, p * 256 : p * 256 + 256] = row[:, 0:256]
                for comp in range(2):
                    at = 256 + chi * 256 + comp * 128
                    to = 1024 + comp * 256 + j * 128
                    o_ref[rows, to : to + 128] = row[:, at : at + 128]


def gram_kernel(d_ref, e_ref, o_ref, rows, rhs, mid, edge):
    rows[0:1024, :] = d_ref[...].reshape(1024, 128).astype(F32)
    for p in range(16):
        lanes = slice(p * 128, p * 128 + 128)
        at = (p % 2) * 8 + p // 2
        rhs[0:32, lanes] = rows[pl.ds(at, 32, stride=32), :].astype(BF)
        rhs[32:64, lanes] = rows[pl.ds(16 + at, 32, stride=32), :].astype(BF)
    block = [e_ref[256:320, 384 + t * 128 : 448 + t * 128] for t in range(2)]
    turns = e_ref[256:512, 128:256].astype(F32) + e_ref[256:512, 256:384].astype(F32)
    tc, ts, ec, es = (turns[n * 64 : n * 64 + 64] for n in range(4))
    first = dot(block[0], rhs[...]) + dot(block[1], rhs[...])
    for p in range(16):
        g = first[:, p * 128 : p * 128 + 128]
        gr = jnp.concatenate([g[0:32], g[0:32]], axis=0)
        gi = jnp.concatenate([g[32:64], g[32:64]], axis=0)
        mid[:, p * 256 : p * 256 + 128] = (gr * tc + gi * ts).astype(BF)
        mid[:, p * 256 + 128 : p * 256 + 256] = (gi * tc - gr * ts).astype(BF)
    pieces = []
    for g in range(4):
        m = mid[:, g * 1024 : (g + 1) * 1024]
        pieces.append(
            (dot(m, e_ref[0:128, 0:1024], LAST) + dot(m, e_ref[128:256, 0:1024], LAST)).astype(BF)
        )
    spec = jnp.concatenate(pieces, axis=1)
    mixed = dot(e_ref[256:640, 0:64], spec)
    lane_slot = (lax.broadcasted_iota(jnp.int32, (64, 512), 1) % 32) // 4
    weighted = jnp.where(lane_slot == 0, mixed[0:64], 0.0)
    for k in range(1, SLOTS):
        weighted = jnp.where(lane_slot == k, mixed[k * 64 : k * 64 + 64], weighted)
    weighted = weighted.astype(BF)
    for g in range(4):
        w = weighted[:, g * 128 : g * 128 + 128]
        z = dot(w, e_ref[0:128, :]) + dot(w, e_ref[128:256, :])
        for v in range(4):
            p = g * 4 + v
            zr = z[:, v * 256 : v * 256 + 128]
            zi = z[:, v * 256 + 128 : v * 256 + 256]
            hr = zr * tc - zi * ts
            hi = zi * tc + zr * ts
            rhs[0:32, p * 128 : p * 128 + 128] = (hr[0:32] + hr[32:64]).astype(BF)
            rhs[32:64, p * 128 : p * 128 + 128] = (hi[0:32] + hi[32:64]).astype(BF)
        for j in range(2):
            zr = z[:, 1024 + j * 128 : 1152 + j * 128]
            zi = z[:, 1280 + j * 128 : 1408 + j * 128]
            hr = zr * ec - zi * es
            hi = zi * ec + zr * es
            lanes = slice((2 * g + j) * 128, (2 * g + j) * 128 + 128)
            edge[0:32, lanes] = (hr[0:32] + hr[32:64]).astype(BF)
            edge[32:64, lanes] = (hi[0:32] + hi[32:64]).astype(BF)
    last = dot(block[0], rhs[...], FIRST) + dot(block[1], rhs[...], FIRST)
    outer = dot(block[0][:, 0:32], edge[...], FIRST) + dot(block[1][:, 0:32], edge[...], FIRST)
    for p in range(16):
        lanes = slice(p * 128, p * 128 + 128)
        at = (p % 2) * 8 + p // 2
        rows[pl.ds(at, 32, stride=40), :] = last[0:32, lanes]
        rows[pl.ds(16 + at, 32, stride=40), :] = last[32:64, lanes]
    for v in range(8):
        rows[pl.ds(32 + v, 32, stride=40), :] = outer[:, v * 128 : v * 128 + 128]
    o_ref[...] = rows[...].reshape(32, 40, 128).astype(BF)


def band_kernel(taps_ref, strip_ref, down_ref):
    lane = lax.broadcasted_iota(jnp.int32, (64, 256), 1)
    for k in range(FRAMES):
        wide = jnp.broadcast_to(taps_ref[k : k + 1, :], (128, 256))
        band = pltpu.roll(wide, 0, 1, stride=1, stride_axis=0)
        high = band.astype(BF)
        low = band - high.astype(F32)
        strip_ref[0, k] = high
        strip_ref[1, k] = low.astype(BF)
        high = jnp.where(lane < 80, high[0:64].astype(F32), 0.0)
        low = jnp.where(lane < 80, low[0:64], 0.0)
        row = high + pltpu.roll(high, 80, 1) + pltpu.roll(low, 160, 1)
        down_ref[k * 64 : k * 64 + 64, :] = row.astype(BF)


def synth_kernel(
    where_ref, live_ref, dual_ref, sky_ref, dirty_ref, strip_ref, o_ref, head_ref, tail_ref, across
):
    channels = sky_ref.shape[0]
    row = lax.broadcasted_iota(jnp.int32, (80, WIDE), 0) + where_ref[2] * ROWS - RADIUS
    lane = lax.broadcasted_iota(jnp.int32, (80, WIDE), 1)
    col = lane + where_ref[3] * COLS - RADIUS
    inside = (row >= 0) & (row < PIXELS) & (col >= 0) & (col < PIXELS)
    for k in range(FRAMES):
        p = dual_ref[:, k + 1].reshape(channels * ROWS, COLS)
        both = jnp.concatenate([p[:, 0:128], p[:, 128:256]], axis=0)
        a = dot(both, strip_ref[0, k]) + dot(both, strip_ref[1, k])
        a0 = a[0 : channels * ROWS]
        a1 = a[channels * ROWS :]
        out = jnp.concatenate([a0[:, 0:128], a0[:, 128:256] + a1[:, 0:128], a1[:, 128:256]], axis=1)
        for c in range(channels):
            across[c, k * ROWS : (k + 1) * ROWS, :] = out[c * ROWS : (c + 1) * ROWS].astype(BF)
    live = lax.broadcasted_iota(jnp.int32, (ROWS, COLS), 0) < live_ref[0]
    none = jnp.zeros((ROWS, 128), F32)
    edge = jnp.zeros((8, WIDE), F32)
    for c in range(channels):
        total = None
        for t in range(2):
            for k in range(FRAMES):
                term = dot(
                    strip_ref[t, k][0:64, 0:128],
                    across[c, k * ROWS : (k + 1) * ROWS, :],
                    FIRST,
                )
                total = term if total is None else total + term
        sky = sky_ref[c]
        own = sky + STEP_PRIMAL * dirty_ref[c] - STEP_PRIMAL * dual_ref[c, 0].astype(F32)
        own = jnp.where(live, own, OUTSIDE)
        own = pltpu.roll(jnp.concatenate([own, none], axis=1), 8, 1)
        sky = pltpu.roll(jnp.concatenate([sky, none], axis=1), 8, 1)
        total = total[0:80] * (-STEP_PRIMAL)
        total = total + jnp.concatenate([edge, own, edge], axis=0)
        total = jnp.where(inside, total, OUTSIDE)
        total = jnp.where(lane < COLS + 2 * RADIUS, total, 0.0)
        sky = jnp.concatenate([edge, sky, edge], axis=0)
        for at, cells in ((c, total), (channels + c, sky)):
            o_ref[at] = cells
            head_ref[at] = cells[0:16].astype(BF)
            tail_ref[at] = cells[64:80].astype(BF)


def edge_kernel(base_ref, before_ref, after_ref, o_ref):
    both = base_ref.shape[0]
    lane = lax.broadcasted_iota(jnp.int32, (80, 128), 1)
    head = jnp.zeros((80, 128), F32)
    tail = jnp.zeros((80, 128), F32)
    for c in range(both):
        o_ref[c, 0:16, 0:WIDE] = base_ref[c, 0:16] + before_ref[c].astype(F32)
        o_ref[c, 16:64, 0:WIDE] = base_ref[c, 16:64]
        o_ref[c, 64:80, 0:WIDE] = base_ref[c, 64:80] + after_ref[c].astype(F32)
        first = o_ref[c, :, 0:128]
        final = o_ref[c, :, 256:384]
        if c < both // 2:
            at = 16 + 16 * c
            head = head + pltpu.roll(jnp.where(lane < 16, first, 0.0), at, 1)
            tail = tail + pltpu.roll(jnp.where(lane < 16, final, 0.0), at, 1)
        else:
            at = 80 + 8 * (c - both // 2)
            head = head + pltpu.roll(jnp.where((lane >= 8) & (lane < 16), first, 0.0), at - 8, 1)
            tail = tail + pltpu.roll(jnp.where(lane < 8, final, 0.0), at, 1)
    o_ref[0, :, WIDE:] = head
    o_ref[1, :, WIDE:] = tail
    for c in range(2, both):
        o_ref[c, :, WIDE:] = jnp.zeros((80, 128), F32)


def frames_kernel(
    bound_ref, where_ref, half_ref, base_ref, dual_ref, strip_ref, down_ref, image_ref, o_ref, probes, wide, down
):
    step = pl.program_id(0)
    channels = image_ref.shape[0]
    bound = bound_ref[step]

    def finish(analysis):
        cand = [dual_ref[c, 0].astype(F32) + STEP_DUAL * analysis(c) for c in range(channels)]
        square = cand[0] * cand[0]
        for c in range(1, channels):
            square = square + cand[c] * cand[c]
        factor = bound * lax.rsqrt(jnp.maximum(square, bound * bound))
        for c in range(channels):
            o_ref[c, 0] = (cand[c] * factor).astype(BF)

    @pl.when(step == 0)
    def _():
        wide[...] = jnp.zeros_like(wide)
        me = where_ref[3]
        last = half_ref.shape[0] - 1
        lane = lax.broadcasted_iota(jnp.int32, (80, 128), 1)
        left = half_ref[jnp.maximum(me - 1, 0), :, 256:384].astype(F32)
        left = jnp.where(me > 0, left, 0.0)
        right = half_ref[jnp.minimum(me + 1, last), :, 256:384].astype(F32)
        right = jnp.where(me < last, right, 0.0)
        for c in range(channels):
            gram = half_ref[2 * c].astype(F32) + half_ref[2 * c + 1].astype(F32)
            gram = [gram[:, 0:128], gram[:, 128:256], jnp.where(lane < 16, gram[:, 256:384], 0.0)]
            base = [base_ref[c, :, b * 128 : b * 128 + 128] for b in range(3)]
            sky = [base_ref[channels + c, :, b * 128 : b * 128 + 128] for b in range(3)]
            at = 16 + 16 * c
            base[0] = base[0] + jnp.where(lane < 16, pltpu.roll(left, 128 - at, 1), 0.0)
            base[2] = base[2] + jnp.where(lane < 16, pltpu.roll(right, 128 - at, 1), 0.0)
            at = 80 + 8 * c
            sky[0] = sky[0] + jnp.where(lane < 8, pltpu.roll(left, 128 - at, 1), 0.0)
            shown = (lane >= 8) & (lane < 16)
            sky[2] = sky[2] + jnp.where(shown, pltpu.roll(right, 136 - at, 1), 0.0)
            image = [jnp.maximum(base[b] - STEP_PRIMAL * gram[b], 0.0) for b in range(3)]
            probe = jnp.concatenate([2.0 * image[b] - sky[b] for b in range(3)], axis=1)
            image = pltpu.roll(jnp.concatenate(image, axis=1), WIDE - 8, 1)
            image_ref[c] = image[8:72, 0:256]
            probes[c] = pltpu.roll(probe, WIDE - 8, 1)[8:72, 0:256]
            high = probe.astype(BF)
            low = (probe - high.astype(F32)).astype(BF)
            wide[0:80, :] = high
            wide[80:160, :] = low
            wide[160:240, :] = high
            d = dot(down_ref[...], wide[...])
            high = d.astype(BF)
            down[0, c] = high
            down[1, c] = (d - high.astype(F32)).astype(BF)
        finish(lambda c: probes[c])

    @pl.when(step > 0)
    def _():
        at = pl.multiple_of((step - 1) * ROWS, ROWS)
        a = None
        for t in range(2):
            d = jnp.concatenate([down[t, c, pl.ds(at, ROWS), :] for c in range(channels)], axis=0)
            both = jnp.concatenate([d[:, 0:256], d[:, 128:384]], axis=0)
            if t == 0:
                band = jnp.concatenate([strip_ref[0, 0], strip_ref[1, 0]], axis=0)
                term = dot(both, band, LAST)
                a = term[:, 0:128] + term[:, 128:256]
            else:
                a = a + dot(both, strip_ref[0, 0], LAST)
        rows = channels * ROWS
        finish(
            lambda c: jnp.concatenate(
                [a[c * ROWS : c * ROWS + ROWS], a[rows + c * ROWS : rows + c * ROWS + ROWS]], axis=1
            )
        )


VM = pl.BlockSpec(memory_space=pltpu.VMEM)
SM = pl.BlockSpec(memory_space=pltpu.SMEM)


def call(kernel, out_shape, scratch, flops, moved, *args, scalars=0):
    return pl.pallas_call(
        kernel,
        out_shape=out_shape,
        in_specs=[SM] * scalars + [VM] * (len(args) - scalars),
        out_specs=jax.tree.map(lambda _: VM, out_shape),
        scratch_shapes=scratch,
        compiler_params=pltpu.CompilerParams(vmem_limit_bytes=VMEM_LIMIT),
        cost_estimate=pl.CostEstimate(flops=flops, bytes_accessed=moved, transcendentals=0),
    )(*args)


def after(values, event):
    return lax.optimization_barrier((*values, event))[:-1]


def body(
    sky_estimate,
    dual_coeffs,
    dirty_image,
    filters,
    thresholds,
    facet_rows,
    tile_slots,
    tile_count,
    gram_tiles,
):
    channels, tile_rows, tile_cols = sky_estimate.shape
    place = lax.axis_index("fou")
    where = jnp.stack([place >> 1, place & 1, lax.axis_index("img"), place]).astype(jnp.int32)

    sent = jnp.repeat(sky_estimate.astype(BF), 2, axis=0)
    lines = lax.all_to_all(sent, "fou", split_axis=0, concat_axis=0, tiled=True)

    line = np.stack(line_table())
    fold = fold_table()
    packed = call(
        forward_kernel,
        jax.ShapeDtypeStruct((PEERS_IMG, 32, 128), BF),
        [],
        1 << 29,
        1 << 20,
        where,
        lines,
        fold,
        line,
        scalars=1,
    )
    received = lax.all_to_all(packed, "img", split_axis=0, concat_axis=0, tiled=True)

    spread = call(
        tiles_kernel,
        jax.ShapeDtypeStruct((640, 1536), BF),
        [],
        1 << 23,
        1 << 20,
        where,
        tile_slots,
        tile_count,
        gram_tiles,
        np.stack(tile_table()),
        fixed_table(),
        scalars=3,
    )

    strip, down = call(
        band_kernel,
        (
            jax.ShapeDtypeStruct((2, FRAMES, 128, 256), BF),
            jax.ShapeDtypeStruct((FRAMES * ROWS, 256), BF),
        ),
        [],
        1 << 20,
        1 << 20,
        jnp.pad(filters, ((0, 0), (0, 256 - filters.shape[1]))),
    )
    ends = jax.ShapeDtypeStruct((2 * channels, 16, WIDE), BF)
    extended = jax.ShapeDtypeStruct((2 * channels, tile_rows + 16, WIDE), F32)
    (late_where,) = after((where,), packed)
    base, head, tail = call(
        synth_kernel,
        (extended, ends, ends),
        [pltpu.VMEM((channels, FRAMES * ROWS, WIDE), BF)],
        1 << 31,
        4 << 20,
        late_where,
        facet_rows,
        dual_coeffs,
        sky_estimate,
        dirty_image,
        strip,
        scalars=2,
    )
    (received,) = after((received,), head)

    scratch = [
        pltpu.VMEM((1280, 128), F32),
        pltpu.VMEM((64, 2048), BF),
        pltpu.VMEM((64, 4096), BF),
        pltpu.VMEM((64, 1024), BF),
    ]
    weighted = call(
        gram_kernel,
        jax.ShapeDtypeStruct((PEERS_IMG, 40, 128), BF),
        scratch,
        1 << 29,
        1 << 20,
        received,
        spread,
    )
    returned = lax.all_to_all(weighted, "img", split_axis=0, concat_axis=0, tiled=True)

    head, tail = after((head, tail), weighted)
    steps = [(i, i + 1) for i in range(PEERS_IMG - 1)]
    from_before = lax.ppermute(tail, "img", steps)
    from_after = lax.ppermute(head, "img", [(j, i) for i, j in steps])
    base = call(
        edge_kernel,
        jax.ShapeDtypeStruct((2 * channels, tile_rows + 16, WIDE + 128), F32),
        [],
        1 << 20,
        4 << 20,
        base,
        from_before,
        from_after,
    )
    blocks = call(
        inverse_kernel,
        jax.ShapeDtypeStruct((8, tile_rows + 16, WIDE), BF),
        [],
        1 << 29,
        1 << 20,
        where,
        returned,
        fold,
        line,
        base,
        scalars=1,
    )
    halves = lax.all_to_all(blocks, "fou", split_axis=0, concat_axis=0, tiled=True)

    dual_spec = pl.BlockSpec((channels, 1, tile_rows, tile_cols), lambda f: (0, f, 0, 0))
    whole = lambda a: pl.BlockSpec(a.shape, lambda f: (0,) * a.ndim)
    return pl.pallas_call(
        frames_kernel,
        out_shape=(
            jax.ShapeDtypeStruct(sky_estimate.shape, F32),
            jax.ShapeDtypeStruct(dual_coeffs.shape, BF),
        ),
        grid=(FRAMES + 1,),
        in_specs=[
            SM,
            SM,
            whole(halves),
            whole(base),
            dual_spec,
            pl.BlockSpec((2, 1, 128, 256), lambda f: (0, jnp.maximum(f - 1, 0), 0, 0)),
            whole(down),
        ],
        out_specs=(pl.BlockSpec(sky_estimate.shape, lambda f: (0, 0, 0)), dual_spec),
        scratch_shapes=[
            pltpu.VMEM(sky_estimate.shape, F32),
            pltpu.VMEM((256, 384), BF),
            pltpu.VMEM((2, channels, FRAMES * ROWS, 384), BF),
        ],
        compiler_params=pltpu.CompilerParams(vmem_limit_bytes=VMEM_LIMIT),
        cost_estimate=pl.CostEstimate(flops=1 << 31, bytes_accessed=3 << 20, transcendentals=0),
    )(thresholds, where, halves, base, dual_coeffs, strip, down)


def solution(mesh):
    in_specs = (
        P(None, "img", "fou"),
        P(None, None, "img", "fou"),
        P(None, "img", "fou"),
        P(),
        P(),
        P("img"),
        P(None, "img", None),
        P(None, "img"),
        P(None, "img", None, None, None),
    )
    out_specs = (P(None, "img", "fou"), P(None, None, "img", "fou"))
    return jax.shard_map(body, mesh=mesh, in_specs=in_specs, out_specs=out_specs, check_vma=False)
```

```python
import math

import jax
import jax.numpy as jnp
import numpy as np
from jax import lax
from jax.experimental import pallas as pl
from jax.experimental.pallas import tpu as pltpu
from jax.sharding import PartitionSpec as P

PIXELS = 2048
RADIUS = 8
SLOTS = 6
ROWS = 64
COLS = 256
FRAMES = 8
PEERS_IMG = 32
STEP_PRIMAL = 0.5
STEP_DUAL = 0.5
BF = jnp.bfloat16
F32 = jnp.float32
VMEM_LIMIT = 20 << 20
WIDE = 384
OUTSIDE = -1.0e30
LAST = ((1,), (1,))
FIRST = ((0,), (0,))


def two_terms_np(table):
    high = table.astype(jnp.bfloat16)
    low = (table - high.astype(np.float64)).astype(jnp.bfloat16)
    return high, low


def two_terms(table):
    high = table.astype(BF)
    return high, (table - high.astype(F32)).astype(BF)


def dot(a, b, dims=((1,), (0,))):
    return lax.dot_general(a, b, (dims, ((), ())), preferred_element_type=F32)


def angle_np(a, b, period):
    return 2.0 * np.pi * ((a[:, None] * b[None, :]) % period) / period


def line_table():
    ang = angle_np(np.arange(256), np.arange(256), 256)
    return two_terms_np(np.concatenate([np.cos(ang), np.sin(ang)], axis=1))


def block_table():
    ang = angle_np(np.arange(32), np.arange(32), 32)
    c, s = np.cos(ang), np.sin(ang)
    return two_terms_np(np.block([[c, s], [-s, c]]))


HALO = np.concatenate([np.arange(-8, 0), np.arange(64, 72)])


def turn_table():
    main = np.tile(np.arange(64), 2)
    halo = np.tile(HALO, 8)
    ang = [angle_np(np.arange(64), r, 2048) for r in (main, halo)]
    return two_terms_np(
        np.concatenate([np.cos(ang[0]), np.sin(ang[0]), np.cos(ang[1]), np.sin(ang[1])])
    )


def fixed_table():
    table = np.zeros((256, 512), jnp.bfloat16)
    for t in range(2):
        table[:, t * 128 : t * 128 + 128] = turn_table()[t]
        table[0:64, 256 + t * 128 : 320 + t * 128] = block_table()[t]
    return table


def tile_table():
    t = np.arange(32)
    ang = angle_np(t, np.arange(64), 32)
    c, s = np.cos(ang), np.sin(ang)
    main = np.zeros((32, 2, 2, 2, 2, 64))
    for p in range(2):
        main[:, p, 0, 0, p] = c
        main[:, p, 1, 0, p] = -s
        main[:, p, 0, 1, p] = s
        main[:, p, 1, 1, p] = c
    ang = angle_np(t, HALO, 32)
    c, s = np.cos(ang), np.sin(ang)
    halo = np.zeros((32, 2, 2, 2, 2, 2, 2, 2, 16))
    for p in range(2):
        for x in range(2):
            halo[:, p, 0, x, 0, 0, x, p] = c
            halo[:, p, 1, x, 0, 0, x, p] = -s
            halo[:, p, 0, x, 1, 0, x, p] = s
            halo[:, p, 1, x, 1, 0, x, p] = c
            halo[:, p, 0, x, 0, 1, x, p] = s
            halo[:, p, 1, x, 0, 1, x, p] = c
            halo[:, p, 0, x, 1, 1, x, p] = -c
            halo[:, p, 1, x, 1, 1, x, p] = s
    table = np.concatenate([main.reshape(128, 256), halo.reshape(128, 512)], axis=1)
    return two_terms_np(table)


def fold_table():
    freq = np.arange(2)[:, None] + 2 * np.arange(4)[None]
    pos = np.arange(4 * COLS).reshape(4, COLS)
    ang = 2.0 * np.pi * ((freq[:, :, None, None] * pos) % PIXELS) / PIXELS
    return np.stack([np.cos(ang), np.sin(ang)], axis=1).astype(np.float32)


def send_kernel(sky_ref, o_ref, taken, rounded, in_sem, out_sem):
    channels = taken.shape[0]

    def fetch(c):
        return pltpu.make_async_copy(sky_ref.at[c], taken.at[c], in_sem.at[c])

    def place(c, h):
        return pltpu.make_async_copy(rounded.at[c], o_ref.at[2 * c + h], out_sem.at[c, h])

    for c in range(channels):
        fetch(c).start()
    for c in range(channels):
        fetch(c).wait()
        rounded[c] = taken[c].astype(BF)
        for h in range(2):
            place(c, h).start()
    for c in range(channels):
        for h in range(2):
            place(c, h).wait()


def forward_kernel(par_ref, x_ref, fold_ref, line_ref, o_ref):
    par = par_ref[1]
    sign = (1 - 2 * par).astype(F32)
    xe = [x_ref[f].astype(F32) + sign * x_ref[f + 4].astype(F32) for f in range(4)]
    rows = [[], []]
    for cls in range(4):
        cos = fold_ref[par, 0, cls]
        sin = fold_ref[par, 1, cls]
        yr = xe[0] * cos[0:1]
        yi = xe[0] * sin[0:1]
        for f in range(1, 4):
            yr = yr + xe[f] * cos[f : f + 1]
            yi = yi + xe[f] * sin[f : f + 1]
        rows[0].append(jnp.concatenate([yr, -yi], axis=1).astype(BF))
        rows[1].append(jnp.concatenate([-yi, -yr], axis=1).astype(BF))
    for part in range(2):
        r = jnp.concatenate(rows[part], axis=0)
        out = dot(line_ref[0], r, LAST) + dot(line_ref[1], r, LAST)
        both = [out[:, chi * 128 : chi * 128 + 128].reshape(32, 8, 128) for chi in range(2)]
        both = jnp.concatenate(both, axis=1)
        o_ref[:, part * 16 : (part + 1) * 16, :] = both.astype(BF)


def inverse_kernel(par_ref, t_ref, fold_ref, line_ref, base_ref, o_ref):
    par = par_ref[1]
    me = par_ref[3]
    sign = (1 - 2 * par).astype(F32)
    re = t_ref[:, 0:16, :].astype(F32)
    im = t_ref[:, 16:32, :].astype(F32)
    edge = t_ref[:, 32:40, :].astype(F32)
    data = [re[:, 0:8], im[:, 0:8], re[:, 8:16], im[:, 8:16], edge]
    data = jnp.concatenate([d.reshape(256, 128).astype(BF) for d in data], axis=1)
    wave = dot(data, line_ref[0], FIRST) + dot(data, line_ref[1], FIRST)

    def joined(a, b):
        return jnp.concatenate([a[:, 0:256] - b[:, 256:512], a[:, 256:512] + b[:, 0:256]], axis=1)

    h = joined(wave[512:576], wave[576:640])
    total = [None] * 4
    for chi in range(2):
        u = joined(wave[chi * 256 : chi * 256 + 128], wave[chi * 256 + 128 : chi * 256 + 256])
        for clo in range(2):
            cls = 2 * chi + clo
            e = h[cls * 16 : cls * 16 + 16]
            whole = jnp.concatenate([e[0:8], u[clo * 64 : clo * 64 + 64], e[8:16]], axis=0)
            ur = whole[:, 0:256]
            ui = whole[:, 256:512]
            cos = fold_ref[par, 0, cls]
            sin = fold_ref[par, 1, cls]
            for f in range(4):
                g = ur * cos[f : f + 1] - ui * sin[f : f + 1]
                total[f] = g if total[f] is None else total[f] + g
    scale = 1.0 / (PIXELS * PIXELS)
    total = [g * scale for g in total]
    total = total + [sign * g for g in total]
    none = jnp.zeros((80, 128), F32)
    lane = lax.broadcasted_iota(jnp.int32, (80, 128), 1)
    for f in range(8):
        before = total[f - 1][:, 128:256] if f > 0 else none
        after = total[f + 1][:, 0:128] if f < 7 else none
        line = jnp.concatenate([before, total[f], after], axis=1)
        line = pltpu.roll(line, 512 - 120, 1)
        pack = jnp.where(f == me - 1, base_ref[0, :, 256:384], 0.0)
        pack = pack + jnp.where(f == me + 1, base_ref[1, :, 256:384], 0.0)
        o_ref[f, :, 0:256] = line[:, 0:256].astype(BF)
        o_ref[f, :, 256:384] = jnp.where(lane < 16, line[:, 256:384], pack).astype(BF)


def tiles_kernel(where_ref, slots_ref, count_ref, tiles_ref, table_ref, fixed_ref, o_ref):
    channel = where_ref[0]
    left = lax.broadcasted_iota(jnp.int32, (32, 128), 0)
    right = lax.broadcasted_iota(jnp.int32, (32, 128), 1)
    tile = jnp.full((32, 128), -1, jnp.int32)
    for k in range(SLOTS):
        slot = jnp.where(k < count_ref[channel, 0], slots_ref[channel, 0, k], -1)
        tile = jnp.where(left // 4 == k, slot, tile)
    pick = (tile == right // 4) & (left % 4 == right % 4)
    pick = jnp.where(pick, 1.0, 0.0).astype(BF)
    o_ref[...] = jnp.zeros_like(o_ref)
    for k in range(SLOTS):
        o_ref[256 + k * 64 : 320 + k * 64, 0:64] = tiles_ref[channel, 0, k].astype(F32).T.astype(BF)
    o_ref[256:512, 128:640] = fixed_ref[...]
    for t in range(2):
        row = dot(pick, table_ref[t]).astype(BF)
        for j in range(2):
            for chi in range(2):
                p = 2 * j + chi
                rows = slice(t * 128 + p * 32, t * 128 + p * 32 + 32)
                o_ref[rows, p * 256 : p * 256 + 256] = row[:, 0:256]
                for comp in range(2):
                    at = 256 + chi * 256 + comp * 128
                    to = 1024 + comp * 256 + j * 128
                    o_ref[rows, to : to + 128] = row[:, at : at + 128]


def gram_kernel(d_ref, e_ref, o_ref, rows, rhs, mid, edge):
    rows[0:1024, :] = d_ref[...].reshape(1024, 128).astype(F32)
    for p in range(16):
        lanes = slice(p * 128, p * 128 + 128)
        at = (p % 2) * 8 + p // 2
        rhs[0:32, lanes] = rows[pl.ds(at, 32, stride=32), :].astype(BF)
        rhs[32:64, lanes] = rows[pl.ds(16 + at, 32, stride=32), :].astype(BF)
    block = [e_ref[256:320, 384 + t * 128 : 448 + t * 128] for t in range(2)]
    turns = e_ref[256:512, 128:256].astype(F32) + e_ref[256:512, 256:384].astype(F32)
    tc, ts, ec, es = (turns[n * 64 : n * 64 + 64] for n in range(4))
    first = dot(jnp.concatenate(block, axis=0), rhs[...])
    first = first[0:64] + first[64:128]
    for p in range(16):
        g = first[:, p * 128 : p * 128 + 128]
        gr = jnp.concatenate([g[0:32], g[0:32]], axis=0)
        gi = jnp.concatenate([g[32:64], g[32:64]], axis=0)
        down = slice(p // 4 * 64, p // 4 * 64 + 64)
        at = p % 4 * 256
        mid[down, at : at + 128] = (gr * tc + gi * ts).astype(BF)
        mid[down, at + 128 : at + 256] = (gi * tc - gr * ts).astype(BF)
    spec = dot(mid[...], e_ref[0:256, 0:1024], LAST)
    spec = (spec[:, 0:128] + spec[:, 128:256]).astype(BF)
    spec = jnp.concatenate([spec[g * 64 : g * 64 + 64] for g in range(4)], axis=1)
    mixed = dot(e_ref[256:640, 0:64], spec)
    lane_slot = (lax.broadcasted_iota(jnp.int32, (64, 512), 1) % 32) // 4
    weighted = jnp.where(lane_slot == 0, mixed[0:64], 0.0)
    for k in range(1, SLOTS):
        weighted = jnp.where(lane_slot == k, mixed[k * 64 : k * 64 + 64], weighted)
    weighted = weighted.astype(BF)
    w = jnp.concatenate([weighted[:, g * 128 : g * 128 + 128] for g in range(4)], axis=0)
    spreads = dot(jnp.concatenate([w, w], axis=1), e_ref[0:256, :])
    for g in range(4):
        z = spreads[g * 64 : g * 64 + 64]
        for v in range(4):
            p = g * 4 + v
            zr = z[:, v * 256 : v * 256 + 128]
            zi = z[:, v * 256 + 128 : v * 256 + 256]
            hr = zr * tc - zi * ts
            hi = zi * tc + zr * ts
            rhs[0:32, p * 128 : p * 128 + 128] = (hr[0:32] + hr[32:64]).astype(BF)
            rhs[32:64, p * 128 : p * 128 + 128] = (hi[0:32] + hi[32:64]).astype(BF)
        for j in range(2):
            zr = z[:, 1024 + j * 128 : 1152 + j * 128]
            zi = z[:, 1280 + j * 128 : 1408 + j * 128]
            hr = zr * ec - zi * es
            hi = zi * ec + zr * es
            lanes = slice((2 * g + j) * 128, (2 * g + j) * 128 + 128)
            edge[0:32, lanes] = (hr[0:32] + hr[32:64]).astype(BF)
            edge[32:64, lanes] = (hi[0:32] + hi[32:64]).astype(BF)
    block = jnp.concatenate(block, axis=1)
    last = dot(block, rhs[...], FIRST)
    last = last[0:64] + last[64:128]
    outer = dot(block, edge[...], FIRST)
    outer = outer[0:32] + outer[64:96]
    for p in range(16):
        lanes = slice(p * 128, p * 128 + 128)
        at = (p % 2) * 8 + p // 2
        rows[pl.ds(at, 32, stride=40), :] = last[0:32, lanes]
        rows[pl.ds(16 + at, 32, stride=40), :] = last[32:64, lanes]
    for v in range(8):
        rows[pl.ds(32 + v, 32, stride=40), :] = outer[:, v * 128 : v * 128 + 128]
    o_ref[...] = rows[...].reshape(32, 40, 128).astype(BF)


def band_kernel(taps_ref, strip_ref):
    for k in range(FRAMES):
        wide = jnp.broadcast_to(taps_ref[k : k + 1, :], (128, 256))
        band = pltpu.roll(wide, 0, 1, stride=1, stride_axis=0)
        high = band.astype(BF)
        strip_ref[0, k] = high
        strip_ref[1, k] = (band - high.astype(F32)).astype(BF)


def bands_kernel(taps_ref, o_ref):
    lane = lax.broadcasted_iota(jnp.int32, (64, 256), 1)
    for k in range(FRAMES):
        wide = jnp.broadcast_to(taps_ref[k : k + 1, :], (128, 256))
        band = pltpu.roll(wide, 0, 1, stride=1, stride_axis=0)
        high = band.astype(BF)
        low = band - high.astype(F32)
        o_ref[k * 128 : k * 128 + 128, :] = high
        o_ref[1024 + k * 128 : 1152 + k * 128, :] = low.astype(BF)
        low = jnp.where(lane < 80, low[0:64], 0.0)
        high = jnp.where(lane < 80, high[0:64].astype(F32), 0.0)
        row = high + pltpu.roll(high, 80, 1) + pltpu.roll(low, 160, 1)
        o_ref[2048 + k * 64 : 2112 + k * 64, :] = row.astype(BF)


def synth_kernel(
    where_ref, live_ref, dual_ref, sky_ref, dirty_ref, strip_ref, o_ref, across
):
    channels = sky_ref.shape[0]
    row = lax.broadcasted_iota(jnp.int32, (80, WIDE), 0) + where_ref[2] * ROWS - RADIUS
    lane = lax.broadcasted_iota(jnp.int32, (80, WIDE), 1)
    col = lane + where_ref[3] * COLS - RADIUS
    inside = (row >= 0) & (row < PIXELS) & (col >= 0) & (col < PIXELS)
    for k in range(FRAMES):
        p = dual_ref[:, k + 1].reshape(channels * ROWS, COLS)
        both = jnp.concatenate([p[:, 0:128], p[:, 128:256]], axis=0)
        a = dot(both, strip_ref[0, k]) + dot(both, strip_ref[1, k])
        a0 = a[0 : channels * ROWS]
        a1 = a[channels * ROWS :]
        out = jnp.concatenate([a0[:, 0:128], a0[:, 128:256] + a1[:, 0:128], a1[:, 128:256]], axis=1)
        for c in range(channels):
            across[c, k * ROWS : (k + 1) * ROWS, :] = out[c * ROWS : (c + 1) * ROWS].astype(BF)
    live = lax.broadcasted_iota(jnp.int32, (ROWS, COLS), 0) < live_ref[0]
    none = jnp.zeros((ROWS, 128), F32)
    edge = jnp.zeros((8, WIDE), F32)
    for c in range(channels):
        total = None
        for t in range(2):
            for k in range(FRAMES):
                term = dot(
                    strip_ref[t, k][0:64, 0:128],
                    across[c, k * ROWS : (k + 1) * ROWS, :],
                    FIRST,
                )
                total = term if total is None else total + term
        sky = sky_ref[c]
        own = sky + STEP_PRIMAL * dirty_ref[c] - STEP_PRIMAL * dual_ref[c, 0].astype(F32)
        own = jnp.where(live, own, OUTSIDE)
        own = pltpu.roll(jnp.concatenate([own, none], axis=1), 8, 1)
        sky = pltpu.roll(jnp.concatenate([sky, none], axis=1), 8, 1)
        total = total[0:80] * (-STEP_PRIMAL)
        total = total + jnp.concatenate([edge, own, edge], axis=0)
        total = jnp.where(inside, total, OUTSIDE)
        total = jnp.where(lane < COLS + 2 * RADIUS, total, 0.0)
        sky = jnp.concatenate([edge, sky, edge], axis=0)
        o_ref[c] = total
        o_ref[channels + c] = sky


def head_kernel(base_ref, o_ref):
    o_ref[...] = base_ref[:, 0:16].astype(BF)


def tail_kernel(base_ref, o_ref):
    o_ref[...] = base_ref[:, 64:80].astype(BF)


def take_kernel(where_ref, dual_ref, o_ref):
    o_ref[...] = dual_ref[...]


def edge_kernel(base_ref, before_ref, after_ref, o_ref):
    both = base_ref.shape[0]
    lane = lax.broadcasted_iota(jnp.int32, (80, 128), 1)
    head = jnp.zeros((80, 128), F32)
    tail = jnp.zeros((80, 128), F32)
    for c in range(both):
        o_ref[c, 0:16] = base_ref[c, 0:16] + before_ref[c].astype(F32)
        o_ref[c, 16:64] = base_ref[c, 16:64]
        o_ref[c, 64:80] = base_ref[c, 64:80] + after_ref[c].astype(F32)
        first = o_ref[c, :, 0:128]
        final = o_ref[c, :, 256:384]
        if c < both // 2:
            at = 16 + 16 * c
            head = head + pltpu.roll(jnp.where(lane < 16, first, 0.0), at, 1)
            tail = tail + pltpu.roll(jnp.where(lane < 16, final, 0.0), at, 1)
        else:
            at = 80 + 8 * (c - both // 2)
            head = head + pltpu.roll(jnp.where((lane >= 8) & (lane < 16), first, 0.0), at - 8, 1)
            tail = tail + pltpu.roll(jnp.where(lane < 8, final, 0.0), at, 1)
    o_ref[0, :, 256:384] = o_ref[0, :, 256:384] + head
    o_ref[1, :, 256:384] = o_ref[1, :, 256:384] + tail


def frames_kernel(
    bound_ref,
    where_ref,
    half_ref,
    base_ref,
    dual_ref,
    bands_ref,
    image_ref,
    o_ref,
    given,
    image_buf,
    dual_buf,
    probes,
    wide,
    down,
    given_sem,
    image_sem,
    dual_sem,
):
    channels = image_buf.shape[0]
    rows = channels * ROWS

    def given_copy(k):
        return pltpu.make_async_copy(dual_ref.at[:, k], given.at[k], given_sem.at[k])

    for k in range(FRAMES + 1):
        given_copy(k).start()

    def dual_copy(k):
        return pltpu.make_async_copy(dual_buf.at[k], o_ref.at[:, k], dual_sem.at[k])

    def finish(k, analysis):
        bound = bound_ref[k]
        given_copy(k).wait()
        cand = [given[k, c].astype(F32) + STEP_DUAL * analysis(c) for c in range(channels)]
        square = cand[0] * cand[0]
        for c in range(1, channels):
            square = square + cand[c] * cand[c]
        factor = bound * lax.rsqrt(jnp.maximum(square, bound * bound))
        for c in range(channels):
            dual_buf[k, c] = (cand[c] * factor).astype(BF)
        dual_copy(k).start()

    wide[...] = jnp.zeros_like(wide)
    me = where_ref[3]
    last = half_ref.shape[0] - 1
    lane = lax.broadcasted_iota(jnp.int32, (80, 128), 1)
    left = half_ref[jnp.maximum(me - 1, 0), :, 256:384].astype(F32)
    left = jnp.where(me > 0, left, 0.0)
    right = half_ref[jnp.minimum(me + 1, last), :, 256:384].astype(F32)
    right = jnp.where(me < last, right, 0.0)
    for c in range(channels):
        gram = half_ref[2 * c].astype(F32) + half_ref[2 * c + 1].astype(F32)
        gram = [gram[:, 0:128], gram[:, 128:256], jnp.where(lane < 16, gram[:, 256:384], 0.0)]
        base = [base_ref[c, :, b * 128 : b * 128 + 128] for b in range(3)]
        sky = [base_ref[channels + c, :, b * 128 : b * 128 + 128] for b in range(3)]
        base[2] = jnp.where(lane < 16, base[2], 0.0)
        at = 16 + 16 * c
        base[0] = base[0] + jnp.where(lane < 16, pltpu.roll(left, 128 - at, 1), 0.0)
        base[2] = base[2] + jnp.where(lane < 16, pltpu.roll(right, 128 - at, 1), 0.0)
        at = 80 + 8 * c
        sky[0] = sky[0] + jnp.where(lane < 8, pltpu.roll(left, 128 - at, 1), 0.0)
        shown = (lane >= 8) & (lane < 16)
        sky[2] = sky[2] + jnp.where(shown, pltpu.roll(right, 136 - at, 1), 0.0)
        image = [jnp.maximum(base[b] - STEP_PRIMAL * gram[b], 0.0) for b in range(3)]
        probe = jnp.concatenate([2.0 * image[b] - sky[b] for b in range(3)], axis=1)
        image = pltpu.roll(jnp.concatenate(image, axis=1), WIDE - 8, 1)
        image_buf[c] = image[8:72, 0:256]
        probes[c] = pltpu.roll(probe, WIDE - 8, 1)[8:72, 0:256]
        high = probe.astype(BF)
        low = (probe - high.astype(F32)).astype(BF)
        wide[0:80, :] = high
        wide[80:160, :] = low
        wide[160:240, :] = high
        d = dot(bands_ref[2048:2560, :], wide[...])
        high = d.astype(BF)
        down[0, c] = high
        down[1, c] = (d - high.astype(F32)).astype(BF)
    image_copy = pltpu.make_async_copy(image_buf, image_ref, image_sem)
    image_copy.start()
    finish(0, lambda c: probes[c])
    for k in range(1, FRAMES + 1):
        at = (k - 1) * ROWS
        a = None
        for t in range(2):
            d = jnp.concatenate([down[t, c, at : at + ROWS, :] for c in range(channels)], axis=0)
            both = jnp.concatenate([d[:, 0:256], d[:, 128:384]], axis=0)
            high = bands_ref[(k - 1) * 128 : k * 128, :]
            if t == 0:
                band = jnp.concatenate([high, bands_ref[896 + k * 128 : 1024 + k * 128, :]], axis=0)
                term = dot(both, band, LAST)
                a = term[:, 0:128] + term[:, 128:256]
            else:
                a = a + dot(both, high, LAST)
        finish(
            k,
            lambda c: jnp.concatenate(
                [a[c * ROWS : c * ROWS + ROWS], a[rows + c * ROWS : rows + c * ROWS + ROWS]], axis=1
            ),
        )
    image_copy.wait()
    for k in range(FRAMES + 1):
        dual_copy(k).wait()


VM = pl.BlockSpec(memory_space=pltpu.VMEM)
SM = pl.BlockSpec(memory_space=pltpu.SMEM)


def call(kernel, out_shape, scratch, flops, moved, *args, scalars=0):
    return pl.pallas_call(
        kernel,
        out_shape=out_shape,
        in_specs=[SM] * scalars + [VM] * (len(args) - scalars),
        out_specs=jax.tree.map(lambda _: VM, out_shape),
        scratch_shapes=scratch,
        compiler_params=pltpu.CompilerParams(vmem_limit_bytes=VMEM_LIMIT),
        cost_estimate=pl.CostEstimate(flops=flops, bytes_accessed=moved, transcendentals=0),
    )(*args)


def frames_call(thresholds, where, halves, base, dual, bands):
    channels = dual.shape[0]
    block = (channels, ROWS, COLS)
    return pl.pallas_call(
        frames_kernel,
        out_shape=(jax.ShapeDtypeStruct(block, F32), jax.ShapeDtypeStruct(dual.shape, BF)),
        in_specs=[SM, SM, VM, VM, pl.BlockSpec(memory_space=pltpu.HBM), VM],
        out_specs=(pl.BlockSpec(memory_space=pl.ANY), pl.BlockSpec(memory_space=pl.ANY)),
        scratch_shapes=[
            pltpu.VMEM((FRAMES + 1, *block), BF),
            pltpu.VMEM(block, F32),
            pltpu.VMEM((FRAMES + 1, *block), BF),
            pltpu.VMEM(block, F32),
            pltpu.VMEM((256, WIDE), BF),
            pltpu.VMEM((2, channels, FRAMES * ROWS, WIDE), BF),
            pltpu.SemaphoreType.DMA((FRAMES + 1,)),
            pltpu.SemaphoreType.DMA(()),
            pltpu.SemaphoreType.DMA((FRAMES + 1,)),
        ],
        compiler_params=pltpu.CompilerParams(vmem_limit_bytes=VMEM_LIMIT),
        cost_estimate=pl.CostEstimate(flops=1 << 31, bytes_accessed=3 << 20, transcendentals=0),
    )(thresholds, where, halves, base, dual, bands)


def after(values, *events):
    return lax.optimization_barrier((*values, *events))[: len(values)]


def body(
    sky_estimate,
    dual_coeffs,
    dirty_image,
    filters,
    thresholds,
    facet_rows,
    tile_slots,
    tile_count,
    gram_tiles,
):
    channels, tile_rows, tile_cols = sky_estimate.shape
    place = lax.axis_index("fou")
    where = jnp.stack([place >> 1, place & 1, lax.axis_index("img"), place]).astype(jnp.int32)

    sent = pl.pallas_call(
        send_kernel,
        out_shape=jax.ShapeDtypeStruct((2 * channels, tile_rows, tile_cols), BF),
        in_specs=[pl.BlockSpec(memory_space=pltpu.HBM)],
        out_specs=pl.BlockSpec(memory_space=pltpu.HBM),
        scratch_shapes=[
            pltpu.VMEM(sky_estimate.shape, F32),
            pltpu.VMEM(sky_estimate.shape, BF),
            pltpu.SemaphoreType.DMA((channels,)),
            pltpu.SemaphoreType.DMA((channels, 2)),
        ],
        compiler_params=pltpu.CompilerParams(vmem_limit_bytes=62 << 20),
    )(sky_estimate)
    lines = lax.all_to_all(sent, "fou", split_axis=0, concat_axis=0, tiled=True)

    spread = call(
        tiles_kernel,
        jax.ShapeDtypeStruct((640, 1536), BF),
        [],
        1 << 23,
        1 << 20,
        where,
        tile_slots,
        tile_count,
        gram_tiles,
        np.stack(tile_table()),
        fixed_table(),
        scalars=3,
    )

    taps = jnp.pad(filters, ((0, 0), (0, 256 - filters.shape[1])))
    strip = call(
        band_kernel, jax.ShapeDtypeStruct((2, FRAMES, 128, 256), BF), [], 1 << 20, 1 << 20, taps
    )

    (ready_where,) = after((where,), strip)

    line = np.stack(line_table())
    fold = fold_table()
    packed = call(
        forward_kernel,
        jax.ShapeDtypeStruct((PEERS_IMG, 32, 128), BF),
        [],
        1 << 29,
        1 << 20,
        ready_where,
        lines,
        fold,
        line,
        scalars=1,
    )
    received = lax.all_to_all(packed, "img", split_axis=0, concat_axis=0, tiled=True)

    extended = jax.ShapeDtypeStruct((2 * channels, tile_rows + 16, WIDE), F32)
    (late_where,) = after((where,), packed)
    base = call(
        synth_kernel,
        extended,
        [pltpu.VMEM((channels, FRAMES * ROWS, WIDE), BF)],
        1 << 31,
        4 << 20,
        late_where,
        facet_rows,
        dual_coeffs,
        sky_estimate,
        dirty_image,
        strip,
        scalars=2,
    )
    ends = jax.ShapeDtypeStruct((2 * channels, 16, WIDE), BF)
    head = call(head_kernel, ends, [], 1 << 16, 1 << 18, base)
    tail = call(tail_kernel, ends, [], 1 << 16, 1 << 18, base)
    (received,) = after((received,), head, tail)

    scratch = [
        pltpu.VMEM((1280, 128), F32),
        pltpu.VMEM((64, 2048), BF),
        pltpu.VMEM((256, 1024), BF),
        pltpu.VMEM((64, 1024), BF),
    ]
    weighted = call(
        gram_kernel,
        jax.ShapeDtypeStruct((PEERS_IMG, 40, 128), BF),
        scratch,
        1 << 29,
        1 << 20,
        received,
        spread,
    )
    returned = lax.all_to_all(weighted, "img", split_axis=0, concat_axis=0, tiled=True)

    head, tail = after((head, tail), weighted)
    steps = [(i, i + 1) for i in range(PEERS_IMG - 1)]
    from_before = lax.ppermute(tail, "img", steps)
    from_after = lax.ppermute(head, "img", [(j, i) for i, j in steps])
    base = call(
        edge_kernel,
        extended,
        [],
        1 << 20,
        4 << 20,
        base,
        from_before,
        from_after,
    )
    blocks = call(
        inverse_kernel,
        jax.ShapeDtypeStruct((8, tile_rows + 16, WIDE), BF),
        [],
        1 << 29,
        1 << 20,
        where,
        returned,
        fold,
        line,
        base,
        scalars=1,
    )
    halves = lax.all_to_all(blocks, "fou", split_axis=0, concat_axis=0, tiled=True)

    (late_taps,) = after((taps,), blocks)
    bands = call(
        bands_kernel, jax.ShapeDtypeStruct((2560, 256), BF), [], 1 << 20, 1 << 20, late_taps
    )
    return frames_call(thresholds, where, halves, base, pltpu.with_memory_space_constraint(dual_coeffs, pltpu.HBM), bands)


def solution(mesh):
    in_specs = (
        P(None, "img", "fou"),
        P(None, None, "img", "fou"),
        P(None, "img", "fou"),
        P(),
        P(),
        P("img"),
        P(None, "img", None),
        P(None, "img"),
        P(None, "img", None, None, None),
    )
    out_specs = (P(None, "img", "fou"), P(None, None, "img", "fou"))
    return jax.shard_map(body, mesh=mesh, in_specs=in_specs, out_specs=out_specs, check_vma=False)
```

```python
import math

import jax
import jax.numpy as jnp
import numpy as np
from jax import lax
from jax.experimental import pallas as pl
from jax.experimental.pallas import tpu as pltpu
from jax.sharding import PartitionSpec as P

PIXELS = 2048
RADIUS = 8
SLOTS = 6
ROWS = 64
COLS = 256
FRAMES = 8
PEERS_IMG = 32
STEP_PRIMAL = 0.5
STEP_DUAL = 0.5
BF = jnp.bfloat16
F32 = jnp.float32
VMEM_LIMIT = 20 << 20
WIDE = 384
OUTSIDE = -1.0e30
LAST = ((1,), (1,))
FIRST = ((0,), (0,))


def two_terms_np(table):
    high = table.astype(jnp.bfloat16)
    low = (table - high.astype(np.float64)).astype(jnp.bfloat16)
    return high, low


def two_terms(table):
    high = table.astype(BF)
    return high, (table - high.astype(F32)).astype(BF)


def dot(a, b, dims=((1,), (0,))):
    return lax.dot_general(a, b, (dims, ((), ())), preferred_element_type=F32)


def angle_np(a, b, period):
    return 2.0 * np.pi * ((a[:, None] * b[None, :]) % period) / period


def line_table():
    ang = angle_np(np.arange(256), np.arange(256), 256)
    return two_terms_np(np.concatenate([np.cos(ang), np.sin(ang)], axis=1))


def block_table():
    ang = angle_np(np.arange(32), np.arange(32), 32)
    c, s = np.cos(ang), np.sin(ang)
    return two_terms_np(np.block([[c, s], [-s, c]]))


HALO = np.concatenate([np.arange(-8, 0), np.arange(64, 72)])


def turn_table():
    main = np.tile(np.arange(64), 2)
    halo = np.tile(HALO, 8)
    ang = [angle_np(np.arange(64), r, 2048) for r in (main, halo)]
    return two_terms_np(
        np.concatenate([np.cos(ang[0]), np.sin(ang[0]), np.cos(ang[1]), np.sin(ang[1])])
    )


def fixed_table():
    table = np.zeros((256, 512), jnp.bfloat16)
    for t in range(2):
        table[:, t * 128 : t * 128 + 128] = turn_table()[t]
        table[0:64, 256 + t * 128 : 320 + t * 128] = block_table()[t]
    return table


def tile_table():
    t = np.arange(32)
    ang = angle_np(t, np.arange(64), 32)
    c, s = np.cos(ang), np.sin(ang)
    main = np.zeros((32, 2, 2, 2, 2, 64))
    for p in range(2):
        main[:, p, 0, 0, p] = c
        main[:, p, 1, 0, p] = -s
        main[:, p, 0, 1, p] = s
        main[:, p, 1, 1, p] = c
    ang = angle_np(t, HALO, 32)
    c, s = np.cos(ang), np.sin(ang)
    halo = np.zeros((32, 2, 2, 2, 2, 2, 2, 2, 16))
    for p in range(2):
        for x in range(2):
            halo[:, p, 0, x, 0, 0, x, p] = c
            halo[:, p, 1, x, 0, 0, x, p] = -s
            halo[:, p, 0, x, 1, 0, x, p] = s
            halo[:, p, 1, x, 1, 0, x, p] = c
            halo[:, p, 0, x, 0, 1, x, p] = s
            halo[:, p, 1, x, 0, 1, x, p] = c
            halo[:, p, 0, x, 1, 1, x, p] = -c
            halo[:, p, 1, x, 1, 1, x, p] = s
    table = np.concatenate([main.reshape(128, 256), halo.reshape(128, 512)], axis=1)
    return two_terms_np(table)


def wave_table():
    freq = np.arange(2)[:, None] + 2 * np.arange(4)[None]
    pos = np.arange(4 * COLS).reshape(4, COLS)
    ang = 2.0 * np.pi * ((freq[:, :, None, None] * pos) % PIXELS) / PIXELS
    fold = np.concatenate([np.cos(ang), np.sin(ang)], axis=3).reshape(32, 2 * COLS)
    return np.concatenate([np.stack(line_table()), np.stack(two_terms_np(fold))], axis=1)


def fold_rows(line_ref, par):
    at = pl.multiple_of(256 + 16 * par, 16)
    fold = line_ref[0, pl.ds(at, 16), :].astype(F32) + line_ref[1, pl.ds(at, 16), :].astype(F32)
    return fold[:, 0:256], fold[:, 256:512]


def hold_kernel(table_ref, o_ref):
    o_ref[...] = table_ref[...]


def send_kernel(sky_ref, o_ref, taken, rounded, in_sem, out_sem):
    channels = taken.shape[0]

    def fetch(c):
        return pltpu.make_async_copy(sky_ref.at[c], taken.at[c], in_sem.at[c])

    def place(c, h):
        return pltpu.make_async_copy(rounded.at[c], o_ref.at[2 * c + h], out_sem.at[c, h])

    for c in range(channels):
        fetch(c).start()
    for c in range(channels):
        fetch(c).wait()
        rounded[c] = taken[c].astype(BF)
        for h in range(2):
            place(c, h).start()
    for c in range(channels):
        for h in range(2):
            place(c, h).wait()


def forward_kernel(par_ref, x_ref, line_ref, o_ref):
    par = par_ref[1]
    folds = fold_rows(line_ref, par)
    sign = (1 - 2 * par).astype(F32)
    xe = [x_ref[f].astype(F32) + sign * x_ref[f + 4].astype(F32) for f in range(4)]
    rows = [[], []]
    for cls in range(4):
        cos = folds[0][cls * 4 : cls * 4 + 4]
        sin = folds[1][cls * 4 : cls * 4 + 4]
        yr = xe[0] * cos[0:1]
        yi = xe[0] * sin[0:1]
        for f in range(1, 4):
            yr = yr + xe[f] * cos[f : f + 1]
            yi = yi + xe[f] * sin[f : f + 1]
        rows[0].append(jnp.concatenate([yr, -yi], axis=1).astype(BF))
        rows[1].append(jnp.concatenate([-yi, -yr], axis=1).astype(BF))
    for part in range(2):
        r = jnp.concatenate(rows[part], axis=0)
        out = dot(line_ref[0, 0:256], r, LAST) + dot(line_ref[1, 0:256], r, LAST)
        both = [out[:, chi * 128 : chi * 128 + 128].reshape(32, 8, 128) for chi in range(2)]
        both = jnp.concatenate(both, axis=1)
        o_ref[:, part * 16 : (part + 1) * 16, :] = both.astype(BF)


def inverse_kernel(par_ref, t_ref, line_ref, base_ref, o_ref):
    par = par_ref[1]
    folds = fold_rows(line_ref, par)
    me = par_ref[3]
    sign = (1 - 2 * par).astype(F32)
    re = t_ref[:, 0:16, :].astype(F32)
    im = t_ref[:, 16:32, :].astype(F32)
    edge = t_ref[:, 32:40, :].astype(F32)
    data = [re[:, 0:8], im[:, 0:8], re[:, 8:16], im[:, 8:16], edge]
    data = jnp.concatenate([d.reshape(256, 128).astype(BF) for d in data], axis=1)
    wave = dot(data, line_ref[0, 0:256], FIRST) + dot(data, line_ref[1, 0:256], FIRST)

    def joined(a, b):
        return jnp.concatenate([a[:, 0:256] - b[:, 256:512], a[:, 256:512] + b[:, 0:256]], axis=1)

    h = joined(wave[512:576], wave[576:640])
    total = [None] * 4
    for chi in range(2):
        u = joined(wave[chi * 256 : chi * 256 + 128], wave[chi * 256 + 128 : chi * 256 + 256])
        for clo in range(2):
            cls = 2 * chi + clo
            e = h[cls * 16 : cls * 16 + 16]
            whole = jnp.concatenate([e[0:8], u[clo * 64 : clo * 64 + 64], e[8:16]], axis=0)
            ur = whole[:, 0:256]
            ui = whole[:, 256:512]
            cos = folds[0][cls * 4 : cls * 4 + 4]
            sin = folds[1][cls * 4 : cls * 4 + 4]
            for f in range(4):
                g = ur * cos[f : f + 1] - ui * sin[f : f + 1]
                total[f] = g if total[f] is None else total[f] + g
    scale = 1.0 / (PIXELS * PIXELS)
    total = [g * scale for g in total]
    total = total + [sign * g for g in total]
    none = jnp.zeros((80, 128), F32)
    lane = lax.broadcasted_iota(jnp.int32, (80, 128), 1)
    for f in range(8):
        before = total[f - 1][:, 128:256] if f > 0 else none
        after = total[f + 1][:, 0:128] if f < 7 else none
        line = jnp.concatenate([before, total[f], after], axis=1)
        line = pltpu.roll(line, 512 - 120, 1)
        pack = jnp.where(f == me - 1, base_ref[0, :, 256:384], 0.0)
        pack = pack + jnp.where(f == me + 1, base_ref[1, :, 256:384], 0.0)
        o_ref[f, :, 0:256] = line[:, 0:256].astype(BF)
        o_ref[f, :, 256:384] = jnp.where(lane < 16, line[:, 256:384], pack).astype(BF)


def tiles_kernel(where_ref, slots_ref, count_ref, tiles_ref, table_ref, fixed_ref, o_ref):
    channel = where_ref[0]
    left = lax.broadcasted_iota(jnp.int32, (32, 128), 0)
    right = lax.broadcasted_iota(jnp.int32, (32, 128), 1)
    tile = jnp.full((32, 128), -1, jnp.int32)
    for k in range(SLOTS):
        slot = jnp.where(k < count_ref[channel, 0], slots_ref[channel, 0, k], -1)
        tile = jnp.where(left // 4 == k, slot, tile)
    pick = (tile == right // 4) & (left % 4 == right % 4)
    pick = jnp.where(pick, 1.0, 0.0).astype(BF)
    o_ref[...] = jnp.zeros_like(o_ref)
    for k in range(SLOTS):
        o_ref[256 + k * 64 : 320 + k * 64, 0:64] = tiles_ref[channel, 0, k].astype(F32).T.astype(BF)
    o_ref[256:512, 128:640] = fixed_ref[...]
    for t in range(2):
        row = dot(pick, table_ref[t]).astype(BF)
        for j in range(2):
            for chi in range(2):
                p = 2 * j + chi
                rows = slice(t * 128 + p * 32, t * 128 + p * 32 + 32)
                o_ref[rows, p * 256 : p * 256 + 256] = row[:, 0:256]
                for comp in range(2):
                    at = 256 + chi * 256 + comp * 128
                    to = 1024 + comp * 256 + j * 128
                    o_ref[rows, to : to + 128] = row[:, at : at + 128]


def gram_kernel(d_ref, e_ref, o_ref, rows, rhs, mid, edge):
    rows[0:1024, :] = d_ref[...].reshape(1024, 128).astype(F32)
    for p in range(16):
        lanes = slice(p * 128, p * 128 + 128)
        at = (p % 2) * 8 + p // 2
        rhs[0:32, lanes] = rows[pl.ds(at, 32, stride=32), :].astype(BF)
        rhs[32:64, lanes] = rows[pl.ds(16 + at, 32, stride=32), :].astype(BF)
    block = [e_ref[256:320, 384 + t * 128 : 448 + t * 128] for t in range(2)]
    turns = e_ref[256:512, 128:256].astype(F32) + e_ref[256:512, 256:384].astype(F32)
    tc, ts, ec, es = (turns[n * 64 : n * 64 + 64] for n in range(4))
    first = dot(jnp.concatenate(block, axis=0), rhs[...])
    first = first[0:64] + first[64:128]
    for p in range(16):
        g = first[:, p * 128 : p * 128 + 128]
        gr = jnp.concatenate([g[0:32], g[0:32]], axis=0)
        gi = jnp.concatenate([g[32:64], g[32:64]], axis=0)
        down = slice(p // 4 * 64, p // 4 * 64 + 64)
        at = p % 4 * 256
        mid[down, at : at + 128] = (gr * tc + gi * ts).astype(BF)
        mid[down, at + 128 : at + 256] = (gi * tc - gr * ts).astype(BF)
    spec = dot(mid[...], e_ref[0:256, 0:1024], LAST)
    spec = (spec[:, 0:128] + spec[:, 128:256]).astype(BF)
    spec = jnp.concatenate([spec[g * 64 : g * 64 + 64] for g in range(4)], axis=1)
    mixed = dot(e_ref[256:640, 0:64], spec)
    lane_slot = (lax.broadcasted_iota(jnp.int32, (64, 512), 1) % 32) // 4
    weighted = jnp.where(lane_slot == 0, mixed[0:64], 0.0)
    for k in range(1, SLOTS):
        weighted = jnp.where(lane_slot == k, mixed[k * 64 : k * 64 + 64], weighted)
    weighted = weighted.astype(BF)
    w = jnp.concatenate([weighted[:, g * 128 : g * 128 + 128] for g in range(4)], axis=0)
    spreads = dot(jnp.concatenate([w, w], axis=1), e_ref[0:256, :])
    for g in range(4):
        z = spreads[g * 64 : g * 64 + 64]
        for v in range(4):
            p = g * 4 + v
            zr = z[:, v * 256 : v * 256 + 128]
            zi = z[:, v * 256 + 128 : v * 256 + 256]
            hr = zr * tc - zi * ts
            hi = zi * tc + zr * ts
            rhs[0:32, p * 128 : p * 128 + 128] = (hr[0:32] + hr[32:64]).astype(BF)
            rhs[32:64, p * 128 : p * 128 + 128] = (hi[0:32] + hi[32:64]).astype(BF)
        for j in range(2):
            zr = z[:, 1024 + j * 128 : 1152 + j * 128]
            zi = z[:, 1280 + j * 128 : 1408 + j * 128]
            hr = zr * ec - zi * es
            hi = zi * ec + zr * es
            lanes = slice((2 * g + j) * 128, (2 * g + j) * 128 + 128)
            edge[0:32, lanes] = (hr[0:32] + hr[32:64]).astype(BF)
            edge[32:64, lanes] = (hi[0:32] + hi[32:64]).astype(BF)
    block = jnp.concatenate(block, axis=1)
    last = dot(block, rhs[...], FIRST)
    last = last[0:64] + last[64:128]
    outer = dot(block, edge[...], FIRST)
    outer = outer[0:32] + outer[64:96]
    for p in range(16):
        lanes = slice(p * 128, p * 128 + 128)
        at = (p % 2) * 8 + p // 2
        rows[pl.ds(at, 32, stride=40), :] = last[0:32, lanes]
        rows[pl.ds(16 + at, 32, stride=40), :] = last[32:64, lanes]
    for v in range(8):
        rows[pl.ds(32 + v, 32, stride=40), :] = outer[:, v * 128 : v * 128 + 128]
    o_ref[...] = rows[...].reshape(32, 40, 128).astype(BF)


def band_kernel(taps_ref, strip_ref, down_ref):
    lane = lax.broadcasted_iota(jnp.int32, (64, 256), 1)
    for k in range(FRAMES):
        wide = jnp.broadcast_to(taps_ref[k : k + 1, :], (128, 256))
        band = pltpu.roll(wide, 0, 1, stride=1, stride_axis=0)
        high = band.astype(BF)
        low = band - high.astype(F32)
        strip_ref[0, k] = high
        strip_ref[1, k] = low.astype(BF)
        high = jnp.where(lane < 80, high[0:64].astype(F32), 0.0)
        low = jnp.where(lane < 80, low[0:64], 0.0)
        row = high + pltpu.roll(high, 80, 1) + pltpu.roll(low, 160, 1)
        down_ref[k * 64 : k * 64 + 64, :] = row.astype(BF)


def synth_kernel(
    where_ref, live_ref, dual_ref, sky_ref, dirty_ref, strip_ref, o_ref, head_ref, tail_ref, across
):
    channels = sky_ref.shape[0]
    row = lax.broadcasted_iota(jnp.int32, (80, WIDE), 0) + where_ref[2] * ROWS - RADIUS
    lane = lax.broadcasted_iota(jnp.int32, (80, WIDE), 1)
    col = lane + where_ref[3] * COLS - RADIUS
    inside = (row >= 0) & (row < PIXELS) & (col >= 0) & (col < PIXELS)
    for k in range(FRAMES):
        p = dual_ref[:, k + 1].reshape(channels * ROWS, COLS)
        both = jnp.concatenate([p[:, 0:128], p[:, 128:256]], axis=0)
        a = dot(both, strip_ref[0, k]) + dot(both, strip_ref[1, k])
        a0 = a[0 : channels * ROWS]
        a1 = a[channels * ROWS :]
        out = jnp.concatenate([a0[:, 0:128], a0[:, 128:256] + a1[:, 0:128], a1[:, 128:256]], axis=1)
        for c in range(channels):
            across[c, k * ROWS : (k + 1) * ROWS, :] = out[c * ROWS : (c + 1) * ROWS].astype(BF)
    live = lax.broadcasted_iota(jnp.int32, (ROWS, COLS), 0) < live_ref[0]
    none = jnp.zeros((ROWS, 128), F32)
    edge = jnp.zeros((8, WIDE), F32)
    for c in range(channels):
        total = None
        for t in range(2):
            for k in range(FRAMES):
                term = dot(
                    strip_ref[t, k][0:64, 0:128],
                    across[c, k * ROWS : (k + 1) * ROWS, :],
                    FIRST,
                )
                total = term if total is None else total + term
        sky = sky_ref[c]
        own = sky + STEP_PRIMAL * dirty_ref[c] - STEP_PRIMAL * dual_ref[c, 0].astype(F32)
        own = jnp.where(live, own, OUTSIDE)
        own = pltpu.roll(jnp.concatenate([own, none], axis=1), 8, 1)
        sky = pltpu.roll(jnp.concatenate([sky, none], axis=1), 8, 1)
        total = total[0:80] * (-STEP_PRIMAL)
        total = total + jnp.concatenate([edge, own, edge], axis=0)
        total = jnp.where(inside, total, OUTSIDE)
        total = jnp.where(lane < COLS + 2 * RADIUS, total, 0.0)
        sky = jnp.concatenate([edge, sky, edge], axis=0)
        for at, cells in ((c, total), (channels + c, sky)):
            o_ref[at] = cells
            head_ref[at] = cells[0:16].astype(BF)
            tail_ref[at] = cells[64:80].astype(BF)


def edge_kernel(base_ref, before_ref, after_ref, o_ref):
    both = base_ref.shape[0]
    lane = lax.broadcasted_iota(jnp.int32, (80, 128), 1)
    head = jnp.zeros((80, 128), F32)
    tail = jnp.zeros((80, 128), F32)
    for c in range(both):
        o_ref[c, 0:16] = base_ref[c, 0:16] + before_ref[c].astype(F32)
        o_ref[c, 16:64] = base_ref[c, 16:64]
        o_ref[c, 64:80] = base_ref[c, 64:80] + after_ref[c].astype(F32)
        first = o_ref[c, :, 0:128]
        final = o_ref[c, :, 256:384]
        if c < both // 2:
            at = 16 + 16 * c
            head = head + pltpu.roll(jnp.where(lane < 16, first, 0.0), at, 1)
            tail = tail + pltpu.roll(jnp.where(lane < 16, final, 0.0), at, 1)
        else:
            at = 80 + 8 * (c - both // 2)
            head = head + pltpu.roll(jnp.where((lane >= 8) & (lane < 16), first, 0.0), at - 8, 1)
            tail = tail + pltpu.roll(jnp.where(lane < 8, final, 0.0), at, 1)
    o_ref[0, :, 256:384] = o_ref[0, :, 256:384] + head
    o_ref[1, :, 256:384] = o_ref[1, :, 256:384] + tail


def frames_kernel(
    bound_ref,
    where_ref,
    half_ref,
    base_ref,
    dual_ref,
    strip_ref,
    down_ref,
    image_ref,
    o_ref,
    image_buf,
    dual_buf,
    probes,
    wide,
    down,
    image_sem,
    dual_sem,
):
    channels = image_buf.shape[0]
    rows = channels * ROWS

    def dual_copy(k):
        return pltpu.make_async_copy(dual_buf.at[k], o_ref.at[:, k], dual_sem.at[k])

    def finish(k, analysis):
        bound = bound_ref[k]
        cand = [dual_ref[c, k].astype(F32) + STEP_DUAL * analysis(c) for c in range(channels)]
        square = cand[0] * cand[0]
        for c in range(1, channels):
            square = square + cand[c] * cand[c]
        factor = bound * lax.rsqrt(jnp.maximum(square, bound * bound))
        for c in range(channels):
            dual_buf[k, c] = (cand[c] * factor).astype(BF)
        dual_copy(k).start()

    wide[...] = jnp.zeros_like(wide)
    me = where_ref[3]
    last = half_ref.shape[0] - 1
    lane = lax.broadcasted_iota(jnp.int32, (80, 128), 1)
    left = half_ref[jnp.maximum(me - 1, 0), :, 256:384].astype(F32)
    left = jnp.where(me > 0, left, 0.0)
    right = half_ref[jnp.minimum(me + 1, last), :, 256:384].astype(F32)
    right = jnp.where(me < last, right, 0.0)
    for c in range(channels):
        gram = half_ref[2 * c].astype(F32) + half_ref[2 * c + 1].astype(F32)
        gram = [gram[:, 0:128], gram[:, 128:256], jnp.where(lane < 16, gram[:, 256:384], 0.0)]
        base = [base_ref[c, :, b * 128 : b * 128 + 128] for b in range(3)]
        sky = [base_ref[channels + c, :, b * 128 : b * 128 + 128] for b in range(3)]
        base[2] = jnp.where(lane < 16, base[2], 0.0)
        at = 16 + 16 * c
        base[0] = base[0] + jnp.where(lane < 16, pltpu.roll(left, 128 - at, 1), 0.0)
        base[2] = base[2] + jnp.where(lane < 16, pltpu.roll(right, 128 - at, 1), 0.0)
        at = 80 + 8 * c
        sky[0] = sky[0] + jnp.where(lane < 8, pltpu.roll(left, 128 - at, 1), 0.0)
        shown = (lane >= 8) & (lane < 16)
        sky[2] = sky[2] + jnp.where(shown, pltpu.roll(right, 136 - at, 1), 0.0)
        image = [jnp.maximum(base[b] - STEP_PRIMAL * gram[b], 0.0) for b in range(3)]
        probe = jnp.concatenate([2.0 * image[b] - sky[b] for b in range(3)], axis=1)
        image = pltpu.roll(jnp.concatenate(image, axis=1), WIDE - 8, 1)
        image_buf[c] = image[8:72, 0:256]
        probes[c] = pltpu.roll(probe, WIDE - 8, 1)[8:72, 0:256]
        high = probe.astype(BF)
        low = (probe - high.astype(F32)).astype(BF)
        wide[0:80, :] = high
        wide[80:160, :] = low
        wide[160:240, :] = high
        d = dot(down_ref[...], wide[...])
        high = d.astype(BF)
        down[0, c] = high
        down[1, c] = (d - high.astype(F32)).astype(BF)
    image_copy = pltpu.make_async_copy(image_buf, image_ref, image_sem)
    image_copy.start()
    finish(0, lambda c: probes[c])
    for k in range(1, FRAMES + 1):
        at = (k - 1) * ROWS
        a = None
        for t in range(2):
            d = jnp.concatenate([down[t, c, at : at + ROWS, :] for c in range(channels)], axis=0)
            both = jnp.concatenate([d[:, 0:256], d[:, 128:384]], axis=0)
            if t == 0:
                band = jnp.concatenate([strip_ref[0, k - 1], strip_ref[1, k - 1]], axis=0)
                term = dot(both, band, LAST)
                a = term[:, 0:128] + term[:, 128:256]
            else:
                a = a + dot(both, strip_ref[0, k - 1], LAST)
        finish(
            k,
            lambda c: jnp.concatenate(
                [a[c * ROWS : c * ROWS + ROWS], a[rows + c * ROWS : rows + c * ROWS + ROWS]], axis=1
            ),
        )
    image_copy.wait()
    for k in range(FRAMES + 1):
        dual_copy(k).wait()


VM = pl.BlockSpec(memory_space=pltpu.VMEM)
SM = pl.BlockSpec(memory_space=pltpu.SMEM)


def call(kernel, out_shape, scratch, flops, moved, *args, scalars=0):
    return pl.pallas_call(
        kernel,
        out_shape=out_shape,
        in_specs=[SM] * scalars + [VM] * (len(args) - scalars),
        out_specs=jax.tree.map(lambda _: VM, out_shape),
        scratch_shapes=scratch,
        compiler_params=pltpu.CompilerParams(vmem_limit_bytes=VMEM_LIMIT),
        cost_estimate=pl.CostEstimate(flops=flops, bytes_accessed=moved, transcendentals=0),
    )(*args)


def frames_call(thresholds, where, halves, base, dual, strip, down):
    channels = dual.shape[0]
    block = (channels, ROWS, COLS)
    return pl.pallas_call(
        frames_kernel,
        out_shape=(jax.ShapeDtypeStruct(block, F32), jax.ShapeDtypeStruct(dual.shape, BF)),
        in_specs=[SM, SM, VM, VM, VM, VM, VM],
        out_specs=(pl.BlockSpec(memory_space=pl.ANY), pl.BlockSpec(memory_space=pl.ANY)),
        scratch_shapes=[
            pltpu.VMEM(block, F32),
            pltpu.VMEM((FRAMES + 1, *block), BF),
            pltpu.VMEM(block, F32),
            pltpu.VMEM((256, WIDE), BF),
            pltpu.VMEM((2, channels, FRAMES * ROWS, WIDE), BF),
            pltpu.SemaphoreType.DMA(()),
            pltpu.SemaphoreType.DMA((FRAMES + 1,)),
        ],
        compiler_params=pltpu.CompilerParams(vmem_limit_bytes=VMEM_LIMIT),
        cost_estimate=pl.CostEstimate(flops=1 << 31, bytes_accessed=3 << 20, transcendentals=0),
    )(thresholds, where, halves, base, dual, strip, down)


def after(values, *events):
    return lax.optimization_barrier((*values, *events))[: len(values)]


def body(
    sky_estimate,
    dual_coeffs,
    dirty_image,
    filters,
    thresholds,
    facet_rows,
    tile_slots,
    tile_count,
    gram_tiles,
):
    channels, tile_rows, tile_cols = sky_estimate.shape
    place = lax.axis_index("fou")
    where = jnp.stack([place >> 1, place & 1, lax.axis_index("img"), place]).astype(jnp.int32)

    sent = pl.pallas_call(
        send_kernel,
        out_shape=jax.ShapeDtypeStruct((2 * channels, tile_rows, tile_cols), BF),
        in_specs=[pl.BlockSpec(memory_space=pltpu.HBM)],
        out_specs=pl.BlockSpec(memory_space=pltpu.HBM),
        scratch_shapes=[
            pltpu.VMEM(sky_estimate.shape, F32),
            pltpu.VMEM(sky_estimate.shape, BF),
            pltpu.SemaphoreType.DMA((channels,)),
            pltpu.SemaphoreType.DMA((channels, 2)),
        ],
        compiler_params=pltpu.CompilerParams(vmem_limit_bytes=VMEM_LIMIT),
    )(pltpu.with_memory_space_constraint(sky_estimate, pltpu.HBM))
    lines = lax.all_to_all(sent, "fou", split_axis=0, concat_axis=0, tiled=True)

    strip, down = call(
        band_kernel,
        (
            jax.ShapeDtypeStruct((2, FRAMES, 128, 256), BF),
            jax.ShapeDtypeStruct((FRAMES * ROWS, 256), BF),
        ),
        [],
        1 << 20,
        1 << 20,
        jnp.pad(filters, ((0, 0), (0, 256 - filters.shape[1]))),
    )
    (ready_where,) = after((where,), strip)
    line = wave_table()
    held = call(hold_kernel, jax.ShapeDtypeStruct(line.shape, BF), [], 1 << 10, 1 << 20, line)
    packed = call(
        forward_kernel,
        jax.ShapeDtypeStruct((PEERS_IMG, 32, 128), BF),
        [],
        1 << 29,
        1 << 20,
        ready_where,
        lines,
        held,
        scalars=1,
    )
    received = lax.all_to_all(packed, "img", split_axis=0, concat_axis=0, tiled=True)

    spread = call(
        tiles_kernel,
        jax.ShapeDtypeStruct((640, 1536), BF),
        [],
        1 << 23,
        1 << 20,
        where,
        tile_slots,
        tile_count,
        gram_tiles,
        np.stack(tile_table()),
        fixed_table(),
        scalars=3,
    )

    ends = jax.ShapeDtypeStruct((2 * channels, 16, WIDE), BF)
    extended = jax.ShapeDtypeStruct((2 * channels, tile_rows + 16, WIDE), F32)
    (late_where,) = after((where,), packed)
    base, head, tail = call(
        synth_kernel,
        (extended, ends, ends),
        [pltpu.VMEM((channels, FRAMES * ROWS, WIDE), BF)],
        1 << 31,
        4 << 20,
        late_where,
        facet_rows,
        dual_coeffs,
        sky_estimate,
        dirty_image,
        strip,
        scalars=2,
    )
    (received,) = after((received,), head)

    scratch = [
        pltpu.VMEM((1280, 128), F32),
        pltpu.VMEM((64, 2048), BF),
        pltpu.VMEM((256, 1024), BF),
        pltpu.VMEM((64, 1024), BF),
    ]
    weighted = call(
        gram_kernel,
        jax.ShapeDtypeStruct((PEERS_IMG, 40, 128), BF),
        scratch,
        1 << 29,
        1 << 20,
        received,
        spread,
    )
    returned = lax.all_to_all(weighted, "img", split_axis=0, concat_axis=0, tiled=True)

    head, tail = after((head, tail), weighted)
    steps = [(i, i + 1) for i in range(PEERS_IMG - 1)]
    from_before = lax.ppermute(tail, "img", steps)
    from_after = lax.ppermute(head, "img", [(j, i) for i, j in steps])
    base = call(
        edge_kernel,
        extended,
        [],
        1 << 20,
        4 << 20,
        base,
        from_before,
        from_after,
    )
    blocks = call(
        inverse_kernel,
        jax.ShapeDtypeStruct((8, tile_rows + 16, WIDE), BF),
        [],
        1 << 29,
        1 << 20,
        where,
        returned,
        line,
        base,
        scalars=1,
    )
    halves = lax.all_to_all(blocks, "fou", split_axis=0, concat_axis=0, tiled=True)

    return frames_call(thresholds, where, halves, base, dual_coeffs, strip, down)


def solution(mesh):
    in_specs = (
        P(None, "img", "fou"),
        P(None, None, "img", "fou"),
        P(None, "img", "fou"),
        P(),
        P(),
        P("img"),
        P(None, "img", None),
        P(None, "img"),
        P(None, "img", None, None, None),
    )
    out_specs = (P(None, "img", "fou"), P(None, None, "img", "fou"))
    return jax.shard_map(body, mesh=mesh, in_specs=in_specs, out_specs=out_specs, check_vma=False)
```

```python
import math

import jax
import jax.numpy as jnp
import numpy as np
from jax import lax
from jax.experimental import pallas as pl
from jax.experimental.pallas import tpu as pltpu
from jax.sharding import PartitionSpec as P

PIXELS = 2048
RADIUS = 8
SLOTS = 6
ROWS = 64
COLS = 256
FRAMES = 8
PEERS_IMG = 32
STEP_PRIMAL = 0.5
STEP_DUAL = 0.5
BF = jnp.bfloat16
F32 = jnp.float32
VMEM_LIMIT = 20 << 20
WIDE = 384
OUTSIDE = -1.0e30
LAST = ((1,), (1,))
FIRST = ((0,), (0,))


def two_terms_np(table):
    high = table.astype(jnp.bfloat16)
    low = (table - high.astype(np.float64)).astype(jnp.bfloat16)
    return high, low


def two_terms(table):
    high = table.astype(BF)
    return high, (table - high.astype(F32)).astype(BF)


def dot(a, b, dims=((1,), (0,))):
    return lax.dot_general(a, b, (dims, ((), ())), preferred_element_type=F32)


def angle_np(a, b, period):
    return 2.0 * np.pi * ((a[:, None] * b[None, :]) % period) / period


def line_table():
    ang = angle_np(np.arange(256), np.arange(256), 256)
    return two_terms_np(np.concatenate([np.cos(ang), np.sin(ang)], axis=1))


def block_table():
    ang = angle_np(np.arange(32), np.arange(32), 32)
    c, s = np.cos(ang), np.sin(ang)
    return two_terms_np(np.block([[c, s], [-s, c]]))


HALO = np.concatenate([np.arange(-8, 0), np.arange(64, 72)])


def turn_table():
    main = np.tile(np.arange(64), 2)
    halo = np.tile(HALO, 8)
    ang = [angle_np(np.arange(64), r, 2048) for r in (main, halo)]
    return two_terms_np(
        np.concatenate([np.cos(ang[0]), np.sin(ang[0]), np.cos(ang[1]), np.sin(ang[1])])
    )


def fixed_table():
    turns = [np.concatenate(np.split(t, 4), axis=1) for t in turn_table()]
    return np.concatenate([*block_table(), *turns], axis=1)


def tile_table():
    t = np.arange(32)
    ang = angle_np(t, np.arange(64), 32)
    c, s = np.cos(ang), np.sin(ang)
    main = np.zeros((32, 2, 2, 2, 2, 64))
    for p in range(2):
        main[:, p, 0, 0, p] = c
        main[:, p, 1, 0, p] = -s
        main[:, p, 0, 1, p] = s
        main[:, p, 1, 1, p] = c
    ang = angle_np(t, HALO, 32)
    c, s = np.cos(ang), np.sin(ang)
    halo = np.zeros((32, 2, 2, 2, 2, 2, 2, 2, 16))
    for p in range(2):
        for x in range(2):
            halo[:, p, 0, x, 0, 0, x, p] = c
            halo[:, p, 1, x, 0, 0, x, p] = -s
            halo[:, p, 0, x, 1, 0, x, p] = s
            halo[:, p, 1, x, 1, 0, x, p] = c
            halo[:, p, 0, x, 0, 1, x, p] = s
            halo[:, p, 1, x, 0, 1, x, p] = c
            halo[:, p, 0, x, 1, 1, x, p] = -c
            halo[:, p, 1, x, 1, 1, x, p] = s
    table = np.concatenate([main.reshape(128, 256), halo.reshape(128, 512)], axis=1)
    return two_terms_np(table)


def wave_table():
    freq = np.arange(2)[:, None] + 2 * np.arange(4)[None]
    pos = np.arange(4 * COLS).reshape(4, COLS)
    ang = 2.0 * np.pi * ((freq[:, :, None, None] * pos) % PIXELS) / PIXELS
    fold = np.concatenate([np.cos(ang), np.sin(ang)], axis=3).reshape(32, 2 * COLS)
    return np.concatenate([np.stack(line_table()), np.stack(two_terms_np(fold))], axis=1)


def fold_rows(line_ref, par):
    at = pl.multiple_of(256 + 16 * par, 16)
    fold = line_ref[0, pl.ds(at, 16), :].astype(F32) + line_ref[1, pl.ds(at, 16), :].astype(F32)
    return fold[:, 0:256], fold[:, 256:512]


def hold_kernel(table_ref, o_ref):
    o_ref[...] = table_ref[...]


def send_kernel(sky_ref, o_ref, taken, rounded, in_sem, out_sem):
    channels = taken.shape[0]

    def fetch(c):
        return pltpu.make_async_copy(sky_ref.at[c], taken.at[c], in_sem.at[c])

    def place(c, h):
        return pltpu.make_async_copy(rounded.at[c], o_ref.at[2 * c + h], out_sem.at[c, h])

    for c in range(channels):
        fetch(c).start()
    for c in range(channels):
        fetch(c).wait()
        rounded[c] = taken[c].astype(BF)
        for h in range(2):
            place(c, h).start()
    for c in range(channels):
        for h in range(2):
            place(c, h).wait()


def forward_kernel(par_ref, x_ref, line_ref, o_ref):
    par = par_ref[1]
    folds = fold_rows(line_ref, par)
    sign = (1 - 2 * par).astype(F32)
    xe = [x_ref[f].astype(F32) + sign * x_ref[f + 4].astype(F32) for f in range(4)]
    rows = [[], []]
    for cls in range(4):
        cos = folds[0][cls * 4 : cls * 4 + 4]
        sin = folds[1][cls * 4 : cls * 4 + 4]
        yr = xe[0] * cos[0:1]
        yi = xe[0] * sin[0:1]
        for f in range(1, 4):
            yr = yr + xe[f] * cos[f : f + 1]
            yi = yi + xe[f] * sin[f : f + 1]
        rows[0].append(jnp.concatenate([yr, -yi], axis=1).astype(BF))
        rows[1].append(jnp.concatenate([-yi, -yr], axis=1).astype(BF))
    for part in range(2):
        r = jnp.concatenate(rows[part], axis=0)
        out = dot(line_ref[0, 0:256], r, LAST) + dot(line_ref[1, 0:256], r, LAST)
        both = [out[:, chi * 128 : chi * 128 + 128].reshape(32, 8, 128) for chi in range(2)]
        both = jnp.concatenate(both, axis=1)
        o_ref[:, part * 16 : (part + 1) * 16, :] = both.astype(BF)


def inverse_kernel(par_ref, t_ref, line_ref, base_ref, o_ref):
    par = par_ref[1]
    folds = fold_rows(line_ref, par)
    me = par_ref[3]
    sign = (1 - 2 * par).astype(F32)
    re = t_ref[:, 0:16, :].astype(F32)
    im = t_ref[:, 16:32, :].astype(F32)
    edge = t_ref[:, 32:40, :].astype(F32)
    data = [re[:, 0:8], im[:, 0:8], re[:, 8:16], im[:, 8:16], edge]
    data = jnp.concatenate([d.reshape(256, 128).astype(BF) for d in data], axis=1)
    wave = dot(data, line_ref[0, 0:256], FIRST) + dot(data, line_ref[1, 0:256], FIRST)

    def joined(a, b):
        return jnp.concatenate([a[:, 0:256] - b[:, 256:512], a[:, 256:512] + b[:, 0:256]], axis=1)

    h = joined(wave[512:576], wave[576:640])
    total = [None] * 4
    for chi in range(2):
        u = joined(wave[chi * 256 : chi * 256 + 128], wave[chi * 256 + 128 : chi * 256 + 256])
        for clo in range(2):
            cls = 2 * chi + clo
            e = h[cls * 16 : cls * 16 + 16]
            whole = jnp.concatenate([e[0:8], u[clo * 64 : clo * 64 + 64], e[8:16]], axis=0)
            ur = whole[:, 0:256]
            ui = whole[:, 256:512]
            cos = folds[0][cls * 4 : cls * 4 + 4]
            sin = folds[1][cls * 4 : cls * 4 + 4]
            for f in range(4):
                g = ur * cos[f : f + 1] - ui * sin[f : f + 1]
                total[f] = g if total[f] is None else total[f] + g
    scale = 1.0 / (PIXELS * PIXELS)
    total = [g * scale for g in total]
    total = total + [sign * g for g in total]
    none = jnp.zeros((80, 128), F32)
    lane = lax.broadcasted_iota(jnp.int32, (80, 128), 1)
    for f in range(8):
        before = total[f - 1][:, 128:256] if f > 0 else none
        after = total[f + 1][:, 0:128] if f < 7 else none
        line = jnp.concatenate([before, total[f], after], axis=1)
        line = pltpu.roll(line, 512 - 120, 1)
        pack = jnp.where(f == me - 1, base_ref[0, :, 256:384], 0.0)
        pack = pack + jnp.where(f == me + 1, base_ref[1, :, 256:384], 0.0)
        o_ref[f, :, 0:256] = line[:, 0:256].astype(BF)
        o_ref[f, :, 256:384] = jnp.where(lane < 16, line[:, 256:384], pack).astype(BF)


def tiles_kernel(where_ref, slots_ref, count_ref, tiles_ref, table_ref, fixed_ref, o_ref):
    channel = where_ref[0]
    left = lax.broadcasted_iota(jnp.int32, (32, 128), 0)
    right = lax.broadcasted_iota(jnp.int32, (32, 128), 1)
    tile = jnp.full((32, 128), -1, jnp.int32)
    for k in range(SLOTS):
        slot = jnp.where(k < count_ref[channel, 0], slots_ref[channel, 0, k], -1)
        tile = jnp.where(left // 4 == k, slot, tile)
    pick = (tile == right // 4) & (left % 4 == right % 4)
    pick = jnp.where(pick, 1.0, 0.0).astype(BF)
    o_ref[...] = jnp.zeros_like(o_ref)
    for k in range(0, SLOTS, 2):
        pair = [tiles_ref[channel, 0, k + n].astype(F32).T for n in range(2)]
        o_ref[256:320, k * 64 : k * 64 + 128] = jnp.concatenate(pair, axis=1).astype(BF)
    o_ref[256:320, 384:1536] = fixed_ref[...]
    for t in range(2):
        row = dot(pick, table_ref[t]).astype(BF)
        for j in range(2):
            for chi in range(2):
                p = 2 * j + chi
                rows = slice(t * 128 + p * 32, t * 128 + p * 32 + 32)
                o_ref[rows, p * 256 : p * 256 + 256] = row[:, 0:256]
                for comp in range(2):
                    at = 256 + chi * 256 + comp * 128
                    to = 1024 + comp * 256 + j * 128
                    o_ref[rows, to : to + 128] = row[:, at : at + 128]


def gram_kernel(d_ref, e_ref, o_ref, rows, rhs, mid, edge, out, sem):
    rows[0:1024, :] = d_ref[...].reshape(1024, 128).astype(F32)
    for p in range(16):
        lanes = slice(p * 128, p * 128 + 128)
        at = (p % 2) * 8 + p // 2
        rhs[0:32, lanes] = rows[pl.ds(at, 32, stride=32), :].astype(BF)
        rhs[32:64, lanes] = rows[pl.ds(16 + at, 32, stride=32), :].astype(BF)
    fixed = e_ref[256:320, :]
    block = [fixed[:, 384:448], fixed[:, 448:512]]
    turns = fixed[:, 512:1024].astype(F32) + fixed[:, 1024:1536].astype(F32)
    tc, ts, ec, es = (turns[:, n * 128 : n * 128 + 128] for n in range(4))
    first = dot(jnp.concatenate(block, axis=0), rhs[...])
    first = first[0:64] + first[64:128]
    for p in range(16):
        g = first[:, p * 128 : p * 128 + 128]
        gr = jnp.concatenate([g[0:32], g[0:32]], axis=0)
        gi = jnp.concatenate([g[32:64], g[32:64]], axis=0)
        down = slice(p // 4 * 64, p // 4 * 64 + 64)
        at = p % 4 * 256
        mid[down, at : at + 128] = (gr * tc + gi * ts).astype(BF)
        mid[down, at + 128 : at + 256] = (gi * tc - gr * ts).astype(BF)
    spec = dot(mid[...], e_ref[0:256, 0:1024], LAST)
    spec = (spec[:, 0:128] + spec[:, 128:256]).astype(BF)
    spec = jnp.concatenate([spec[g * 64 : g * 64 + 64] for g in range(4)], axis=1)
    tiles = [fixed[:, k * 64 : k * 64 + 64] for k in range(SLOTS)]
    mixed = dot(jnp.concatenate(tiles, axis=0), spec)
    lane_slot = (lax.broadcasted_iota(jnp.int32, (64, 512), 1) % 32) // 4
    weighted = jnp.where(lane_slot == 0, mixed[0:64], 0.0)
    for k in range(1, SLOTS):
        weighted = jnp.where(lane_slot == k, mixed[k * 64 : k * 64 + 64], weighted)
    weighted = weighted.astype(BF)
    w = jnp.concatenate([weighted[:, g * 128 : g * 128 + 128] for g in range(4)], axis=0)
    spreads = dot(jnp.concatenate([w, w], axis=1), e_ref[0:256, :])
    for g in range(4):
        z = spreads[g * 64 : g * 64 + 64]
        for v in range(4):
            p = g * 4 + v
            zr = z[:, v * 256 : v * 256 + 128]
            zi = z[:, v * 256 + 128 : v * 256 + 256]
            hr = zr * tc - zi * ts
            hi = zi * tc + zr * ts
            rhs[0:32, p * 128 : p * 128 + 128] = (hr[0:32] + hr[32:64]).astype(BF)
            rhs[32:64, p * 128 : p * 128 + 128] = (hi[0:32] + hi[32:64]).astype(BF)
        for j in range(2):
            zr = z[:, 1024 + j * 128 : 1152 + j * 128]
            zi = z[:, 1280 + j * 128 : 1408 + j * 128]
            hr = zr * ec - zi * es
            hi = zi * ec + zr * es
            lanes = slice((2 * g + j) * 128, (2 * g + j) * 128 + 128)
            edge[0:32, lanes] = (hr[0:32] + hr[32:64]).astype(BF)
            edge[32:64, lanes] = (hi[0:32] + hi[32:64]).astype(BF)
    block = jnp.concatenate(block, axis=1)
    last = dot(block, rhs[...], FIRST)
    last = last[0:64] + last[64:128]
    outer = dot(block, edge[...], FIRST)
    outer = outer[0:32] + outer[64:96]
    for p in range(16):
        lanes = slice(p * 128, p * 128 + 128)
        at = (p % 2) * 8 + p // 2
        rows[pl.ds(at, 32, stride=40), :] = last[0:32, lanes]
        rows[pl.ds(16 + at, 32, stride=40), :] = last[32:64, lanes]
    for v in range(8):
        rows[pl.ds(32 + v, 32, stride=40), :] = outer[:, v * 128 : v * 128 + 128]
    leave = []
    for n in range(2):
        half = rows[n * 640 : n * 640 + 640, :]
        out[n] = half.reshape(16, 40, 128).astype(BF)
        to = o_ref.at[pl.ds(n * 16, 16)]
        leave.append(pltpu.make_async_copy(out.at[n], to, sem.at[n]))
        leave[n].start()
    for n in range(2):
        leave[n].wait()


def bands_kernel(taps_ref, o_ref):
    lane = lax.broadcasted_iota(jnp.int32, (64, 256), 1)
    for k in range(FRAMES):
        wide = jnp.broadcast_to(taps_ref[k : k + 1, :], (128, 256))
        band = pltpu.roll(wide, 0, 1, stride=1, stride_axis=0)
        high = band.astype(BF)
        low = band - high.astype(F32)
        o_ref[k * 128 : k * 128 + 128, :] = high
        o_ref[1024 + k * 128 : 1152 + k * 128, :] = low.astype(BF)
        low = jnp.where(lane < 80, low[0:64], 0.0)
        high = jnp.where(lane < 80, high[0:64].astype(F32), 0.0)
        row = high + pltpu.roll(high, 80, 1) + pltpu.roll(low, 160, 1)
        o_ref[2048 + k * 64 : 2112 + k * 64, :] = row.astype(BF)


def synth_kernel(
    where_ref,
    live_ref,
    dual_hbm,
    sky_hbm,
    dirty_hbm,
    bands_ref,
    o_ref,
    head_ref,
    tail_ref,
    dual_ref,
    sky_ref,
    dirty_ref,
    across,
    dual_sem,
    sky_sem,
    dirty_sem,
):
    channels = sky_ref.shape[0]
    copies = [
        pltpu.make_async_copy(dual_hbm.at[:, k], dual_ref.at[k], dual_sem.at[k])
        for k in range(FRAMES + 1)
    ]
    for k in range(1, FRAMES + 1):
        copies[k].start()
    copies[0].start()
    sky_copy = pltpu.make_async_copy(sky_hbm, sky_ref, sky_sem)
    sky_copy.start()
    dirty_copy = pltpu.make_async_copy(dirty_hbm, dirty_ref, dirty_sem)
    dirty_copy.start()
    row = lax.broadcasted_iota(jnp.int32, (80, WIDE), 0) + where_ref[2] * ROWS - RADIUS
    lane = lax.broadcasted_iota(jnp.int32, (80, WIDE), 1)
    col = lane + where_ref[3] * COLS - RADIUS
    inside = (row >= 0) & (row < PIXELS) & (col >= 0) & (col < PIXELS)
    for k in range(FRAMES):
        copies[k + 1].wait()
        p = dual_ref[k + 1].reshape(channels * ROWS, COLS)
        both = jnp.concatenate([p[:, 0:128], p[:, 128:256]], axis=0)
        both = jnp.concatenate([both, both], axis=1)
        at = k * 128
        band = jnp.concatenate(
            [bands_ref[at : at + 128, :], bands_ref[1024 + at : 1152 + at, :]], axis=0
        )
        a = dot(both, band)
        a0 = a[0 : channels * ROWS]
        a1 = a[channels * ROWS :]
        out = jnp.concatenate([a0[:, 0:128], a0[:, 128:256] + a1[:, 0:128], a1[:, 128:256]], axis=1)
        for c in range(channels):
            across[c, k * ROWS : (k + 1) * ROWS, :] = out[c * ROWS : (c + 1) * ROWS].astype(BF)
    copies[0].wait()
    sky_copy.wait()
    dirty_copy.wait()
    live = lax.broadcasted_iota(jnp.int32, (ROWS, COLS), 0) < live_ref[0]
    none = jnp.zeros((ROWS, 128), F32)
    edge = jnp.zeros((8, WIDE), F32)
    for c in range(channels):
        total = dot(bands_ref[2048:2560, :], across[c], FIRST)
        total = total[0:80] + total[160:240]
        sky = sky_ref[c]
        own = sky + STEP_PRIMAL * dirty_ref[c] - STEP_PRIMAL * dual_ref[0, c].astype(F32)
        own = jnp.where(live, own, OUTSIDE)
        own = pltpu.roll(jnp.concatenate([own, none], axis=1), 8, 1)
        sky = pltpu.roll(jnp.concatenate([sky, none], axis=1), 8, 1)
        total = total * (-STEP_PRIMAL)
        total = total + jnp.concatenate([edge, own, edge], axis=0)
        total = jnp.where(inside, total, OUTSIDE)
        total = jnp.where(lane < COLS + 2 * RADIUS, total, 0.0)
        sky = jnp.concatenate([edge, sky, edge], axis=0)
        for at, cells in ((c, total), (channels + c, sky)):
            o_ref[at] = cells
            head_ref[at] = cells[0:16].astype(BF)
            tail_ref[at] = cells[64:80].astype(BF)


def edge_kernel(base_ref, before_ref, after_ref, o_ref):
    both = base_ref.shape[0]
    lane = lax.broadcasted_iota(jnp.int32, (80, 128), 1)
    head = jnp.zeros((80, 128), F32)
    tail = jnp.zeros((80, 128), F32)
    for c in range(both):
        o_ref[c, 0:16] = base_ref[c, 0:16] + before_ref[c].astype(F32)
        o_ref[c, 16:64] = base_ref[c, 16:64]
        o_ref[c, 64:80] = base_ref[c, 64:80] + after_ref[c].astype(F32)
        first = o_ref[c, :, 0:128]
        final = o_ref[c, :, 256:384]
        if c < both // 2:
            at = 16 + 16 * c
            head = head + pltpu.roll(jnp.where(lane < 16, first, 0.0), at, 1)
            tail = tail + pltpu.roll(jnp.where(lane < 16, final, 0.0), at, 1)
        else:
            at = 80 + 8 * (c - both // 2)
            head = head + pltpu.roll(jnp.where((lane >= 8) & (lane < 16), first, 0.0), at - 8, 1)
            tail = tail + pltpu.roll(jnp.where(lane < 8, final, 0.0), at, 1)
    o_ref[0, :, 256:384] = o_ref[0, :, 256:384] + head
    o_ref[1, :, 256:384] = o_ref[1, :, 256:384] + tail


def frames_kernel(
    bound_ref,
    where_ref,
    half_ref,
    base_ref,
    dual_ref,
    bands_ref,
    image_ref,
    o_ref,
    image_buf,
    dual_buf,
    probes,
    wide,
    down,
    image_sem,
    dual_sem,
):
    channels = image_buf.shape[0]
    rows = channels * ROWS

    def dual_copy(k):
        return pltpu.make_async_copy(dual_buf.at[k], o_ref.at[:, k], dual_sem.at[k])

    def finish(k, analysis):
        bound = bound_ref[k]
        cand = [dual_ref[c, k].astype(F32) + STEP_DUAL * analysis(c) for c in range(channels)]
        square = cand[0] * cand[0]
        for c in range(1, channels):
            square = square + cand[c] * cand[c]
        factor = bound * lax.rsqrt(jnp.maximum(square, bound * bound))
        for c in range(channels):
            dual_buf[k, c] = (cand[c] * factor).astype(BF)
        dual_copy(k).start()

    wide[...] = jnp.zeros_like(wide)
    me = where_ref[3]
    last = half_ref.shape[0] - 1
    lane = lax.broadcasted_iota(jnp.int32, (80, 128), 1)
    left = half_ref[jnp.maximum(me - 1, 0), :, 256:384].astype(F32)
    left = jnp.where(me > 0, left, 0.0)
    right = half_ref[jnp.minimum(me + 1, last), :, 256:384].astype(F32)
    right = jnp.where(me < last, right, 0.0)
    for c in range(channels):
        gram = half_ref[2 * c].astype(F32) + half_ref[2 * c + 1].astype(F32)
        gram = [gram[:, 0:128], gram[:, 128:256], jnp.where(lane < 16, gram[:, 256:384], 0.0)]
        base = [base_ref[c, :, b * 128 : b * 128 + 128] for b in range(3)]
        sky = [base_ref[channels + c, :, b * 128 : b * 128 + 128] for b in range(3)]
        base[2] = jnp.where(lane < 16, base[2], 0.0)
        at = 16 + 16 * c
        base[0] = base[0] + jnp.where(lane < 16, pltpu.roll(left, 128 - at, 1), 0.0)
        base[2] = base[2] + jnp.where(lane < 16, pltpu.roll(right, 128 - at, 1), 0.0)
        at = 80 + 8 * c
        sky[0] = sky[0] + jnp.where(lane < 8, pltpu.roll(left, 128 - at, 1), 0.0)
        shown = (lane >= 8) & (lane < 16)
        sky[2] = sky[2] + jnp.where(shown, pltpu.roll(right, 136 - at, 1), 0.0)
        image = [jnp.maximum(base[b] - STEP_PRIMAL * gram[b], 0.0) for b in range(3)]
        probe = jnp.concatenate([2.0 * image[b] - sky[b] for b in range(3)], axis=1)
        image = pltpu.roll(jnp.concatenate(image, axis=1), WIDE - 8, 1)
        image_buf[c] = image[8:72, 0:256]
        probes[c] = pltpu.roll(probe, WIDE - 8, 1)[8:72, 0:256]
        high = probe.astype(BF)
        low = (probe - high.astype(F32)).astype(BF)
        wide[0:80, :] = high
        wide[80:160, :] = low
        wide[160:240, :] = high
        d = dot(bands_ref[2048:2560, :], wide[...])
        high = d.astype(BF)
        down[0, c] = high
        down[1, c] = (d - high.astype(F32)).astype(BF)
    image_copy = pltpu.make_async_copy(image_buf, image_ref, image_sem)
    image_copy.start()
    finish(0, lambda c: probes[c])
    for k in range(1, FRAMES + 1):
        at = (k - 1) * ROWS
        a = None
        for t in range(2):
            d = jnp.concatenate([down[t, c, at : at + ROWS, :] for c in range(channels)], axis=0)
            both = jnp.concatenate([d[:, 0:256], d[:, 128:384]], axis=0)
            high = bands_ref[(k - 1) * 128 : k * 128, :]
            if t == 0:
                band = jnp.concatenate([high, bands_ref[896 + k * 128 : 1024 + k * 128, :]], axis=0)
                term = dot(both, band, LAST)
                a = term[:, 0:128] + term[:, 128:256]
            else:
                a = a + dot(both, high, LAST)
        finish(
            k,
            lambda c: jnp.concatenate(
                [a[c * ROWS : c * ROWS + ROWS], a[rows + c * ROWS : rows + c * ROWS + ROWS]], axis=1
            ),
        )
    image_copy.wait()
    for k in range(FRAMES + 1):
        dual_copy(k).wait()


VM = pl.BlockSpec(memory_space=pltpu.VMEM)
SM = pl.BlockSpec(memory_space=pltpu.SMEM)
HB = pl.BlockSpec(memory_space=pltpu.HBM)


def call(kernel, out_shape, scratch, flops, moved, *args, scalars=0, result=VM):
    return pl.pallas_call(
        kernel,
        out_shape=out_shape,
        in_specs=[SM] * scalars + [VM] * (len(args) - scalars),
        out_specs=jax.tree.map(lambda _: result, out_shape),
        scratch_shapes=scratch,
        compiler_params=pltpu.CompilerParams(vmem_limit_bytes=VMEM_LIMIT),
        cost_estimate=pl.CostEstimate(flops=flops, bytes_accessed=moved, transcendentals=0),
    )(*args)


def frames_call(thresholds, where, halves, base, dual, bands):
    channels = dual.shape[0]
    block = (channels, ROWS, COLS)
    return pl.pallas_call(
        frames_kernel,
        out_shape=(jax.ShapeDtypeStruct(block, F32), jax.ShapeDtypeStruct(dual.shape, BF)),
        in_specs=[SM, SM, VM, VM, VM, VM],
        out_specs=(pl.BlockSpec(memory_space=pl.ANY), pl.BlockSpec(memory_space=pl.ANY)),
        scratch_shapes=[
            pltpu.VMEM(block, F32),
            pltpu.VMEM((FRAMES + 1, *block), BF),
            pltpu.VMEM(block, F32),
            pltpu.VMEM((256, WIDE), BF),
            pltpu.VMEM((2, channels, FRAMES * ROWS, WIDE), BF),
            pltpu.SemaphoreType.DMA(()),
            pltpu.SemaphoreType.DMA((FRAMES + 1,)),
        ],
        compiler_params=pltpu.CompilerParams(vmem_limit_bytes=VMEM_LIMIT),
        cost_estimate=pl.CostEstimate(flops=1 << 31, bytes_accessed=3 << 20, transcendentals=0),
    )(thresholds, where, halves, base, dual, bands)


def after(values, *events):
    return lax.optimization_barrier((*values, *events))[: len(values)]


def body(
    sky_estimate,
    dual_coeffs,
    dirty_image,
    filters,
    thresholds,
    facet_rows,
    tile_slots,
    tile_count,
    gram_tiles,
):
    channels, tile_rows, tile_cols = sky_estimate.shape
    place = lax.axis_index("fou")
    where = jnp.stack([place >> 1, place & 1, lax.axis_index("img"), place]).astype(jnp.int32)

    sent = pl.pallas_call(
        send_kernel,
        out_shape=jax.ShapeDtypeStruct((2 * channels, tile_rows, tile_cols), BF),
        in_specs=[pl.BlockSpec(memory_space=pltpu.HBM)],
        out_specs=pl.BlockSpec(memory_space=pltpu.HBM),
        scratch_shapes=[
            pltpu.VMEM(sky_estimate.shape, F32),
            pltpu.VMEM(sky_estimate.shape, BF),
            pltpu.SemaphoreType.DMA((channels,)),
            pltpu.SemaphoreType.DMA((channels, 2)),
        ],
        compiler_params=pltpu.CompilerParams(vmem_limit_bytes=VMEM_LIMIT),
    )(pltpu.with_memory_space_constraint(sky_estimate, pltpu.HBM))
    lines = lax.all_to_all(sent, "fou", split_axis=0, concat_axis=0, tiled=True)

    taps = jnp.pad(filters, ((0, 0), (0, 256 - filters.shape[1])))
    bands = call(
        bands_kernel, jax.ShapeDtypeStruct((2560, 256), BF), [], 1 << 20, 1 << 20, taps
    )
    (ready_where,) = after((where,), bands)
    line = wave_table()
    held = call(hold_kernel, jax.ShapeDtypeStruct(line.shape, BF), [], 1 << 10, 1 << 20, line)
    packed = call(
        forward_kernel,
        jax.ShapeDtypeStruct((PEERS_IMG, 32, 128), BF),
        [],
        1 << 29,
        1 << 20,
        ready_where,
        lines,
        held,
        scalars=1,
    )
    received = lax.all_to_all(packed, "img", split_axis=0, concat_axis=0, tiled=True)

    spread = call(
        tiles_kernel,
        jax.ShapeDtypeStruct((320, 1536), BF),
        [],
        1 << 23,
        1 << 20,
        where,
        tile_slots,
        tile_count,
        gram_tiles,
        np.stack(tile_table()),
        fixed_table(),
        scalars=3,
    )

    ends = jax.ShapeDtypeStruct((2 * channels, 16, WIDE), BF)
    extended = jax.ShapeDtypeStruct((2 * channels, tile_rows + 16, WIDE), F32)
    (late_where,) = after((where,), packed)
    base, head, tail = pl.pallas_call(
        synth_kernel,
        out_shape=(extended, ends, ends),
        in_specs=[SM, SM, HB, HB, HB, VM],
        out_specs=(VM, VM, VM),
        scratch_shapes=[
            pltpu.VMEM((FRAMES + 1, channels, tile_rows, tile_cols), BF),
            pltpu.VMEM(sky_estimate.shape, F32),
            pltpu.VMEM(sky_estimate.shape, F32),
            pltpu.VMEM((channels, FRAMES * ROWS, WIDE), BF),
            pltpu.SemaphoreType.DMA((FRAMES + 1,)),
            pltpu.SemaphoreType.DMA(()),
            pltpu.SemaphoreType.DMA(()),
        ],
        compiler_params=pltpu.CompilerParams(vmem_limit_bytes=VMEM_LIMIT),
        cost_estimate=pl.CostEstimate(flops=1 << 31, bytes_accessed=4 << 20, transcendentals=0),
    )(
        late_where,
        facet_rows,
        *(pltpu.with_memory_space_constraint(a, pltpu.HBM) for a in (dual_coeffs, sky_estimate, dirty_image)),
        bands,
    )
    (received,) = after((received,), head)

    scratch = [
        pltpu.VMEM((1280, 128), F32),
        pltpu.VMEM((64, 2048), BF),
        pltpu.VMEM((256, 1024), BF),
        pltpu.VMEM((64, 1024), BF),
        pltpu.VMEM((2, 16, 40, 128), BF),
        pltpu.SemaphoreType.DMA((2,)),
    ]
    weighted = call(
        gram_kernel,
        jax.ShapeDtypeStruct((PEERS_IMG, 40, 128), BF),
        scratch,
        1 << 29,
        1 << 20,
        received,
        spread,
        result=HB,
    )
    returned = lax.all_to_all(weighted, "img", split_axis=0, concat_axis=0, tiled=True)

    head, tail = after((head, tail), weighted)
    steps = [(i, i + 1) for i in range(PEERS_IMG - 1)]
    from_before = lax.ppermute(tail, "img", steps)
    from_after = lax.ppermute(head, "img", [(j, i) for i, j in steps])
    base = call(
        edge_kernel,
        extended,
        [],
        1 << 20,
        4 << 20,
        base,
        from_before,
        from_after,
    )
    blocks = call(
        inverse_kernel,
        jax.ShapeDtypeStruct((8, tile_rows + 16, WIDE), BF),
        [],
        1 << 29,
        1 << 20,
        where,
        returned,
        line,
        base,
        scalars=1,
    )
    halves = lax.all_to_all(blocks, "fou", split_axis=0, concat_axis=0, tiled=True)

    return frames_call(thresholds, where, halves, base, dual_coeffs, bands)


def solution(mesh):
    in_specs = (
        P(None, "img", "fou"),
        P(None, None, "img", "fou"),
        P(None, "img", "fou"),
        P(),
        P(),
        P("img"),
        P(None, "img", None),
        P(None, "img"),
        P(None, "img", None, None, None),
    )
    out_specs = (P(None, "img", "fou"), P(None, None, "img", "fou"))
    return jax.shard_map(body, mesh=mesh, in_specs=in_specs, out_specs=out_specs, check_vma=False)
```

```python
import math

import jax
import jax.numpy as jnp
import numpy as np
from jax import lax
from jax.experimental import pallas as pl
from jax.experimental.pallas import tpu as pltpu
from jax.sharding import PartitionSpec as P

PIXELS = 2048
RADIUS = 8
SLOTS = 6
ROWS = 64
COLS = 256
FRAMES = 8
PEERS_IMG = 32
STEP_PRIMAL = 0.5
STEP_DUAL = 0.5
BF = jnp.bfloat16
F32 = jnp.float32
VMEM_LIMIT = 20 << 20
WIDE = 384
OUTSIDE = -1.0e30
LAST = ((1,), (1,))
FIRST = ((0,), (0,))


def two_terms_np(table):
    high = table.astype(jnp.bfloat16)
    low = (table - high.astype(np.float64)).astype(jnp.bfloat16)
    return high, low


def two_terms(table):
    high = table.astype(BF)
    return high, (table - high.astype(F32)).astype(BF)


def dot(a, b, dims=((1,), (0,))):
    return lax.dot_general(a, b, (dims, ((), ())), preferred_element_type=F32)


def angle_np(a, b, period):
    return 2.0 * np.pi * ((a[:, None] * b[None, :]) % period) / period


def line_table():
    ang = angle_np(np.arange(256), np.arange(256), 256)
    return two_terms_np(np.concatenate([np.cos(ang), np.sin(ang)], axis=1))


def block_table():
    ang = angle_np(np.arange(32), np.arange(32), 32)
    c, s = np.cos(ang), np.sin(ang)
    return two_terms_np(np.block([[c, s], [-s, c]]))


HALO = np.concatenate([np.arange(-8, 0), np.arange(64, 72)])


def turn_table():
    main = np.tile(np.arange(64), 2)
    halo = np.tile(HALO, 8)
    ang = [angle_np(np.arange(64), r, 2048) for r in (main, halo)]
    return two_terms_np(
        np.concatenate([np.cos(ang[0]), np.sin(ang[0]), np.cos(ang[1]), np.sin(ang[1])])
    )


def fixed_table():
    turns = [np.concatenate(np.split(t, 4), axis=1) for t in turn_table()]
    return np.concatenate([*block_table(), *turns], axis=1)


def sampled_table():
    fixed = fixed_table()
    rest = np.zeros((64, 768), fixed.dtype)
    rest[:, 0:384] = fixed[:, 768:1152]
    return np.concatenate([*tile_table(), fixed[:, 0:768], rest], axis=0)


def tile_table():
    t = np.arange(32)
    ang = angle_np(t, np.arange(64), 32)
    c, s = np.cos(ang), np.sin(ang)
    main = np.zeros((32, 2, 2, 2, 2, 64))
    for p in range(2):
        main[:, p, 0, 0, p] = c
        main[:, p, 1, 0, p] = -s
        main[:, p, 0, 1, p] = s
        main[:, p, 1, 1, p] = c
    ang = angle_np(t, HALO, 32)
    c, s = np.cos(ang), np.sin(ang)
    halo = np.zeros((32, 2, 2, 2, 2, 2, 2, 2, 16))
    for p in range(2):
        for x in range(2):
            halo[:, p, 0, x, 0, 0, x, p] = c
            halo[:, p, 1, x, 0, 0, x, p] = -s
            halo[:, p, 0, x, 1, 0, x, p] = s
            halo[:, p, 1, x, 1, 0, x, p] = c
            halo[:, p, 0, x, 0, 1, x, p] = s
            halo[:, p, 1, x, 0, 1, x, p] = c
            halo[:, p, 0, x, 1, 1, x, p] = -c
            halo[:, p, 1, x, 1, 1, x, p] = s
    table = np.concatenate([main.reshape(128, 256), halo.reshape(128, 512)], axis=1)
    return two_terms_np(table)


def wave_table():
    freq = np.arange(2)[:, None] + 2 * np.arange(4)[None]
    pos = np.arange(4 * COLS).reshape(4, COLS)
    ang = 2.0 * np.pi * ((freq[:, :, None, None] * pos) % PIXELS) / PIXELS
    fold = np.concatenate([np.cos(ang), np.sin(ang)], axis=3).reshape(32, 2 * COLS)
    return np.concatenate([np.stack(line_table()), np.stack(two_terms_np(fold))], axis=1)


def fold_rows(line_ref, par):
    at = pl.multiple_of(256 + 16 * par, 16)
    fold = line_ref[0, pl.ds(at, 16), :].astype(F32) + line_ref[1, pl.ds(at, 16), :].astype(F32)
    return fold[:, 0:256], fold[:, 256:512]


def hold_kernel(table_ref, o_ref):
    o_ref[...] = table_ref[...]


def send_kernel(sky_ref, o_ref, taken, rounded, in_sem, out_sem):
    channels = taken.shape[0]

    def fetch(c):
        return pltpu.make_async_copy(sky_ref.at[c], taken.at[c], in_sem.at[c])

    def place(c, h):
        return pltpu.make_async_copy(rounded.at[c], o_ref.at[2 * c + h], out_sem.at[c, h])

    for c in range(channels):
        fetch(c).start()
    for c in range(channels):
        fetch(c).wait()
        rounded[c] = taken[c].astype(BF)
        for h in range(2):
            place(c, h).start()
    for c in range(channels):
        for h in range(2):
            place(c, h).wait()


def forward_kernel(par_ref, x_ref, line_ref, o_ref):
    par = par_ref[1]
    folds = fold_rows(line_ref, par)
    sign = (1 - 2 * par).astype(F32)
    xe = [x_ref[f].astype(F32) + sign * x_ref[f + 4].astype(F32) for f in range(4)]
    rows = [[], []]
    for cls in range(4):
        cos = folds[0][cls * 4 : cls * 4 + 4]
        sin = folds[1][cls * 4 : cls * 4 + 4]
        yr = xe[0] * cos[0:1]
        yi = xe[0] * sin[0:1]
        for f in range(1, 4):
            yr = yr + xe[f] * cos[f : f + 1]
            yi = yi + xe[f] * sin[f : f + 1]
        rows[0].append(jnp.concatenate([yr, -yi], axis=1).astype(BF))
        rows[1].append(jnp.concatenate([-yi, -yr], axis=1).astype(BF))
    for part in range(2):
        r = jnp.concatenate(rows[part], axis=0)
        out = dot(line_ref[0, 0:256], r, LAST) + dot(line_ref[1, 0:256], r, LAST)
        both = [out[:, chi * 128 : chi * 128 + 128].reshape(32, 8, 128) for chi in range(2)]
        both = jnp.concatenate(both, axis=1)
        o_ref[:, part * 16 : (part + 1) * 16, :] = both.astype(BF)


def inverse_kernel(par_ref, t_ref, line_ref, base_ref, o_ref):
    par = par_ref[1]
    folds = fold_rows(line_ref, par)
    me = par_ref[3]
    sign = (1 - 2 * par).astype(F32)
    re = t_ref[:, 0:16, :].astype(F32)
    im = t_ref[:, 16:32, :].astype(F32)
    edge = t_ref[:, 32:40, :].astype(F32)
    data = [re[:, 0:8], im[:, 0:8], re[:, 8:16], im[:, 8:16], edge]
    data = jnp.concatenate([d.reshape(256, 128).astype(BF) for d in data], axis=1)
    wave = dot(data, line_ref[0, 0:256], FIRST) + dot(data, line_ref[1, 0:256], FIRST)

    def joined(a, b):
        return jnp.concatenate([a[:, 0:256] - b[:, 256:512], a[:, 256:512] + b[:, 0:256]], axis=1)

    h = joined(wave[512:576], wave[576:640])
    total = [None] * 4
    for chi in range(2):
        u = joined(wave[chi * 256 : chi * 256 + 128], wave[chi * 256 + 128 : chi * 256 + 256])
        for clo in range(2):
            cls = 2 * chi + clo
            e = h[cls * 16 : cls * 16 + 16]
            whole = jnp.concatenate([e[0:8], u[clo * 64 : clo * 64 + 64], e[8:16]], axis=0)
            ur = whole[:, 0:256]
            ui = whole[:, 256:512]
            cos = folds[0][cls * 4 : cls * 4 + 4]
            sin = folds[1][cls * 4 : cls * 4 + 4]
            for f in range(4):
                g = ur * cos[f : f + 1] - ui * sin[f : f + 1]
                total[f] = g if total[f] is None else total[f] + g
    scale = 1.0 / (PIXELS * PIXELS)
    total = [g * scale for g in total]
    total = total + [sign * g for g in total]
    none = jnp.zeros((80, 128), F32)
    lane = lax.broadcasted_iota(jnp.int32, (80, 128), 1)
    for f in range(8):
        before = total[f - 1][:, 128:256] if f > 0 else none
        after = total[f + 1][:, 0:128] if f < 7 else none
        line = jnp.concatenate([before, total[f], after], axis=1)
        line = pltpu.roll(line, 512 - 120, 1)
        pack = jnp.where(f == me - 1, base_ref[0, :, 256:384], 0.0)
        pack = pack + jnp.where(f == me + 1, base_ref[1, :, 256:384], 0.0)
        o_ref[f, :, 0:256] = line[:, 0:256].astype(BF)
        o_ref[f, :, 256:384] = jnp.where(lane < 16, line[:, 256:384], pack).astype(BF)


def tiles_kernel(where_ref, slots_ref, count_ref, tiles_ref, table_ref, o_ref):
    channel = where_ref[0]
    left = lax.broadcasted_iota(jnp.int32, (32, 128), 0)
    right = lax.broadcasted_iota(jnp.int32, (32, 128), 1)
    tile = jnp.full((32, 128), -1, jnp.int32)
    for k in range(SLOTS):
        slot = jnp.where(k < count_ref[channel, 0], slots_ref[channel, 0, k], -1)
        tile = jnp.where(left // 4 == k, slot, tile)
    pick = (tile == right // 4) & (left % 4 == right % 4)
    pick = jnp.where(pick, 1.0, 0.0).astype(BF)
    o_ref[...] = jnp.zeros_like(o_ref)
    for k in range(0, SLOTS, 2):
        pair = [tiles_ref[channel, 0, k + n].astype(F32).T for n in range(2)]
        o_ref[256:320, k * 64 : k * 64 + 128] = jnp.concatenate(pair, axis=1).astype(BF)
    o_ref[256:320, 384:1152] = table_ref[256:320, :]
    o_ref[256:320, 1152:1536] = table_ref[320:384, 0:384]
    for t in range(2):
        row = dot(pick, table_ref[t * 128 : t * 128 + 128, :]).astype(BF)
        for j in range(2):
            for chi in range(2):
                p = 2 * j + chi
                rows = slice(t * 128 + p * 32, t * 128 + p * 32 + 32)
                o_ref[rows, p * 256 : p * 256 + 256] = row[:, 0:256]
                for comp in range(2):
                    at = 256 + chi * 256 + comp * 128
                    to = 1024 + comp * 256 + j * 128
                    o_ref[rows, to : to + 128] = row[:, at : at + 128]


def gram_kernel(d_ref, e_ref, o_ref, rows, rhs, mid, edge, out, sem):
    rows[0:1024, :] = d_ref[...].reshape(1024, 128).astype(F32)
    for p in range(16):
        lanes = slice(p * 128, p * 128 + 128)
        at = (p % 2) * 8 + p // 2
        rhs[0:32, lanes] = rows[pl.ds(at, 32, stride=32), :].astype(BF)
        rhs[32:64, lanes] = rows[pl.ds(16 + at, 32, stride=32), :].astype(BF)
    fixed = e_ref[256:320, :]
    block = [fixed[:, 384:448], fixed[:, 448:512]]
    turns = fixed[:, 512:1024].astype(F32) + fixed[:, 1024:1536].astype(F32)
    tc, ts, ec, es = (turns[:, n * 128 : n * 128 + 128] for n in range(4))
    first = dot(jnp.concatenate(block, axis=0), rhs[...])
    first = first[0:64] + first[64:128]
    for p in range(16):
        g = first[:, p * 128 : p * 128 + 128]
        gr = jnp.concatenate([g[0:32], g[0:32]], axis=0)
        gi = jnp.concatenate([g[32:64], g[32:64]], axis=0)
        down = slice(p // 4 * 64, p // 4 * 64 + 64)
        at = p % 4 * 256
        mid[down, at : at + 128] = (gr * tc + gi * ts).astype(BF)
        mid[down, at + 128 : at + 256] = (gi * tc - gr * ts).astype(BF)
    spec = dot(mid[...], e_ref[0:256, 0:1024], LAST)
    spec = (spec[:, 0:128] + spec[:, 128:256]).astype(BF)
    spec = jnp.concatenate([spec[g * 64 : g * 64 + 64] for g in range(4)], axis=1)
    tiles = [fixed[:, k * 64 : k * 64 + 64] for k in range(SLOTS)]
    mixed = dot(jnp.concatenate(tiles, axis=0), spec)
    lane_slot = (lax.broadcasted_iota(jnp.int32, (64, 512), 1) % 32) // 4
    weighted = jnp.where(lane_slot == 0, mixed[0:64], 0.0)
    for k in range(1, SLOTS):
        weighted = jnp.where(lane_slot == k, mixed[k * 64 : k * 64 + 64], weighted)
    weighted = weighted.astype(BF)
    w = jnp.concatenate([weighted[:, g * 128 : g * 128 + 128] for g in range(4)], axis=0)
    spreads = dot(jnp.concatenate([w, w], axis=1), e_ref[0:256, :])
    for g in range(4):
        z = spreads[g * 64 : g * 64 + 64]
        for v in range(4):
            p = g * 4 + v
            zr = z[:, v * 256 : v * 256 + 128]
            zi = z[:, v * 256 + 128 : v * 256 + 256]
            hr = zr * tc - zi * ts
            hi = zi * tc + zr * ts
            rhs[0:32, p * 128 : p * 128 + 128] = (hr[0:32] + hr[32:64]).astype(BF)
            rhs[32:64, p * 128 : p * 128 + 128] = (hi[0:32] + hi[32:64]).astype(BF)
        for j in range(2):
            zr = z[:, 1024 + j * 128 : 1152 + j * 128]
            zi = z[:, 1280 + j * 128 : 1408 + j * 128]
            hr = zr * ec - zi * es
            hi = zi * ec + zr * es
            lanes = slice((2 * g + j) * 128, (2 * g + j) * 128 + 128)
            edge[0:32, lanes] = (hr[0:32] + hr[32:64]).astype(BF)
            edge[32:64, lanes] = (hi[0:32] + hi[32:64]).astype(BF)
    block = jnp.concatenate(block, axis=1)
    last = dot(block, rhs[...], FIRST)
    last = last[0:64] + last[64:128]
    outer = dot(block, edge[...], FIRST)
    outer = outer[0:32] + outer[64:96]
    for p in range(16):
        lanes = slice(p * 128, p * 128 + 128)
        at = (p % 2) * 8 + p // 2
        rows[pl.ds(at, 32, stride=40), :] = last[0:32, lanes]
        rows[pl.ds(16 + at, 32, stride=40), :] = last[32:64, lanes]
    for v in range(8):
        rows[pl.ds(32 + v, 32, stride=40), :] = outer[:, v * 128 : v * 128 + 128]
    leave = []
    for n in range(2):
        half = rows[n * 640 : n * 640 + 640, :]
        out[n] = half.reshape(16, 40, 128).astype(BF)
        to = o_ref.at[pl.ds(n * 16, 16)]
        leave.append(pltpu.make_async_copy(out.at[n], to, sem.at[n]))
        leave[n].start()
    for n in range(2):
        leave[n].wait()


def bands_kernel(taps_ref, o_ref):
    lane = lax.broadcasted_iota(jnp.int32, (64, 256), 1)
    for k in range(FRAMES):
        wide = jnp.broadcast_to(taps_ref[k : k + 1, :], (128, 256))
        band = pltpu.roll(wide, 0, 1, stride=1, stride_axis=0)
        high = band.astype(BF)
        low = band - high.astype(F32)
        o_ref[k * 128 : k * 128 + 128, :] = high
        o_ref[1024 + k * 128 : 1152 + k * 128, :] = low.astype(BF)
        low = jnp.where(lane < 80, low[0:64], 0.0)
        high = jnp.where(lane < 80, high[0:64].astype(F32), 0.0)
        row = high + pltpu.roll(high, 80, 1) + pltpu.roll(low, 160, 1)
        o_ref[2048 + k * 64 : 2112 + k * 64, :] = row.astype(BF)


def synth_kernel(
    where_ref,
    live_ref,
    dual_ref,
    sky_hbm,
    dirty_hbm,
    bands_ref,
    o_ref,
    head_ref,
    tail_ref,
    sky_ref,
    dirty_ref,
    across,
    sky_sem,
    dirty_sem,
):
    channels = sky_ref.shape[0]
    sky_copy = pltpu.make_async_copy(sky_hbm, sky_ref, sky_sem)
    sky_copy.start()
    dirty_copy = pltpu.make_async_copy(dirty_hbm, dirty_ref, dirty_sem)
    dirty_copy.start()
    row = lax.broadcasted_iota(jnp.int32, (80, WIDE), 0) + where_ref[2] * ROWS - RADIUS
    lane = lax.broadcasted_iota(jnp.int32, (80, WIDE), 1)
    col = lane + where_ref[3] * COLS - RADIUS
    inside = (row >= 0) & (row < PIXELS) & (col >= 0) & (col < PIXELS)
    for k in range(FRAMES):
        p = dual_ref[:, k + 1].reshape(channels * ROWS, COLS)
        both = jnp.concatenate([p[:, 0:128], p[:, 128:256]], axis=0)
        both = jnp.concatenate([both, both], axis=1)
        at = k * 128
        band = jnp.concatenate(
            [bands_ref[at : at + 128, :], bands_ref[1024 + at : 1152 + at, :]], axis=0
        )
        a = dot(both, band)
        a0 = a[0 : channels * ROWS]
        a1 = a[channels * ROWS :]
        out = jnp.concatenate([a0[:, 0:128], a0[:, 128:256] + a1[:, 0:128], a1[:, 128:256]], axis=1)
        for c in range(channels):
            across[c, k * ROWS : (k + 1) * ROWS, :] = out[c * ROWS : (c + 1) * ROWS].astype(BF)
    sky_copy.wait()
    dirty_copy.wait()
    live = lax.broadcasted_iota(jnp.int32, (ROWS, COLS), 0) < live_ref[0]
    none = jnp.zeros((ROWS, 128), F32)
    edge = jnp.zeros((8, WIDE), F32)
    for c in range(channels):
        total = dot(bands_ref[2048:2560, :], across[c], FIRST)
        total = total[0:80] + total[160:240]
        sky = sky_ref[c]
        own = sky + STEP_PRIMAL * dirty_ref[c] - STEP_PRIMAL * dual_ref[c, 0].astype(F32)
        own = jnp.where(live, own, OUTSIDE)
        own = pltpu.roll(jnp.concatenate([own, none], axis=1), 8, 1)
        sky = pltpu.roll(jnp.concatenate([sky, none], axis=1), 8, 1)
        total = total * (-STEP_PRIMAL)
        total = total + jnp.concatenate([edge, own, edge], axis=0)
        total = jnp.where(inside, total, OUTSIDE)
        total = jnp.where(lane < COLS + 2 * RADIUS, total, 0.0)
        sky = jnp.concatenate([edge, sky, edge], axis=0)
        for at, cells in ((c, total), (channels + c, sky)):
            o_ref[at] = cells
            head_ref[at] = cells[0:16].astype(BF)
            tail_ref[at] = cells[64:80].astype(BF)


def edge_kernel(base_ref, before_ref, after_ref, o_ref):
    both = base_ref.shape[0]
    lane = lax.broadcasted_iota(jnp.int32, (80, 128), 1)
    head = jnp.zeros((80, 128), F32)
    tail = jnp.zeros((80, 128), F32)
    for c in range(both):
        o_ref[c, 0:16] = base_ref[c, 0:16] + before_ref[c].astype(F32)
        o_ref[c, 16:64] = base_ref[c, 16:64]
        o_ref[c, 64:80] = base_ref[c, 64:80] + after_ref[c].astype(F32)
        first = o_ref[c, :, 0:128]
        final = o_ref[c, :, 256:384]
        if c < both // 2:
            at = 16 + 16 * c
            head = head + pltpu.roll(jnp.where(lane < 16, first, 0.0), at, 1)
            tail = tail + pltpu.roll(jnp.where(lane < 16, final, 0.0), at, 1)
        else:
            at = 80 + 8 * (c - both // 2)
            head = head + pltpu.roll(jnp.where((lane >= 8) & (lane < 16), first, 0.0), at - 8, 1)
            tail = tail + pltpu.roll(jnp.where(lane < 8, final, 0.0), at, 1)
    o_ref[0, :, 256:384] = o_ref[0, :, 256:384] + head
    o_ref[1, :, 256:384] = o_ref[1, :, 256:384] + tail


def frames_kernel(
    bound_ref,
    where_ref,
    half_ref,
    base_ref,
    dual_ref,
    bands_ref,
    image_ref,
    o_ref,
    image_buf,
    dual_buf,
    probes,
    wide,
    down,
    image_sem,
    dual_sem,
):
    channels = image_buf.shape[0]
    rows = channels * ROWS

    def dual_copy(k):
        return pltpu.make_async_copy(dual_buf.at[k], o_ref.at[:, k], dual_sem.at[k])

    def finish(k, analysis):
        bound = bound_ref[k]
        cand = [dual_ref[c, k].astype(F32) + STEP_DUAL * analysis(c) for c in range(channels)]
        square = cand[0] * cand[0]
        for c in range(1, channels):
            square = square + cand[c] * cand[c]
        factor = bound * lax.rsqrt(jnp.maximum(square, bound * bound))
        for c in range(channels):
            dual_buf[k, c] = (cand[c] * factor).astype(BF)
        dual_copy(k).start()

    wide[...] = jnp.zeros_like(wide)
    me = where_ref[3]
    last = half_ref.shape[0] - 1
    lane = lax.broadcasted_iota(jnp.int32, (80, 128), 1)
    left = half_ref[jnp.maximum(me - 1, 0), :, 256:384].astype(F32)
    left = jnp.where(me > 0, left, 0.0)
    right = half_ref[jnp.minimum(me + 1, last), :, 256:384].astype(F32)
    right = jnp.where(me < last, right, 0.0)
    for c in range(channels):
        gram = half_ref[2 * c].astype(F32) + half_ref[2 * c + 1].astype(F32)
        gram = [gram[:, 0:128], gram[:, 128:256], jnp.where(lane < 16, gram[:, 256:384], 0.0)]
        base = [base_ref[c, :, b * 128 : b * 128 + 128] for b in range(3)]
        sky = [base_ref[channels + c, :, b * 128 : b * 128 + 128] for b in range(3)]
        base[2] = jnp.where(lane < 16, base[2], 0.0)
        at = 16 + 16 * c
        base[0] = base[0] + jnp.where(lane < 16, pltpu.roll(left, 128 - at, 1), 0.0)
        base[2] = base[2] + jnp.where(lane < 16, pltpu.roll(right, 128 - at, 1), 0.0)
        at = 80 + 8 * c
        sky[0] = sky[0] + jnp.where(lane < 8, pltpu.roll(left, 128 - at, 1), 0.0)
        shown = (lane >= 8) & (lane < 16)
        sky[2] = sky[2] + jnp.where(shown, pltpu.roll(right, 136 - at, 1), 0.0)
        image = [jnp.maximum(base[b] - STEP_PRIMAL * gram[b], 0.0) for b in range(3)]
        probe = jnp.concatenate([2.0 * image[b] - sky[b] for b in range(3)], axis=1)
        image = pltpu.roll(jnp.concatenate(image, axis=1), WIDE - 8, 1)
        image_buf[c] = image[8:72, 0:256]
        probes[c] = pltpu.roll(probe, WIDE - 8, 1)[8:72, 0:256]
        high = probe.astype(BF)
        low = (probe - high.astype(F32)).astype(BF)
        wide[0:80, :] = high
        wide[80:160, :] = low
        wide[160:240, :] = high
        d = dot(bands_ref[2048:2560, :], wide[...])
        high = d.astype(BF)
        down[0, c] = high
        down[1, c] = (d - high.astype(F32)).astype(BF)
    image_copy = pltpu.make_async_copy(image_buf, image_ref, image_sem)
    image_copy.start()
    finish(0, lambda c: probes[c])
    for k in range(1, FRAMES + 1):
        at = (k - 1) * ROWS
        a = None
        for t in range(2):
            d = jnp.concatenate([down[t, c, at : at + ROWS, :] for c in range(channels)], axis=0)
            both = jnp.concatenate([d[:, 0:256], d[:, 128:384]], axis=0)
            high = bands_ref[(k - 1) * 128 : k * 128, :]
            if t == 0:
                band = jnp.concatenate([high, bands_ref[896 + k * 128 : 1024 + k * 128, :]], axis=0)
                term = dot(both, band, LAST)
                a = term[:, 0:128] + term[:, 128:256]
            else:
                a = a + dot(both, high, LAST)
        finish(
            k,
            lambda c: jnp.concatenate(
                [a[c * ROWS : c * ROWS + ROWS], a[rows + c * ROWS : rows + c * ROWS + ROWS]], axis=1
            ),
        )
    image_copy.wait()
    for k in range(FRAMES + 1):
        dual_copy(k).wait()


VM = pl.BlockSpec(memory_space=pltpu.VMEM)
SM = pl.BlockSpec(memory_space=pltpu.SMEM)
HB = pl.BlockSpec(memory_space=pltpu.HBM)


def call(kernel, out_shape, scratch, flops, moved, *args, scalars=0, result=VM):
    return pl.pallas_call(
        kernel,
        out_shape=out_shape,
        in_specs=[SM] * scalars + [VM] * (len(args) - scalars),
        out_specs=jax.tree.map(lambda _: result, out_shape),
        scratch_shapes=scratch,
        compiler_params=pltpu.CompilerParams(vmem_limit_bytes=VMEM_LIMIT),
        cost_estimate=pl.CostEstimate(flops=flops, bytes_accessed=moved, transcendentals=0),
    )(*args)


def frames_call(thresholds, where, halves, base, dual, bands):
    channels = dual.shape[0]
    block = (channels, ROWS, COLS)
    return pl.pallas_call(
        frames_kernel,
        out_shape=(jax.ShapeDtypeStruct(block, F32), jax.ShapeDtypeStruct(dual.shape, BF)),
        in_specs=[SM, SM, VM, VM, VM, VM],
        out_specs=(pl.BlockSpec(memory_space=pl.ANY), pl.BlockSpec(memory_space=pl.ANY)),
        scratch_shapes=[
            pltpu.VMEM(block, F32),
            pltpu.VMEM((FRAMES + 1, *block), BF),
            pltpu.VMEM(block, F32),
            pltpu.VMEM((256, WIDE), BF),
            pltpu.VMEM((2, channels, FRAMES * ROWS, WIDE), BF),
            pltpu.SemaphoreType.DMA(()),
            pltpu.SemaphoreType.DMA((FRAMES + 1,)),
        ],
        compiler_params=pltpu.CompilerParams(vmem_limit_bytes=VMEM_LIMIT),
        cost_estimate=pl.CostEstimate(flops=1 << 31, bytes_accessed=3 << 20, transcendentals=0),
    )(thresholds, where, halves, base, dual, bands)


def after(values, *events):
    return lax.optimization_barrier((*values, *events))[: len(values)]


def body(
    sky_estimate,
    dual_coeffs,
    dirty_image,
    filters,
    thresholds,
    facet_rows,
    tile_slots,
    tile_count,
    gram_tiles,
):
    channels, tile_rows, tile_cols = sky_estimate.shape
    place = lax.axis_index("fou")
    where = jnp.stack([place >> 1, place & 1, lax.axis_index("img"), place]).astype(jnp.int32)

    sent = pl.pallas_call(
        send_kernel,
        out_shape=jax.ShapeDtypeStruct((2 * channels, tile_rows, tile_cols), BF),
        in_specs=[pl.BlockSpec(memory_space=pltpu.HBM)],
        out_specs=pl.BlockSpec(memory_space=pltpu.HBM),
        scratch_shapes=[
            pltpu.VMEM(sky_estimate.shape, F32),
            pltpu.VMEM(sky_estimate.shape, BF),
            pltpu.SemaphoreType.DMA((channels,)),
            pltpu.SemaphoreType.DMA((channels, 2)),
        ],
        compiler_params=pltpu.CompilerParams(vmem_limit_bytes=VMEM_LIMIT),
    )(pltpu.with_memory_space_constraint(sky_estimate, pltpu.HBM))
    lines = lax.all_to_all(sent, "fou", split_axis=0, concat_axis=0, tiled=True)

    taps = jnp.pad(filters, ((0, 0), (0, 256 - filters.shape[1])))
    bands = call(
        bands_kernel, jax.ShapeDtypeStruct((2560, 256), BF), [], 1 << 20, 1 << 20, taps
    )
    (ready_where,) = after((where,), bands)
    line = wave_table()
    held = call(hold_kernel, jax.ShapeDtypeStruct(line.shape, BF), [], 1 << 10, 1 << 20, line)
    packed = call(
        forward_kernel,
        jax.ShapeDtypeStruct((PEERS_IMG, 32, 128), BF),
        [],
        1 << 29,
        1 << 20,
        ready_where,
        lines,
        held,
        scalars=1,
    )
    received = lax.all_to_all(packed, "img", split_axis=0, concat_axis=0, tiled=True)

    spread = call(
        tiles_kernel,
        jax.ShapeDtypeStruct((320, 1536), BF),
        [],
        1 << 23,
        1 << 20,
        where,
        tile_slots,
        tile_count,
        gram_tiles,
        sampled_table(),
        scalars=3,
    )

    ends = jax.ShapeDtypeStruct((2 * channels, 16, WIDE), BF)
    extended = jax.ShapeDtypeStruct((2 * channels, tile_rows + 16, WIDE), F32)
    (late_where,) = after((where,), packed)
    base, head, tail = pl.pallas_call(
        synth_kernel,
        out_shape=(extended, ends, ends),
        in_specs=[SM, SM, VM, HB, HB, VM],
        out_specs=(VM, VM, VM),
        scratch_shapes=[
            pltpu.VMEM(sky_estimate.shape, F32),
            pltpu.VMEM(sky_estimate.shape, F32),
            pltpu.VMEM((channels, FRAMES * ROWS, WIDE), BF),
            pltpu.SemaphoreType.DMA(()),
            pltpu.SemaphoreType.DMA(()),
        ],
        compiler_params=pltpu.CompilerParams(vmem_limit_bytes=VMEM_LIMIT),
        cost_estimate=pl.CostEstimate(flops=1 << 31, bytes_accessed=4 << 20, transcendentals=0),
    )(
        late_where,
        facet_rows,
        dual_coeffs,
        pltpu.with_memory_space_constraint(sky_estimate, pltpu.HBM),
        pltpu.with_memory_space_constraint(dirty_image, pltpu.HBM),
        bands,
    )
    (received,) = after((received,), head)

    scratch = [
        pltpu.VMEM((1280, 128), F32),
        pltpu.VMEM((64, 2048), BF),
        pltpu.VMEM((256, 1024), BF),
        pltpu.VMEM((64, 1024), BF),
        pltpu.VMEM((2, 16, 40, 128), BF),
        pltpu.SemaphoreType.DMA((2,)),
    ]
    weighted = call(
        gram_kernel,
        jax.ShapeDtypeStruct((PEERS_IMG, 40, 128), BF),
        scratch,
        1 << 29,
        1 << 20,
        received,
        spread,
        result=HB,
    )
    returned = lax.all_to_all(weighted, "img", split_axis=0, concat_axis=0, tiled=True)

    head, tail = after((head, tail), weighted)
    steps = [(i, i + 1) for i in range(PEERS_IMG - 1)]
    from_before = lax.ppermute(tail, "img", steps)
    from_after = lax.ppermute(head, "img", [(j, i) for i, j in steps])
    base = call(
        edge_kernel,
        extended,
        [],
        1 << 20,
        4 << 20,
        base,
        from_before,
        from_after,
    )
    blocks = call(
        inverse_kernel,
        jax.ShapeDtypeStruct((8, tile_rows + 16, WIDE), BF),
        [],
        1 << 29,
        1 << 20,
        where,
        returned,
        line,
        base,
        scalars=1,
    )
    halves = lax.all_to_all(blocks, "fou", split_axis=0, concat_axis=0, tiled=True)

    return frames_call(thresholds, where, halves, base, dual_coeffs, bands)


def solution(mesh):
    in_specs = (
        P(None, "img", "fou"),
        P(None, None, "img", "fou"),
        P(None, "img", "fou"),
        P(),
        P(),
        P("img"),
        P(None, "img", None),
        P(None, "img"),
        P(None, "img", None, None, None),
    )
    out_specs = (P(None, "img", "fou"), P(None, None, "img", "fou"))
    return jax.shard_map(body, mesh=mesh, in_specs=in_specs, out_specs=out_specs, check_vma=False)
```

```python
import math

import jax
import jax.numpy as jnp
import numpy as np
from jax import lax
from jax.experimental import pallas as pl
from jax.experimental.pallas import tpu as pltpu
from jax.sharding import PartitionSpec as P

PIXELS = 2048
RADIUS = 8
SLOTS = 6
ROWS = 64
COLS = 256
FRAMES = 8
PEERS_IMG = 32
STEP_PRIMAL = 0.5
STEP_DUAL = 0.5
BF = jnp.bfloat16
F32 = jnp.float32
VMEM_LIMIT = 20 << 20
WIDE = 384
OUTSIDE = -1.0e30
LAST = ((1,), (1,))
FIRST = ((0,), (0,))


def two_terms_np(table):
    high = table.astype(jnp.bfloat16)
    low = (table - high.astype(np.float64)).astype(jnp.bfloat16)
    return high, low


def two_terms(table):
    high = table.astype(BF)
    return high, (table - high.astype(F32)).astype(BF)


def dot(a, b, dims=((1,), (0,))):
    return lax.dot_general(a, b, (dims, ((), ())), preferred_element_type=F32)


def angle_np(a, b, period):
    return 2.0 * np.pi * ((a[:, None] * b[None, :]) % period) / period


def line_table():
    ang = angle_np(np.arange(256), np.arange(256), 256)
    return two_terms_np(np.concatenate([np.cos(ang), np.sin(ang)], axis=1))


def block_table():
    ang = angle_np(np.arange(32), np.arange(32), 32)
    c, s = np.cos(ang), np.sin(ang)
    return two_terms_np(np.block([[c, s], [-s, c]]))


HALO = np.concatenate([np.arange(-8, 0), np.arange(64, 72)])


def turn_table():
    main = np.tile(np.arange(64), 2)
    halo = np.tile(HALO, 8)
    ang = [angle_np(np.arange(64), r, 2048) for r in (main, halo)]
    return two_terms_np(
        np.concatenate([np.cos(ang[0]), np.sin(ang[0]), np.cos(ang[1]), np.sin(ang[1])])
    )


def fixed_table():
    turns = [np.concatenate(np.split(t, 4), axis=1) for t in turn_table()]
    return np.concatenate([*block_table(), *turns], axis=1)


def sampled_table():
    fixed = fixed_table()
    rest = np.zeros((64, 768), fixed.dtype)
    rest[:, 0:384] = fixed[:, 768:1152]
    return np.concatenate([*tile_table(), fixed[:, 0:768], rest], axis=0)


def tile_table():
    t = np.arange(32)
    ang = angle_np(t, np.arange(64), 32)
    c, s = np.cos(ang), np.sin(ang)
    main = np.zeros((32, 2, 2, 2, 2, 64))
    for p in range(2):
        main[:, p, 0, 0, p] = c
        main[:, p, 1, 0, p] = -s
        main[:, p, 0, 1, p] = s
        main[:, p, 1, 1, p] = c
    ang = angle_np(t, HALO, 32)
    c, s = np.cos(ang), np.sin(ang)
    halo = np.zeros((32, 2, 2, 2, 2, 2, 2, 2, 16))
    for p in range(2):
        for x in range(2):
            halo[:, p, 0, x, 0, 0, x, p] = c
            halo[:, p, 1, x, 0, 0, x, p] = -s
            halo[:, p, 0, x, 1, 0, x, p] = s
            halo[:, p, 1, x, 1, 0, x, p] = c
            halo[:, p, 0, x, 0, 1, x, p] = s
            halo[:, p, 1, x, 0, 1, x, p] = c
            halo[:, p, 0, x, 1, 1, x, p] = -c
            halo[:, p, 1, x, 1, 1, x, p] = s
    table = np.concatenate([main.reshape(128, 256), halo.reshape(128, 512)], axis=1)
    return two_terms_np(table)


def wave_table():
    freq = np.arange(2)[:, None] + 2 * np.arange(4)[None]
    pos = np.arange(4 * COLS).reshape(4, COLS)
    ang = 2.0 * np.pi * ((freq[:, :, None, None] * pos) % PIXELS) / PIXELS
    fold = np.concatenate([np.cos(ang), np.sin(ang)], axis=3).reshape(32, 2 * COLS)
    return np.concatenate([np.stack(line_table()), np.stack(two_terms_np(fold))], axis=1)


def fold_rows(line_ref, par):
    at = pl.multiple_of(256 + 16 * par, 16)
    fold = line_ref[0, pl.ds(at, 16), :].astype(F32) + line_ref[1, pl.ds(at, 16), :].astype(F32)
    return fold[:, 0:256], fold[:, 256:512]


def hold_kernel(table_ref, o_ref):
    o_ref[...] = table_ref[...]


def send_kernel(sky_ref, o_ref, taken, rounded, in_sem, out_sem):
    channels = taken.shape[0]

    def fetch(c):
        return pltpu.make_async_copy(sky_ref.at[c], taken.at[c], in_sem.at[c])

    def place(c, h):
        return pltpu.make_async_copy(rounded.at[c], o_ref.at[2 * c + h], out_sem.at[c, h])

    for c in range(channels):
        fetch(c).start()
    for c in range(channels):
        fetch(c).wait()
        rounded[c] = taken[c].astype(BF)
        for h in range(2):
            place(c, h).start()
    for c in range(channels):
        for h in range(2):
            place(c, h).wait()


def forward_kernel(par_ref, x_ref, line_ref, o_ref, out, sem):
    par = par_ref[1]
    folds = fold_rows(line_ref, par)
    sign = (1 - 2 * par).astype(F32)
    xe = [x_ref[f].astype(F32) + sign * x_ref[f + 4].astype(F32) for f in range(4)]
    rows = [[], []]
    for cls in range(4):
        cos = folds[0][cls * 4 : cls * 4 + 4]
        sin = folds[1][cls * 4 : cls * 4 + 4]
        yr = xe[0] * cos[0:1]
        yi = xe[0] * sin[0:1]
        for f in range(1, 4):
            yr = yr + xe[f] * cos[f : f + 1]
            yi = yi + xe[f] * sin[f : f + 1]
        rows[0].append(jnp.concatenate([yr, -yi], axis=1).astype(BF))
        rows[1].append(jnp.concatenate([-yi, -yr], axis=1).astype(BF))
    def leave(part):
        to = o_ref.at[:, pl.ds(part * 16, 16), :]
        return pltpu.make_async_copy(out.at[part], to, sem.at[part])

    for part in range(2):
        r = jnp.concatenate(rows[part], axis=0)
        wave = dot(line_ref[0, 0:256], r, LAST) + dot(line_ref[1, 0:256], r, LAST)
        both = [wave[:, chi * 128 : chi * 128 + 128].reshape(32, 8, 128) for chi in range(2)]
        out[part] = jnp.concatenate(both, axis=1).astype(BF)
        leave(part).start()
    for part in range(2):
        leave(part).wait()


def inverse_kernel(par_ref, t_ref, line_ref, base_ref, o_ref):
    par = par_ref[1]
    folds = fold_rows(line_ref, par)
    me = par_ref[3]
    sign = (1 - 2 * par).astype(F32)
    re = t_ref[:, 0:16, :].astype(F32)
    im = t_ref[:, 16:32, :].astype(F32)
    edge = t_ref[:, 32:40, :].astype(F32)
    data = [re[:, 0:8], im[:, 0:8], re[:, 8:16], im[:, 8:16], edge]
    data = jnp.concatenate([d.reshape(256, 128).astype(BF) for d in data], axis=1)
    wave = dot(data, line_ref[0, 0:256], FIRST) + dot(data, line_ref[1, 0:256], FIRST)

    def joined(a, b):
        return jnp.concatenate([a[:, 0:256] - b[:, 256:512], a[:, 256:512] + b[:, 0:256]], axis=1)

    h = joined(wave[512:576], wave[576:640])
    total = [None] * 4
    for chi in range(2):
        u = joined(wave[chi * 256 : chi * 256 + 128], wave[chi * 256 + 128 : chi * 256 + 256])
        for clo in range(2):
            cls = 2 * chi + clo
            e = h[cls * 16 : cls * 16 + 16]
            whole = jnp.concatenate([e[0:8], u[clo * 64 : clo * 64 + 64], e[8:16]], axis=0)
            ur = whole[:, 0:256]
            ui = whole[:, 256:512]
            cos = folds[0][cls * 4 : cls * 4 + 4]
            sin = folds[1][cls * 4 : cls * 4 + 4]
            for f in range(4):
                g = ur * cos[f : f + 1] - ui * sin[f : f + 1]
                total[f] = g if total[f] is None else total[f] + g
    scale = 1.0 / (PIXELS * PIXELS)
    total = [g * scale for g in total]
    total = total + [sign * g for g in total]
    none = jnp.zeros((80, 128), F32)
    lane = lax.broadcasted_iota(jnp.int32, (80, 128), 1)
    for f in range(8):
        before = total[f - 1][:, 128:256] if f > 0 else none
        after = total[f + 1][:, 0:128] if f < 7 else none
        line = jnp.concatenate([before, total[f], after], axis=1)
        line = pltpu.roll(line, 512 - 120, 1)
        pack = jnp.where(f == me - 1, base_ref[0, :, 256:384], 0.0)
        pack = pack + jnp.where(f == me + 1, base_ref[1, :, 256:384], 0.0)
        o_ref[f, :, 0:256] = line[:, 0:256].astype(BF)
        o_ref[f, :, 256:384] = jnp.where(lane < 16, line[:, 256:384], pack).astype(BF)


def tiles_kernel(where_ref, slots_ref, count_ref, tiles_ref, table_ref, o_ref):
    channel = where_ref[0]
    left = lax.broadcasted_iota(jnp.int32, (32, 128), 0)
    right = lax.broadcasted_iota(jnp.int32, (32, 128), 1)
    tile = jnp.full((32, 128), -1, jnp.int32)
    for k in range(SLOTS):
        slot = jnp.where(k < count_ref[channel, 0], slots_ref[channel, 0, k], -1)
        tile = jnp.where(left // 4 == k, slot, tile)
    pick = (tile == right // 4) & (left % 4 == right % 4)
    pick = jnp.where(pick, 1.0, 0.0).astype(BF)
    o_ref[...] = jnp.zeros_like(o_ref)
    for k in range(0, SLOTS, 2):
        pair = [tiles_ref[channel, 0, k + n].astype(F32).T for n in range(2)]
        o_ref[256:320, k * 64 : k * 64 + 128] = jnp.concatenate(pair, axis=1).astype(BF)
    o_ref[256:320, 384:1152] = table_ref[256:320, :]
    o_ref[256:320, 1152:1536] = table_ref[320:384, 0:384]
    for t in range(2):
        row = dot(pick, table_ref[t * 128 : t * 128 + 128, :]).astype(BF)
        for j in range(2):
            for chi in range(2):
                p = 2 * j + chi
                rows = slice(t * 128 + p * 32, t * 128 + p * 32 + 32)
                o_ref[rows, p * 256 : p * 256 + 256] = row[:, 0:256]
                for comp in range(2):
                    at = 256 + chi * 256 + comp * 128
                    to = 1024 + comp * 256 + j * 128
                    o_ref[rows, to : to + 128] = row[:, at : at + 128]


def gram_kernel(d_ref, e_ref, o_ref, rows, rhs, mid, edge, out, sem):
    rows[0:1024, :] = d_ref[...].reshape(1024, 128).astype(F32)
    for p in range(16):
        lanes = slice(p * 128, p * 128 + 128)
        at = (p % 2) * 8 + p // 2
        rhs[0:32, lanes] = rows[pl.ds(at, 32, stride=32), :].astype(BF)
        rhs[32:64, lanes] = rows[pl.ds(16 + at, 32, stride=32), :].astype(BF)
    fixed = e_ref[256:320, :]
    block = [fixed[:, 384:448], fixed[:, 448:512]]
    turns = fixed[:, 512:1024].astype(F32) + fixed[:, 1024:1536].astype(F32)
    tc, ts, ec, es = (turns[:, n * 128 : n * 128 + 128] for n in range(4))
    first = dot(jnp.concatenate(block, axis=0), rhs[...])
    first = first[0:64] + first[64:128]
    for p in range(16):
        g = first[:, p * 128 : p * 128 + 128]
        gr = jnp.concatenate([g[0:32], g[0:32]], axis=0)
        gi = jnp.concatenate([g[32:64], g[32:64]], axis=0)
        down = slice(p // 4 * 64, p // 4 * 64 + 64)
        at = p % 4 * 256
        mid[down, at : at + 128] = (gr * tc + gi * ts).astype(BF)
        mid[down, at + 128 : at + 256] = (gi * tc - gr * ts).astype(BF)
    spec = dot(mid[...], e_ref[0:256, 0:1024], LAST)
    spec = (spec[:, 0:128] + spec[:, 128:256]).astype(BF)
    spec = jnp.concatenate([spec[g * 64 : g * 64 + 64] for g in range(4)], axis=1)
    tiles = [fixed[:, k * 64 : k * 64 + 64] for k in range(SLOTS)]
    mixed = dot(jnp.concatenate(tiles, axis=0), spec)
    lane_slot = (lax.broadcasted_iota(jnp.int32, (64, 512), 1) % 32) // 4
    weighted = jnp.where(lane_slot == 0, mixed[0:64], 0.0)
    for k in range(1, SLOTS):
        weighted = jnp.where(lane_slot == k, mixed[k * 64 : k * 64 + 64], weighted)
    weighted = weighted.astype(BF)
    w = jnp.concatenate([weighted[:, g * 128 : g * 128 + 128] for g in range(4)], axis=0)
    spreads = dot(jnp.concatenate([w, w], axis=1), e_ref[0:256, :])
    for g in range(4):
        z = spreads[g * 64 : g * 64 + 64]
        for v in range(4):
            p = g * 4 + v
            zr = z[:, v * 256 : v * 256 + 128]
            zi = z[:, v * 256 + 128 : v * 256 + 256]
            hr = zr * tc - zi * ts
            hi = zi * tc + zr * ts
            rhs[0:32, p * 128 : p * 128 + 128] = (hr[0:32] + hr[32:64]).astype(BF)
            rhs[32:64, p * 128 : p * 128 + 128] = (hi[0:32] + hi[32:64]).astype(BF)
        for j in range(2):
            zr = z[:, 1024 + j * 128 : 1152 + j * 128]
            zi = z[:, 1280 + j * 128 : 1408 + j * 128]
            hr = zr * ec - zi * es
            hi = zi * ec + zr * es
            lanes = slice((2 * g + j) * 128, (2 * g + j) * 128 + 128)
            edge[0:32, lanes] = (hr[0:32] + hr[32:64]).astype(BF)
            edge[32:64, lanes] = (hi[0:32] + hi[32:64]).astype(BF)
    block = jnp.concatenate(block, axis=1)
    last = dot(block, rhs[...], FIRST)
    last = last[0:64] + last[64:128]
    outer = dot(block, edge[...], FIRST)
    outer = outer[0:32] + outer[64:96]
    for p in range(16):
        lanes = slice(p * 128, p * 128 + 128)
        at = (p % 2) * 8 + p // 2
        rows[pl.ds(at, 32, stride=40), :] = last[0:32, lanes]
        rows[pl.ds(16 + at, 32, stride=40), :] = last[32:64, lanes]
    for v in range(8):
        rows[pl.ds(32 + v, 32, stride=40), :] = outer[:, v * 128 : v * 128 + 128]
    leave = []
    for n in range(2):
        half = rows[n * 640 : n * 640 + 640, :]
        out[n] = half.reshape(16, 40, 128).astype(BF)
        to = o_ref.at[pl.ds(n * 16, 16)]
        leave.append(pltpu.make_async_copy(out.at[n], to, sem.at[n]))
        leave[n].start()
    for n in range(2):
        leave[n].wait()


def bands_kernel(taps_ref, o_ref):
    lane = lax.broadcasted_iota(jnp.int32, (64, 256), 1)
    for k in range(FRAMES):
        wide = jnp.broadcast_to(taps_ref[k : k + 1, :], (128, 256))
        band = pltpu.roll(wide, 0, 1, stride=1, stride_axis=0)
        high = band.astype(BF)
        low = band - high.astype(F32)
        o_ref[k * 128 : k * 128 + 128, :] = high
        o_ref[1024 + k * 128 : 1152 + k * 128, :] = low.astype(BF)
        low = jnp.where(lane < 80, low[0:64], 0.0)
        high = jnp.where(lane < 80, high[0:64].astype(F32), 0.0)
        row = high + pltpu.roll(high, 80, 1) + pltpu.roll(low, 160, 1)
        o_ref[2048 + k * 64 : 2112 + k * 64, :] = row.astype(BF)


def synth_kernel(
    where_ref,
    live_ref,
    dual_ref,
    sky_hbm,
    dirty_hbm,
    bands_ref,
    o_ref,
    head_ref,
    tail_ref,
    sky_ref,
    dirty_ref,
    across,
    sky_sem,
    dirty_sem,
):
    channels = sky_ref.shape[0]
    sky_copy = pltpu.make_async_copy(sky_hbm, sky_ref, sky_sem)
    sky_copy.start()
    dirty_copy = pltpu.make_async_copy(dirty_hbm, dirty_ref, dirty_sem)
    dirty_copy.start()
    row = lax.broadcasted_iota(jnp.int32, (80, WIDE), 0) + where_ref[2] * ROWS - RADIUS
    lane = lax.broadcasted_iota(jnp.int32, (80, WIDE), 1)
    col = lane + where_ref[3] * COLS - RADIUS
    inside = (row >= 0) & (row < PIXELS) & (col >= 0) & (col < PIXELS)
    for k in range(FRAMES):
        p = dual_ref[:, k + 1].reshape(channels * ROWS, COLS)
        both = jnp.concatenate([p[:, 0:128], p[:, 128:256]], axis=0)
        both = jnp.concatenate([both, both], axis=1)
        at = k * 128
        band = jnp.concatenate(
            [bands_ref[at : at + 128, :], bands_ref[1024 + at : 1152 + at, :]], axis=0
        )
        a = dot(both, band)
        a0 = a[0 : channels * ROWS]
        a1 = a[channels * ROWS :]
        out = jnp.concatenate([a0[:, 0:128], a0[:, 128:256] + a1[:, 0:128], a1[:, 128:256]], axis=1)
        for c in range(channels):
            across[c, k * ROWS : (k + 1) * ROWS, :] = out[c * ROWS : (c + 1) * ROWS].astype(BF)
    sky_copy.wait()
    dirty_copy.wait()
    live = lax.broadcasted_iota(jnp.int32, (ROWS, COLS), 0) < live_ref[0]
    none = jnp.zeros((ROWS, 128), F32)
    edge = jnp.zeros((8, WIDE), F32)
    for c in range(channels):
        total = dot(bands_ref[2048:2560, :], across[c], FIRST)
        total = total[0:80] + total[160:240]
        sky = sky_ref[c]
        own = sky + STEP_PRIMAL * dirty_ref[c] - STEP_PRIMAL * dual_ref[c, 0].astype(F32)
        own = jnp.where(live, own, OUTSIDE)
        own = pltpu.roll(jnp.concatenate([own, none], axis=1), 8, 1)
        sky = pltpu.roll(jnp.concatenate([sky, none], axis=1), 8, 1)
        total = total * (-STEP_PRIMAL)
        total = total + jnp.concatenate([edge, own, edge], axis=0)
        total = jnp.where(inside, total, OUTSIDE)
        total = jnp.where(lane < COLS + 2 * RADIUS, total, 0.0)
        sky = jnp.concatenate([edge, sky, edge], axis=0)
        for at, cells in ((c, total), (channels + c, sky)):
            o_ref[at] = cells
            head_ref[at] = cells[0:16].astype(BF)
            tail_ref[at] = cells[64:80].astype(BF)


def edge_kernel(base_ref, before_ref, after_ref, o_ref):
    both = base_ref.shape[0]
    lane = lax.broadcasted_iota(jnp.int32, (80, 128), 1)
    head = jnp.zeros((80, 128), F32)
    tail = jnp.zeros((80, 128), F32)
    for c in range(both):
        o_ref[c, 0:16] = base_ref[c, 0:16] + before_ref[c].astype(F32)
        o_ref[c, 16:64] = base_ref[c, 16:64]
        o_ref[c, 64:80] = base_ref[c, 64:80] + after_ref[c].astype(F32)
        first = o_ref[c, :, 0:128]
        final = o_ref[c, :, 256:384]
        if c < both // 2:
            at = 16 + 16 * c
            head = head + pltpu.roll(jnp.where(lane < 16, first, 0.0), at, 1)
            tail = tail + pltpu.roll(jnp.where(lane < 16, final, 0.0), at, 1)
        else:
            at = 80 + 8 * (c - both // 2)
            head = head + pltpu.roll(jnp.where((lane >= 8) & (lane < 16), first, 0.0), at - 8, 1)
            tail = tail + pltpu.roll(jnp.where(lane < 8, final, 0.0), at, 1)
    o_ref[0, :, 256:384] = o_ref[0, :, 256:384] + head
    o_ref[1, :, 256:384] = o_ref[1, :, 256:384] + tail


def frames_kernel(
    bound_ref,
    where_ref,
    half_ref,
    base_ref,
    dual_ref,
    bands_ref,
    image_ref,
    o_ref,
    image_buf,
    dual_buf,
    probes,
    wide,
    down,
    image_sem,
    dual_sem,
):
    channels = image_buf.shape[0]
    rows = channels * ROWS

    def dual_copy(k):
        return pltpu.make_async_copy(dual_buf.at[k], o_ref.at[:, k], dual_sem.at[k])

    def finish(k, analysis):
        bound = bound_ref[k]
        cand = [dual_ref[c, k].astype(F32) + STEP_DUAL * analysis(c) for c in range(channels)]
        square = cand[0] * cand[0]
        for c in range(1, channels):
            square = square + cand[c] * cand[c]
        factor = bound * lax.rsqrt(jnp.maximum(square, bound * bound))
        for c in range(channels):
            dual_buf[k, c] = (cand[c] * factor).astype(BF)
        dual_copy(k).start()

    wide[...] = jnp.zeros_like(wide)
    me = where_ref[3]
    last = half_ref.shape[0] - 1
    lane = lax.broadcasted_iota(jnp.int32, (80, 128), 1)
    left = half_ref[jnp.maximum(me - 1, 0), :, 256:384].astype(F32)
    left = jnp.where(me > 0, left, 0.0)
    right = half_ref[jnp.minimum(me + 1, last), :, 256:384].astype(F32)
    right = jnp.where(me < last, right, 0.0)
    for c in range(channels):
        gram = half_ref[2 * c].astype(F32) + half_ref[2 * c + 1].astype(F32)
        gram = [gram[:, 0:128], gram[:, 128:256], jnp.where(lane < 16, gram[:, 256:384], 0.0)]
        base = [base_ref[c, :, b * 128 : b * 128 + 128] for b in range(3)]
        sky = [base_ref[channels + c, :, b * 128 : b * 128 + 128] for b in range(3)]
        base[2] = jnp.where(lane < 16, base[2], 0.0)
        at = 16 + 16 * c
        base[0] = base[0] + jnp.where(lane < 16, pltpu.roll(left, 128 - at, 1), 0.0)
        base[2] = base[2] + jnp.where(lane < 16, pltpu.roll(right, 128 - at, 1), 0.0)
        at = 80 + 8 * c
        sky[0] = sky[0] + jnp.where(lane < 8, pltpu.roll(left, 128 - at, 1), 0.0)
        shown = (lane >= 8) & (lane < 16)
        sky[2] = sky[2] + jnp.where(shown, pltpu.roll(right, 136 - at, 1), 0.0)
        image = [jnp.maximum(base[b] - STEP_PRIMAL * gram[b], 0.0) for b in range(3)]
        probe = jnp.concatenate([2.0 * image[b] - sky[b] for b in range(3)], axis=1)
        image = pltpu.roll(jnp.concatenate(image, axis=1), WIDE - 8, 1)
        image_buf[c] = image[8:72, 0:256]
        probes[c] = pltpu.roll(probe, WIDE - 8, 1)[8:72, 0:256]
        high = probe.astype(BF)
        low = (probe - high.astype(F32)).astype(BF)
        wide[0:80, :] = high
        wide[80:160, :] = low
        wide[160:240, :] = high
        d = dot(bands_ref[2048:2560, :], wide[...])
        high = d.astype(BF)
        down[0, c] = high
        down[1, c] = (d - high.astype(F32)).astype(BF)
    image_copy = pltpu.make_async_copy(image_buf, image_ref, image_sem)
    image_copy.start()
    finish(0, lambda c: probes[c])
    for k in range(1, FRAMES + 1):
        at = (k - 1) * ROWS
        a = None
        for t in range(2):
            d = jnp.concatenate([down[t, c, at : at + ROWS, :] for c in range(channels)], axis=0)
            both = jnp.concatenate([d[:, 0:256], d[:, 128:384]], axis=0)
            high = bands_ref[(k - 1) * 128 : k * 128, :]
            if t == 0:
                band = jnp.concatenate([high, bands_ref[896 + k * 128 : 1024 + k * 128, :]], axis=0)
                term = dot(both, band, LAST)
                a = term[:, 0:128] + term[:, 128:256]
            else:
                a = a + dot(both, high, LAST)
        finish(
            k,
            lambda c: jnp.concatenate(
                [a[c * ROWS : c * ROWS + ROWS], a[rows + c * ROWS : rows + c * ROWS + ROWS]], axis=1
            ),
        )
    image_copy.wait()
    for k in range(FRAMES + 1):
        dual_copy(k).wait()


VM = pl.BlockSpec(memory_space=pltpu.VMEM)
SM = pl.BlockSpec(memory_space=pltpu.SMEM)
HB = pl.BlockSpec(memory_space=pltpu.HBM)


def call(kernel, out_shape, scratch, flops, moved, *args, scalars=0, result=VM):
    return pl.pallas_call(
        kernel,
        out_shape=out_shape,
        in_specs=[SM] * scalars + [VM] * (len(args) - scalars),
        out_specs=jax.tree.map(lambda _: result, out_shape),
        scratch_shapes=scratch,
        compiler_params=pltpu.CompilerParams(vmem_limit_bytes=VMEM_LIMIT),
        cost_estimate=pl.CostEstimate(flops=flops, bytes_accessed=moved, transcendentals=0),
    )(*args)


def frames_call(thresholds, where, halves, base, dual, bands):
    channels = dual.shape[0]
    block = (channels, ROWS, COLS)
    return pl.pallas_call(
        frames_kernel,
        out_shape=(jax.ShapeDtypeStruct(block, F32), jax.ShapeDtypeStruct(dual.shape, BF)),
        in_specs=[SM, SM, VM, VM, VM, VM],
        out_specs=(pl.BlockSpec(memory_space=pl.ANY), pl.BlockSpec(memory_space=pl.ANY)),
        scratch_shapes=[
            pltpu.VMEM(block, F32),
            pltpu.VMEM((FRAMES + 1, *block), BF),
            pltpu.VMEM(block, F32),
            pltpu.VMEM((256, WIDE), BF),
            pltpu.VMEM((2, channels, FRAMES * ROWS, WIDE), BF),
            pltpu.SemaphoreType.DMA(()),
            pltpu.SemaphoreType.DMA((FRAMES + 1,)),
        ],
        compiler_params=pltpu.CompilerParams(vmem_limit_bytes=VMEM_LIMIT),
        cost_estimate=pl.CostEstimate(flops=1 << 31, bytes_accessed=3 << 20, transcendentals=0),
    )(thresholds, where, halves, base, dual, bands)


def after(values, *events):
    return lax.optimization_barrier((*values, *events))[: len(values)]


def body(
    sky_estimate,
    dual_coeffs,
    dirty_image,
    filters,
    thresholds,
    facet_rows,
    tile_slots,
    tile_count,
    gram_tiles,
):
    channels, tile_rows, tile_cols = sky_estimate.shape
    place = lax.axis_index("fou")
    where = jnp.stack([place >> 1, place & 1, lax.axis_index("img"), place]).astype(jnp.int32)

    sent = pl.pallas_call(
        send_kernel,
        out_shape=jax.ShapeDtypeStruct((2 * channels, tile_rows, tile_cols), BF),
        in_specs=[pl.BlockSpec(memory_space=pltpu.HBM)],
        out_specs=pl.BlockSpec(memory_space=pltpu.HBM),
        scratch_shapes=[
            pltpu.VMEM(sky_estimate.shape, F32),
            pltpu.VMEM(sky_estimate.shape, BF),
            pltpu.SemaphoreType.DMA((channels,)),
            pltpu.SemaphoreType.DMA((channels, 2)),
        ],
        compiler_params=pltpu.CompilerParams(vmem_limit_bytes=VMEM_LIMIT),
    )(pltpu.with_memory_space_constraint(sky_estimate, pltpu.HBM))
    lines = lax.all_to_all(sent, "fou", split_axis=0, concat_axis=0, tiled=True)

    taps = jnp.pad(filters, ((0, 0), (0, 256 - filters.shape[1])))
    bands = call(
        bands_kernel, jax.ShapeDtypeStruct((2560, 256), BF), [], 1 << 20, 1 << 20, taps
    )
    (ready_where,) = after((where,), bands)
    line = wave_table()
    held = call(hold_kernel, jax.ShapeDtypeStruct(line.shape, BF), [], 1 << 10, 1 << 20, line)
    packed = call(
        forward_kernel,
        jax.ShapeDtypeStruct((PEERS_IMG, 32, 128), BF),
        [pltpu.VMEM((2, PEERS_IMG, 16, 128), BF), pltpu.SemaphoreType.DMA((2,))],
        1 << 29,
        1 << 20,
        ready_where,
        lines,
        held,
        scalars=1,
        result=HB,
    )
    received = lax.all_to_all(packed, "img", split_axis=0, concat_axis=0, tiled=True)


    ends = jax.ShapeDtypeStruct((2 * channels, 16, WIDE), BF)
    extended = jax.ShapeDtypeStruct((2 * channels, tile_rows + 16, WIDE), F32)
    (late_where,) = after((where,), packed)
    base, head, tail = pl.pallas_call(
        synth_kernel,
        out_shape=(extended, ends, ends),
        in_specs=[SM, SM, VM, HB, HB, VM],
        out_specs=(VM, VM, VM),
        scratch_shapes=[
            pltpu.VMEM(sky_estimate.shape, F32),
            pltpu.VMEM(sky_estimate.shape, F32),
            pltpu.VMEM((channels, FRAMES * ROWS, WIDE), BF),
            pltpu.SemaphoreType.DMA(()),
            pltpu.SemaphoreType.DMA(()),
        ],
        compiler_params=pltpu.CompilerParams(vmem_limit_bytes=VMEM_LIMIT),
        cost_estimate=pl.CostEstimate(flops=1 << 31, bytes_accessed=4 << 20, transcendentals=0),
    )(
        late_where,
        facet_rows,
        dual_coeffs,
        pltpu.with_memory_space_constraint(sky_estimate, pltpu.HBM),
        pltpu.with_memory_space_constraint(dirty_image, pltpu.HBM),
        bands,
    )
    (tiles_where,) = after((where,), head)
    spread = call(
        tiles_kernel,
        jax.ShapeDtypeStruct((320, 1536), BF),
        [],
        1 << 23,
        1 << 20,
        tiles_where,
        tile_slots,
        tile_count,
        gram_tiles,
        sampled_table(),
        scalars=3,
    )
    (received,) = after((received,), head)

    scratch = [
        pltpu.VMEM((1280, 128), F32),
        pltpu.VMEM((64, 2048), BF),
        pltpu.VMEM((256, 1024), BF),
        pltpu.VMEM((64, 1024), BF),
        pltpu.VMEM((2, 16, 40, 128), BF),
        pltpu.SemaphoreType.DMA((2,)),
    ]
    weighted = call(
        gram_kernel,
        jax.ShapeDtypeStruct((PEERS_IMG, 40, 128), BF),
        scratch,
        1 << 29,
        1 << 20,
        received,
        spread,
        result=HB,
    )
    returned = lax.all_to_all(weighted, "img", split_axis=0, concat_axis=0, tiled=True)

    head, tail = after((head, tail), weighted)
    steps = [(i, i + 1) for i in range(PEERS_IMG - 1)]
    from_before = lax.ppermute(tail, "img", steps)
    from_after = lax.ppermute(head, "img", [(j, i) for i, j in steps])
    base = call(
        edge_kernel,
        extended,
        [],
        1 << 20,
        4 << 20,
        base,
        from_before,
        from_after,
    )
    blocks = call(
        inverse_kernel,
        jax.ShapeDtypeStruct((8, tile_rows + 16, WIDE), BF),
        [],
        1 << 29,
        1 << 20,
        where,
        returned,
        line,
        base,
        scalars=1,
    )
    halves = lax.all_to_all(blocks, "fou", split_axis=0, concat_axis=0, tiled=True)

    return frames_call(thresholds, where, halves, base, dual_coeffs, bands)


def solution(mesh):
    in_specs = (
        P(None, "img", "fou"),
        P(None, None, "img", "fou"),
        P(None, "img", "fou"),
        P(),
        P(),
        P("img"),
        P(None, "img", None),
        P(None, "img"),
        P(None, "img", None, None, None),
    )
    out_specs = (P(None, "img", "fou"), P(None, None, "img", "fou"))
    return jax.shard_map(body, mesh=mesh, in_specs=in_specs, out_specs=out_specs, check_vma=False)
```

```python
import math

import jax
import jax.numpy as jnp
import numpy as np
from jax import lax
from jax.experimental import pallas as pl
from jax.experimental.pallas import tpu as pltpu
from jax.sharding import PartitionSpec as P

PIXELS = 2048
RADIUS = 8
SLOTS = 6
ROWS = 64
COLS = 256
FRAMES = 8
PEERS_IMG = 32
STEP_PRIMAL = 0.5
STEP_DUAL = 0.5
BF = jnp.bfloat16
F32 = jnp.float32
VMEM_LIMIT = 20 << 20
WIDE = 384
OUTSIDE = -1.0e30
LAST = ((1,), (1,))
FIRST = ((0,), (0,))


def two_terms_np(table):
    high = table.astype(jnp.bfloat16)
    low = (table - high.astype(np.float64)).astype(jnp.bfloat16)
    return high, low


def two_terms(table):
    high = table.astype(BF)
    return high, (table - high.astype(F32)).astype(BF)


def dot(a, b, dims=((1,), (0,))):
    return lax.dot_general(a, b, (dims, ((), ())), preferred_element_type=F32)


def angle_np(a, b, period):
    return 2.0 * np.pi * ((a[:, None] * b[None, :]) % period) / period


def line_table():
    ang = angle_np(np.arange(256), np.arange(256), 256)
    return two_terms_np(np.concatenate([np.cos(ang), np.sin(ang)], axis=1))


def block_table():
    ang = angle_np(np.arange(32), np.arange(32), 32)
    c, s = np.cos(ang), np.sin(ang)
    return two_terms_np(np.block([[c, s], [-s, c]]))


HALO = np.concatenate([np.arange(-8, 0), np.arange(64, 72)])


def turn_table():
    main = np.tile(np.arange(64), 2)
    halo = np.tile(HALO, 8)
    ang = [angle_np(np.arange(64), r, 2048) for r in (main, halo)]
    return two_terms_np(
        np.concatenate([np.cos(ang[0]), np.sin(ang[0]), np.cos(ang[1]), np.sin(ang[1])])
    )


def fixed_table():
    turns = [np.concatenate(np.split(t, 4), axis=1) for t in turn_table()]
    return np.concatenate([*block_table(), *turns], axis=1)


def sampled_table():
    fixed = fixed_table()
    rest = np.zeros((64, 768), fixed.dtype)
    rest[:, 0:384] = fixed[:, 768:1152]
    return np.concatenate([*tile_table(), fixed[:, 0:768], rest], axis=0)


def tile_table():
    t = np.arange(32)
    ang = angle_np(t, np.arange(64), 32)
    c, s = np.cos(ang), np.sin(ang)
    main = np.zeros((32, 2, 2, 2, 2, 64))
    for p in range(2):
        main[:, p, 0, 0, p] = c
        main[:, p, 1, 0, p] = -s
        main[:, p, 0, 1, p] = s
        main[:, p, 1, 1, p] = c
    ang = angle_np(t, HALO, 32)
    c, s = np.cos(ang), np.sin(ang)
    halo = np.zeros((32, 2, 2, 2, 2, 2, 2, 2, 16))
    for p in range(2):
        for x in range(2):
            halo[:, p, 0, x, 0, 0, x, p] = c
            halo[:, p, 1, x, 0, 0, x, p] = -s
            halo[:, p, 0, x, 1, 0, x, p] = s
            halo[:, p, 1, x, 1, 0, x, p] = c
            halo[:, p, 0, x, 0, 1, x, p] = s
            halo[:, p, 1, x, 0, 1, x, p] = c
            halo[:, p, 0, x, 1, 1, x, p] = -c
            halo[:, p, 1, x, 1, 1, x, p] = s
    table = np.concatenate([main.reshape(128, 256), halo.reshape(128, 512)], axis=1)
    return two_terms_np(table)


def wave_table():
    freq = np.arange(2)[:, None] + 2 * np.arange(4)[None]
    pos = np.arange(4 * COLS).reshape(4, COLS)
    ang = 2.0 * np.pi * ((freq[:, :, None, None] * pos) % PIXELS) / PIXELS
    fold = np.concatenate([np.cos(ang), np.sin(ang)], axis=3).reshape(32, 2 * COLS)
    return np.concatenate([np.stack(line_table()), np.stack(two_terms_np(fold))], axis=1)


def fold_rows(line_ref, par):
    at = pl.multiple_of(256 + 16 * par, 16)
    fold = line_ref[0, pl.ds(at, 16), :].astype(F32) + line_ref[1, pl.ds(at, 16), :].astype(F32)
    return fold[:, 0:256], fold[:, 256:512]


def hold_kernel(table_ref, o_ref):
    o_ref[...] = table_ref[...]


def send_kernel(sky_ref, o_ref, taken, rounded, in_sem, out_sem):
    channels = taken.shape[0]

    def fetch(c):
        return pltpu.make_async_copy(sky_ref.at[c], taken.at[c], in_sem.at[c])

    def place(c, h):
        return pltpu.make_async_copy(rounded.at[c], o_ref.at[2 * c + h], out_sem.at[c, h])

    for c in range(channels):
        fetch(c).start()
    for c in range(channels):
        fetch(c).wait()
        rounded[c] = taken[c].astype(BF)
        for h in range(2):
            place(c, h).start()
    for c in range(channels):
        for h in range(2):
            place(c, h).wait()


def forward_kernel(par_ref, x_ref, line_ref, o_ref, out, sem):
    par = par_ref[1]
    folds = fold_rows(line_ref, par)
    sign = (1 - 2 * par).astype(F32)
    xe = [x_ref[f].astype(F32) + sign * x_ref[f + 4].astype(F32) for f in range(4)]
    rows = [[], []]
    for cls in range(4):
        cos = folds[0][cls * 4 : cls * 4 + 4]
        sin = folds[1][cls * 4 : cls * 4 + 4]
        yr = xe[0] * cos[0:1]
        yi = xe[0] * sin[0:1]
        for f in range(1, 4):
            yr = yr + xe[f] * cos[f : f + 1]
            yi = yi + xe[f] * sin[f : f + 1]
        rows[0].append(jnp.concatenate([yr, -yi], axis=1).astype(BF))
        rows[1].append(jnp.concatenate([-yi, -yr], axis=1).astype(BF))
    def leave(part):
        to = o_ref.at[:, pl.ds(part * 16, 16), :]
        return pltpu.make_async_copy(out.at[part], to, sem.at[part])

    for part in range(2):
        r = jnp.concatenate(rows[part], axis=0)
        wave = dot(line_ref[0, 0:256], r, LAST) + dot(line_ref[1, 0:256], r, LAST)
        both = [wave[:, chi * 128 : chi * 128 + 128].reshape(32, 8, 128) for chi in range(2)]
        out[part] = jnp.concatenate(both, axis=1).astype(BF)
        leave(part).start()
    for part in range(2):
        leave(part).wait()


def inverse_kernel(par_ref, t_ref, line_ref, base_ref, o_ref):
    par = par_ref[1]
    folds = fold_rows(line_ref, par)
    me = par_ref[3]
    sign = (1 - 2 * par).astype(F32)
    re = t_ref[:, 0:16, :].astype(F32)
    im = t_ref[:, 16:32, :].astype(F32)
    edge = t_ref[:, 32:40, :].astype(F32)
    data = [re[:, 0:8], im[:, 0:8], re[:, 8:16], im[:, 8:16], edge]
    data = jnp.concatenate([d.reshape(256, 128).astype(BF) for d in data], axis=1)
    wave = dot(data, line_ref[0, 0:256], FIRST) + dot(data, line_ref[1, 0:256], FIRST)

    def joined(a, b):
        return jnp.concatenate([a[:, 0:256] - b[:, 256:512], a[:, 256:512] + b[:, 0:256]], axis=1)

    h = joined(wave[512:576], wave[576:640])
    total = [None] * 4
    for chi in range(2):
        u = joined(wave[chi * 256 : chi * 256 + 128], wave[chi * 256 + 128 : chi * 256 + 256])
        for clo in range(2):
            cls = 2 * chi + clo
            e = h[cls * 16 : cls * 16 + 16]
            whole = jnp.concatenate([e[0:8], u[clo * 64 : clo * 64 + 64], e[8:16]], axis=0)
            ur = whole[:, 0:256]
            ui = whole[:, 256:512]
            cos = folds[0][cls * 4 : cls * 4 + 4]
            sin = folds[1][cls * 4 : cls * 4 + 4]
            for f in range(4):
                g = ur * cos[f : f + 1] - ui * sin[f : f + 1]
                total[f] = g if total[f] is None else total[f] + g
    scale = 1.0 / (PIXELS * PIXELS)
    total = [g * scale for g in total]
    total = total + [sign * g for g in total]
    none = jnp.zeros((80, 128), F32)
    lane = lax.broadcasted_iota(jnp.int32, (80, 128), 1)
    for f in range(8):
        before = total[f - 1][:, 128:256] if f > 0 else none
        after = total[f + 1][:, 0:128] if f < 7 else none
        line = jnp.concatenate([before, total[f], after], axis=1)
        line = pltpu.roll(line, 512 - 120, 1)
        pack = jnp.where(f == me - 1, base_ref[0, :, 256:384], 0.0)
        pack = pack + jnp.where(f == me + 1, base_ref[1, :, 256:384], 0.0)
        o_ref[f, :, 0:256] = line[:, 0:256].astype(BF)
        o_ref[f, :, 256:384] = jnp.where(lane < 16, line[:, 256:384], pack).astype(BF)


def tiles_kernel(where_ref, slots_ref, count_ref, tiles_ref, table_ref, o_ref):
    channel = where_ref[0]
    left = lax.broadcasted_iota(jnp.int32, (32, 128), 0)
    right = lax.broadcasted_iota(jnp.int32, (32, 128), 1)
    tile = jnp.full((32, 128), -1, jnp.int32)
    for k in range(SLOTS):
        slot = jnp.where(k < count_ref[channel, 0], slots_ref[channel, 0, k], -1)
        tile = jnp.where(left // 4 == k, slot, tile)
    pick = (tile == right // 4) & (left % 4 == right % 4)
    pick = jnp.where(pick, 1.0, 0.0).astype(BF)
    o_ref[...] = jnp.zeros_like(o_ref)
    for k in range(0, SLOTS, 2):
        pair = [tiles_ref[channel, 0, k + n].astype(F32).T for n in range(2)]
        o_ref[256:320, k * 64 : k * 64 + 128] = jnp.concatenate(pair, axis=1).astype(BF)
    o_ref[256:320, 384:1152] = table_ref[256:320, :]
    o_ref[256:320, 1152:1536] = table_ref[320:384, 0:384]
    for t in range(2):
        row = dot(pick, table_ref[t * 128 : t * 128 + 128, :]).astype(BF)
        for j in range(2):
            for chi in range(2):
                p = 2 * j + chi
                rows = slice(t * 128 + p * 32, t * 128 + p * 32 + 32)
                o_ref[rows, p * 256 : p * 256 + 256] = row[:, 0:256]
                for comp in range(2):
                    at = 256 + chi * 256 + comp * 128
                    to = 1024 + comp * 256 + j * 128
                    o_ref[rows, to : to + 128] = row[:, at : at + 128]


def gram_kernel(d_ref, e_ref, o_ref, rows, rhs, mid, edge, out, sem):
    rows[0:1024, :] = d_ref[...].reshape(1024, 128).astype(F32)
    for p in range(16):
        lanes = slice(p * 128, p * 128 + 128)
        at = (p % 2) * 8 + p // 2
        rhs[0:32, lanes] = rows[pl.ds(at, 32, stride=32), :].astype(BF)
        rhs[32:64, lanes] = rows[pl.ds(16 + at, 32, stride=32), :].astype(BF)
    fixed = e_ref[256:320, :]
    block = [fixed[:, 384:448], fixed[:, 448:512]]
    turns = fixed[:, 512:1024].astype(F32) + fixed[:, 1024:1536].astype(F32)
    tc, ts, ec, es = (turns[:, n * 128 : n * 128 + 128] for n in range(4))
    first = dot(jnp.concatenate(block, axis=0), rhs[...])
    first = first[0:64] + first[64:128]
    for p in range(16):
        g = first[:, p * 128 : p * 128 + 128]
        gr = jnp.concatenate([g[0:32], g[0:32]], axis=0)
        gi = jnp.concatenate([g[32:64], g[32:64]], axis=0)
        down = slice(p // 4 * 64, p // 4 * 64 + 64)
        at = p % 4 * 256
        mid[down, at : at + 128] = (gr * tc + gi * ts).astype(BF)
        mid[down, at + 128 : at + 256] = (gi * tc - gr * ts).astype(BF)
    spec = dot(mid[...], e_ref[0:256, 0:1024], LAST)
    spec = (spec[:, 0:128] + spec[:, 128:256]).astype(BF)
    spec = jnp.concatenate([spec[g * 64 : g * 64 + 64] for g in range(4)], axis=1)
    tiles = [fixed[:, k * 64 : k * 64 + 64] for k in range(SLOTS)]
    mixed = dot(jnp.concatenate(tiles, axis=0), spec)
    lane_slot = (lax.broadcasted_iota(jnp.int32, (64, 512), 1) % 32) // 4
    weighted = jnp.where(lane_slot == 0, mixed[0:64], 0.0)
    for k in range(1, SLOTS):
        weighted = jnp.where(lane_slot == k, mixed[k * 64 : k * 64 + 64], weighted)
    weighted = weighted.astype(BF)
    w = jnp.concatenate([weighted[:, g * 128 : g * 128 + 128] for g in range(4)], axis=0)
    spreads = dot(jnp.concatenate([w, w], axis=1), e_ref[0:256, :])
    for g in range(4):
        z = spreads[g * 64 : g * 64 + 64]
        for v in range(4):
            p = g * 4 + v
            zr = z[:, v * 256 : v * 256 + 128]
            zi = z[:, v * 256 + 128 : v * 256 + 256]
            hr = zr * tc - zi * ts
            hi = zi * tc + zr * ts
            rhs[0:32, p * 128 : p * 128 + 128] = (hr[0:32] + hr[32:64]).astype(BF)
            rhs[32:64, p * 128 : p * 128 + 128] = (hi[0:32] + hi[32:64]).astype(BF)
        for j in range(2):
            zr = z[:, 1024 + j * 128 : 1152 + j * 128]
            zi = z[:, 1280 + j * 128 : 1408 + j * 128]
            hr = zr * ec - zi * es
            hi = zi * ec + zr * es
            lanes = slice((2 * g + j) * 128, (2 * g + j) * 128 + 128)
            edge[0:32, lanes] = (hr[0:32] + hr[32:64]).astype(BF)
            edge[32:64, lanes] = (hi[0:32] + hi[32:64]).astype(BF)
    block = jnp.concatenate(block, axis=1)
    last = dot(block, rhs[...], FIRST)
    last = last[0:64] + last[64:128]
    outer = dot(block, edge[...], FIRST)
    outer = outer[0:32] + outer[64:96]
    for p in range(16):
        lanes = slice(p * 128, p * 128 + 128)
        at = (p % 2) * 8 + p // 2
        rows[pl.ds(at, 32, stride=40), :] = last[0:32, lanes]
        rows[pl.ds(16 + at, 32, stride=40), :] = last[32:64, lanes]
    for v in range(8):
        rows[pl.ds(32 + v, 32, stride=40), :] = outer[:, v * 128 : v * 128 + 128]
    leave = []
    for n in range(2):
        half = rows[n * 640 : n * 640 + 640, :]
        out[n] = half.reshape(16, 40, 128).astype(BF)
        to = o_ref.at[pl.ds(n * 16, 16)]
        leave.append(pltpu.make_async_copy(out.at[n], to, sem.at[n]))
        leave[n].start()
    for n in range(2):
        leave[n].wait()


def bands_kernel(taps_ref, o_ref):
    lane = lax.broadcasted_iota(jnp.int32, (64, 256), 1)
    for k in range(FRAMES):
        wide = jnp.broadcast_to(taps_ref[k : k + 1, :], (128, 256))
        band = pltpu.roll(wide, 0, 1, stride=1, stride_axis=0)
        high = band.astype(BF)
        low = band - high.astype(F32)
        o_ref[k * 128 : k * 128 + 128, :] = high
        o_ref[1024 + k * 128 : 1152 + k * 128, :] = low.astype(BF)
        low = jnp.where(lane < 80, low[0:64], 0.0)
        high = jnp.where(lane < 80, high[0:64].astype(F32), 0.0)
        row = high + pltpu.roll(high, 80, 1) + pltpu.roll(low, 160, 1)
        o_ref[2048 + k * 64 : 2112 + k * 64, :] = row.astype(BF)


def synth_kernel(
    where_ref,
    live_ref,
    dual_ref,
    sky_hbm,
    dirty_hbm,
    bands_ref,
    o_ref,
    head_ref,
    tail_ref,
    sky_ref,
    dirty_ref,
    across,
    sky_sem,
    dirty_sem,
):
    channels = sky_ref.shape[0]
    sky_copy = pltpu.make_async_copy(sky_hbm, sky_ref, sky_sem)
    sky_copy.start()
    dirty_copy = pltpu.make_async_copy(dirty_hbm, dirty_ref, dirty_sem)
    dirty_copy.start()
    row = lax.broadcasted_iota(jnp.int32, (80, WIDE), 0) + where_ref[2] * ROWS - RADIUS
    lane = lax.broadcasted_iota(jnp.int32, (80, WIDE), 1)
    col = lane + where_ref[3] * COLS - RADIUS
    inside = (row >= 0) & (row < PIXELS) & (col >= 0) & (col < PIXELS)
    for k in range(FRAMES):
        p = dual_ref[:, k + 1].reshape(channels * ROWS, COLS)
        both = jnp.concatenate([p[:, 0:128], p[:, 128:256]], axis=0)
        both = jnp.concatenate([both, both], axis=1)
        at = k * 128
        band = jnp.concatenate(
            [bands_ref[at : at + 128, :], bands_ref[1024 + at : 1152 + at, :]], axis=0
        )
        a = dot(both, band)
        a0 = a[0 : channels * ROWS]
        a1 = a[channels * ROWS :]
        out = jnp.concatenate([a0[:, 0:128], a0[:, 128:256] + a1[:, 0:128], a1[:, 128:256]], axis=1)
        for c in range(channels):
            across[c, k * ROWS : (k + 1) * ROWS, :] = out[c * ROWS : (c + 1) * ROWS].astype(BF)
    sky_copy.wait()
    dirty_copy.wait()
    live = lax.broadcasted_iota(jnp.int32, (ROWS, COLS), 0) < live_ref[0]
    none = jnp.zeros((ROWS, 128), F32)
    edge = jnp.zeros((8, WIDE), F32)
    for c in range(channels):
        total = dot(bands_ref[2048:2560, :], across[c], FIRST)
        total = total[0:80] + total[160:240]
        sky = sky_ref[c]
        own = sky + STEP_PRIMAL * dirty_ref[c] - STEP_PRIMAL * dual_ref[c, 0].astype(F32)
        own = jnp.where(live, own, OUTSIDE)
        own = pltpu.roll(jnp.concatenate([own, none], axis=1), 8, 1)
        sky = pltpu.roll(jnp.concatenate([sky, none], axis=1), 8, 1)
        total = total * (-STEP_PRIMAL)
        total = total + jnp.concatenate([edge, own, edge], axis=0)
        total = jnp.where(inside, total, OUTSIDE)
        total = jnp.where(lane < COLS + 2 * RADIUS, total, 0.0)
        sky = jnp.concatenate([edge, sky, edge], axis=0)
        for at, cells in ((c, total), (channels + c, sky)):
            o_ref[at] = cells
            head_ref[at] = cells[0:16].astype(BF)
            tail_ref[at] = cells[64:80].astype(BF)


def edge_kernel(base_ref, before_ref, after_ref, o_ref):
    both = base_ref.shape[0]
    lane = lax.broadcasted_iota(jnp.int32, (80, 128), 1)
    head = jnp.zeros((80, 128), F32)
    tail = jnp.zeros((80, 128), F32)
    for c in range(both):
        o_ref[c, 0:16] = base_ref[c, 0:16] + before_ref[c].astype(F32)
        o_ref[c, 16:64] = base_ref[c, 16:64]
        o_ref[c, 64:80] = base_ref[c, 64:80] + after_ref[c].astype(F32)
        first = o_ref[c, :, 0:128]
        final = o_ref[c, :, 256:384]
        if c < both // 2:
            at = 16 + 16 * c
            head = head + pltpu.roll(jnp.where(lane < 16, first, 0.0), at, 1)
            tail = tail + pltpu.roll(jnp.where(lane < 16, final, 0.0), at, 1)
        else:
            at = 80 + 8 * (c - both // 2)
            head = head + pltpu.roll(jnp.where((lane >= 8) & (lane < 16), first, 0.0), at - 8, 1)
            tail = tail + pltpu.roll(jnp.where(lane < 8, final, 0.0), at, 1)
    o_ref[0, :, 256:384] = o_ref[0, :, 256:384] + head
    o_ref[1, :, 256:384] = o_ref[1, :, 256:384] + tail


def frames_kernel(
    bound_ref,
    where_ref,
    half_ref,
    base_ref,
    dual_ref,
    bands_ref,
    image_ref,
    o_ref,
    image_buf,
    dual_buf,
    probes,
    wide,
    down,
    image_sem,
    dual_sem,
):
    channels = image_buf.shape[0]
    rows = channels * ROWS

    def dual_copy(k):
        return pltpu.make_async_copy(dual_buf.at[k], o_ref.at[:, k], dual_sem.at[k])

    def finish(k, analysis):
        bound = bound_ref[k]
        cand = [dual_ref[c, k].astype(F32) + STEP_DUAL * analysis(c) for c in range(channels)]
        square = cand[0] * cand[0]
        for c in range(1, channels):
            square = square + cand[c] * cand[c]
        factor = bound * lax.rsqrt(jnp.maximum(square, bound * bound))
        for c in range(channels):
            dual_buf[k, c] = (cand[c] * factor).astype(BF)
        dual_copy(k).start()

    wide[...] = jnp.zeros_like(wide)
    me = where_ref[3]
    last = half_ref.shape[0] - 1
    lane = lax.broadcasted_iota(jnp.int32, (80, 128), 1)
    left = half_ref[jnp.maximum(me - 1, 0), :, 256:384].astype(F32)
    left = jnp.where(me > 0, left, 0.0)
    right = half_ref[jnp.minimum(me + 1, last), :, 256:384].astype(F32)
    right = jnp.where(me < last, right, 0.0)
    for c in range(channels):
        gram = half_ref[2 * c].astype(F32) + half_ref[2 * c + 1].astype(F32)
        gram = [gram[:, 0:128], gram[:, 128:256], jnp.where(lane < 16, gram[:, 256:384], 0.0)]
        base = [base_ref[c, :, b * 128 : b * 128 + 128] for b in range(3)]
        sky = [base_ref[channels + c, :, b * 128 : b * 128 + 128] for b in range(3)]
        base[2] = jnp.where(lane < 16, base[2], 0.0)
        at = 16 + 16 * c
        base[0] = base[0] + jnp.where(lane < 16, pltpu.roll(left, 128 - at, 1), 0.0)
        base[2] = base[2] + jnp.where(lane < 16, pltpu.roll(right, 128 - at, 1), 0.0)
        at = 80 + 8 * c
        sky[0] = sky[0] + jnp.where(lane < 8, pltpu.roll(left, 128 - at, 1), 0.0)
        shown = (lane >= 8) & (lane < 16)
        sky[2] = sky[2] + jnp.where(shown, pltpu.roll(right, 136 - at, 1), 0.0)
        image = [jnp.maximum(base[b] - STEP_PRIMAL * gram[b], 0.0) for b in range(3)]
        probe = jnp.concatenate([2.0 * image[b] - sky[b] for b in range(3)], axis=1)
        image = pltpu.roll(jnp.concatenate(image, axis=1), WIDE - 8, 1)
        image_buf[c] = image[8:72, 0:256]
        probes[c] = pltpu.roll(probe, WIDE - 8, 1)[8:72, 0:256]
        high = probe.astype(BF)
        low = (probe - high.astype(F32)).astype(BF)
        wide[0:80, :] = high
        wide[80:160, :] = low
        wide[160:240, :] = high
        d = dot(bands_ref[2048:2560, :], wide[...])
        high = d.astype(BF)
        down[0, c] = high
        down[1, c] = (d - high.astype(F32)).astype(BF)
    image_copy = pltpu.make_async_copy(image_buf, image_ref, image_sem)
    image_copy.start()
    finish(0, lambda c: probes[c])
    for k in range(1, FRAMES + 1):
        at = (k - 1) * ROWS
        a = None
        for t in range(2):
            d = jnp.concatenate([down[t, c, at : at + ROWS, :] for c in range(channels)], axis=0)
            both = jnp.concatenate([d[:, 0:256], d[:, 128:384]], axis=0)
            high = bands_ref[(k - 1) * 128 : k * 128, :]
            if t == 0:
                band = jnp.concatenate([high, bands_ref[896 + k * 128 : 1024 + k * 128, :]], axis=0)
                term = dot(both, band, LAST)
                a = term[:, 0:128] + term[:, 128:256]
            else:
                a = a + dot(both, high, LAST)
        finish(
            k,
            lambda c: jnp.concatenate(
                [a[c * ROWS : c * ROWS + ROWS], a[rows + c * ROWS : rows + c * ROWS + ROWS]], axis=1
            ),
        )
    image_copy.wait()
    for k in range(FRAMES + 1):
        dual_copy(k).wait()


VM = pl.BlockSpec(memory_space=pltpu.VMEM)
SM = pl.BlockSpec(memory_space=pltpu.SMEM)
HB = pl.BlockSpec(memory_space=pltpu.HBM)


def call(kernel, out_shape, scratch, flops, moved, *args, scalars=0, result=VM):
    return pl.pallas_call(
        kernel,
        out_shape=out_shape,
        in_specs=[SM] * scalars + [VM] * (len(args) - scalars),
        out_specs=jax.tree.map(lambda _: result, out_shape),
        scratch_shapes=scratch,
        compiler_params=pltpu.CompilerParams(vmem_limit_bytes=VMEM_LIMIT),
        cost_estimate=pl.CostEstimate(flops=flops, bytes_accessed=moved, transcendentals=0),
    )(*args)


def frames_call(thresholds, where, halves, base, dual, bands):
    channels = dual.shape[0]
    block = (channels, ROWS, COLS)
    return pl.pallas_call(
        frames_kernel,
        out_shape=(jax.ShapeDtypeStruct(block, F32), jax.ShapeDtypeStruct(dual.shape, BF)),
        in_specs=[SM, SM, VM, VM, VM, VM],
        out_specs=(pl.BlockSpec(memory_space=pl.ANY), pl.BlockSpec(memory_space=pl.ANY)),
        scratch_shapes=[
            pltpu.VMEM(block, F32),
            pltpu.VMEM((FRAMES + 1, *block), BF),
            pltpu.VMEM(block, F32),
            pltpu.VMEM((256, WIDE), BF),
            pltpu.VMEM((2, channels, FRAMES * ROWS, WIDE), BF),
            pltpu.SemaphoreType.DMA(()),
            pltpu.SemaphoreType.DMA((FRAMES + 1,)),
        ],
        compiler_params=pltpu.CompilerParams(vmem_limit_bytes=VMEM_LIMIT),
        cost_estimate=pl.CostEstimate(flops=1 << 31, bytes_accessed=3 << 20, transcendentals=0),
    )(thresholds, where, halves, base, dual, bands)


def after(values, *events):
    return lax.optimization_barrier((*values, *events))[: len(values)]


def body(
    sky_estimate,
    dual_coeffs,
    dirty_image,
    filters,
    thresholds,
    facet_rows,
    tile_slots,
    tile_count,
    gram_tiles,
):
    channels, tile_rows, tile_cols = sky_estimate.shape
    place = lax.axis_index("fou")
    where = jnp.stack([place >> 1, place & 1, lax.axis_index("img"), place]).astype(jnp.int32)

    sent = pl.pallas_call(
        send_kernel,
        out_shape=jax.ShapeDtypeStruct((2 * channels, tile_rows, tile_cols), BF),
        in_specs=[pl.BlockSpec(memory_space=pltpu.HBM)],
        out_specs=pl.BlockSpec(memory_space=pltpu.HBM),
        scratch_shapes=[
            pltpu.VMEM(sky_estimate.shape, F32),
            pltpu.VMEM(sky_estimate.shape, BF),
            pltpu.SemaphoreType.DMA((channels,)),
            pltpu.SemaphoreType.DMA((channels, 2)),
        ],
        compiler_params=pltpu.CompilerParams(vmem_limit_bytes=VMEM_LIMIT),
    )(pltpu.with_memory_space_constraint(sky_estimate, pltpu.HBM))
    lines = lax.all_to_all(sent, "fou", split_axis=0, concat_axis=0, tiled=True)

    taps = jnp.pad(filters, ((0, 0), (0, 256 - filters.shape[1])))
    bands = call(
        bands_kernel, jax.ShapeDtypeStruct((2560, 256), BF), [], 1 << 20, 1 << 20, taps
    )
    (ready_where,) = after((where,), bands)
    line = wave_table()
    held = call(hold_kernel, jax.ShapeDtypeStruct(line.shape, BF), [], 1 << 10, 1 << 20, line)
    packed = call(
        forward_kernel,
        jax.ShapeDtypeStruct((PEERS_IMG, 32, 128), BF),
        [pltpu.VMEM((2, PEERS_IMG, 16, 128), BF), pltpu.SemaphoreType.DMA((2,))],
        1 << 29,
        1 << 20,
        ready_where,
        lines,
        held,
        scalars=1,
        result=HB,
    )
    received = lax.all_to_all(packed, "img", split_axis=0, concat_axis=0, tiled=True)


    ends = jax.ShapeDtypeStruct((2 * channels, 16, WIDE), BF)
    extended = jax.ShapeDtypeStruct((2 * channels, tile_rows + 16, WIDE), F32)
    (late_where,) = after((where,), packed)
    base, head, tail = pl.pallas_call(
        synth_kernel,
        out_shape=(extended, ends, ends),
        in_specs=[SM, SM, VM, HB, HB, VM],
        out_specs=(VM, VM, VM),
        scratch_shapes=[
            pltpu.VMEM(sky_estimate.shape, F32),
            pltpu.VMEM(sky_estimate.shape, F32),
            pltpu.VMEM((channels, FRAMES * ROWS, WIDE), BF),
            pltpu.SemaphoreType.DMA(()),
            pltpu.SemaphoreType.DMA(()),
        ],
        compiler_params=pltpu.CompilerParams(vmem_limit_bytes=VMEM_LIMIT),
        cost_estimate=pl.CostEstimate(flops=1 << 31, bytes_accessed=4 << 20, transcendentals=0),
    )(
        late_where,
        facet_rows,
        dual_coeffs,
        pltpu.with_memory_space_constraint(sky_estimate, pltpu.HBM),
        pltpu.with_memory_space_constraint(dirty_image, pltpu.HBM),
        bands,
    )
    (tiles_where,) = after((where,), head)
    spread = call(
        tiles_kernel,
        jax.ShapeDtypeStruct((320, 1536), BF),
        [],
        1 << 23,
        1 << 20,
        tiles_where,
        tile_slots,
        tile_count,
        gram_tiles,
        sampled_table(),
        scalars=3,
    )
    (received,) = after((received,), head)

    scratch = [
        pltpu.VMEM((1280, 128), F32),
        pltpu.VMEM((64, 2048), BF),
        pltpu.VMEM((256, 1024), BF),
        pltpu.VMEM((64, 1024), BF),
        pltpu.VMEM((2, 16, 40, 128), BF),
        pltpu.SemaphoreType.DMA((2,)),
    ]
    weighted = call(
        gram_kernel,
        jax.ShapeDtypeStruct((PEERS_IMG, 40, 128), BF),
        scratch,
        1 << 29,
        1 << 20,
        received,
        spread,
        result=HB,
    )
    returned = lax.all_to_all(weighted, "img", split_axis=0, concat_axis=0, tiled=True)

    (late_taps,) = after((taps,), weighted)
    late_bands = call(
        bands_kernel, jax.ShapeDtypeStruct((2560, 256), BF), [], 1 << 20, 1 << 20, late_taps
    )
    (last_where,) = after((where,), late_bands)
    head, tail = after((head, tail), weighted)
    steps = [(i, i + 1) for i in range(PEERS_IMG - 1)]
    from_before = lax.ppermute(tail, "img", steps)
    from_after = lax.ppermute(head, "img", [(j, i) for i, j in steps])
    base = call(
        edge_kernel,
        extended,
        [],
        1 << 20,
        4 << 20,
        base,
        from_before,
        from_after,
    )
    blocks = call(
        inverse_kernel,
        jax.ShapeDtypeStruct((8, tile_rows + 16, WIDE), BF),
        [],
        1 << 29,
        1 << 20,
        last_where,
        returned,
        line,
        base,
        scalars=1,
    )
    halves = lax.all_to_all(blocks, "fou", split_axis=0, concat_axis=0, tiled=True)

    return frames_call(thresholds, where, halves, base, dual_coeffs, late_bands)


def solution(mesh):
    in_specs = (
        P(None, "img", "fou"),
        P(None, None, "img", "fou"),
        P(None, "img", "fou"),
        P(),
        P(),
        P("img"),
        P(None, "img", None),
        P(None, "img"),
        P(None, "img", None, None, None),
    )
    out_specs = (P(None, "img", "fou"), P(None, None, "img", "fou"))
    return jax.shard_map(body, mesh=mesh, in_specs=in_specs, out_specs=out_specs, check_vma=False)
```

```python
import math

import jax
import jax.numpy as jnp
import numpy as np
from jax import lax
from jax.experimental import pallas as pl
from jax.experimental.pallas import tpu as pltpu
from jax.sharding import PartitionSpec as P

PIXELS = 2048
RADIUS = 8
SLOTS = 6
ROWS = 64
COLS = 256
FRAMES = 8
PEERS_IMG = 32
STEP_PRIMAL = 0.5
STEP_DUAL = 0.5
BF = jnp.bfloat16
F32 = jnp.float32
VMEM_LIMIT = 20 << 20
WIDE = 384
OUTSIDE = -1.0e30
LAST = ((1,), (1,))
FIRST = ((0,), (0,))


def two_terms_np(table):
    high = table.astype(jnp.bfloat16)
    low = (table - high.astype(np.float64)).astype(jnp.bfloat16)
    return high, low


def two_terms(table):
    high = table.astype(BF)
    return high, (table - high.astype(F32)).astype(BF)


def dot(a, b, dims=((1,), (0,))):
    return lax.dot_general(a, b, (dims, ((), ())), preferred_element_type=F32)


def angle_np(a, b, period):
    return 2.0 * np.pi * ((a[:, None] * b[None, :]) % period) / period


def line_table():
    ang = angle_np(np.arange(256), np.arange(256), 256)
    return two_terms_np(np.concatenate([np.cos(ang), np.sin(ang)], axis=1))


def block_table():
    ang = angle_np(np.arange(32), np.arange(32), 32)
    c, s = np.cos(ang), np.sin(ang)
    return two_terms_np(np.block([[c, s], [-s, c]]))


HALO = np.concatenate([np.arange(-8, 0), np.arange(64, 72)])


def turn_table():
    main = np.tile(np.arange(64), 2)
    halo = np.tile(HALO, 8)
    ang = [angle_np(np.arange(64), r, 2048) for r in (main, halo)]
    return two_terms_np(
        np.concatenate([np.cos(ang[0]), np.sin(ang[0]), np.cos(ang[1]), np.sin(ang[1])])
    )


def fixed_table():
    turns = [np.concatenate(np.split(t, 4), axis=1) for t in turn_table()]
    return np.concatenate([*block_table(), *turns], axis=1)


def sampled_table():
    fixed = fixed_table()
    rest = np.zeros((64, 768), fixed.dtype)
    rest[:, 0:384] = fixed[:, 768:1152]
    return np.concatenate([*tile_table(), fixed[:, 0:768], rest], axis=0)


def tile_table():
    t = np.arange(32)
    ang = angle_np(t, np.arange(64), 32)
    c, s = np.cos(ang), np.sin(ang)
    main = np.zeros((32, 2, 2, 2, 2, 64))
    for p in range(2):
        main[:, p, 0, 0, p] = c
        main[:, p, 1, 0, p] = -s
        main[:, p, 0, 1, p] = s
        main[:, p, 1, 1, p] = c
    ang = angle_np(t, HALO, 32)
    c, s = np.cos(ang), np.sin(ang)
    halo = np.zeros((32, 2, 2, 2, 2, 2, 2, 2, 16))
    for p in range(2):
        for x in range(2):
            halo[:, p, 0, x, 0, 0, x, p] = c
            halo[:, p, 1, x, 0, 0, x, p] = -s
            halo[:, p, 0, x, 1, 0, x, p] = s
            halo[:, p, 1, x, 1, 0, x, p] = c
            halo[:, p, 0, x, 0, 1, x, p] = s
            halo[:, p, 1, x, 0, 1, x, p] = c
            halo[:, p, 0, x, 1, 1, x, p] = -c
            halo[:, p, 1, x, 1, 1, x, p] = s
    table = np.concatenate([main.reshape(128, 256), halo.reshape(128, 512)], axis=1)
    return two_terms_np(table)


def wave_table():
    freq = np.arange(2)[:, None] + 2 * np.arange(4)[None]
    pos = np.arange(4 * COLS).reshape(4, COLS)
    ang = 2.0 * np.pi * ((freq[:, :, None, None] * pos) % PIXELS) / PIXELS
    fold = np.concatenate([np.cos(ang), np.sin(ang)], axis=3).reshape(32, 2 * COLS)
    return np.concatenate([np.stack(line_table()), np.stack(two_terms_np(fold))], axis=1)


def fold_rows(line_ref, par):
    at = pl.multiple_of(256 + 16 * par, 16)
    fold = line_ref[0, pl.ds(at, 16), :].astype(F32) + line_ref[1, pl.ds(at, 16), :].astype(F32)
    return fold[:, 0:256], fold[:, 256:512]


def hold_kernel(table_ref, o_ref):
    o_ref[...] = table_ref[...]


def send_kernel(sky_ref, o_ref, taken, rounded, in_sem, out_sem):
    channels = taken.shape[0]

    def fetch(c):
        return pltpu.make_async_copy(sky_ref.at[c], taken.at[c], in_sem.at[c])

    def place(c, h):
        return pltpu.make_async_copy(rounded.at[c], o_ref.at[2 * c + h], out_sem.at[c, h])

    for c in range(channels):
        fetch(c).start()
    for c in range(channels):
        fetch(c).wait()
        rounded[c] = taken[c].astype(BF)
        for h in range(2):
            place(c, h).start()
    for c in range(channels):
        for h in range(2):
            place(c, h).wait()


def forward_kernel(par_ref, x_ref, line_ref, o_ref, out, sem):
    par = par_ref[1]
    folds = fold_rows(line_ref, par)
    sign = (1 - 2 * par).astype(F32)
    xe = [x_ref[f].astype(F32) + sign * x_ref[f + 4].astype(F32) for f in range(4)]
    rows = [[], []]
    for cls in range(4):
        cos = folds[0][cls * 4 : cls * 4 + 4]
        sin = folds[1][cls * 4 : cls * 4 + 4]
        yr = xe[0] * cos[0:1]
        yi = xe[0] * sin[0:1]
        for f in range(1, 4):
            yr = yr + xe[f] * cos[f : f + 1]
            yi = yi + xe[f] * sin[f : f + 1]
        rows[0].append(jnp.concatenate([yr, -yi], axis=1).astype(BF))
        rows[1].append(jnp.concatenate([-yi, -yr], axis=1).astype(BF))
    def leave(part):
        to = o_ref.at[:, pl.ds(part * 16, 16), :]
        return pltpu.make_async_copy(out.at[part], to, sem.at[part])

    for part in range(2):
        r = jnp.concatenate(rows[part], axis=0)
        wave = dot(line_ref[0, 0:256], r, LAST) + dot(line_ref[1, 0:256], r, LAST)
        both = [wave[:, chi * 128 : chi * 128 + 128].reshape(32, 8, 128) for chi in range(2)]
        out[part] = jnp.concatenate(both, axis=1).astype(BF)
        leave(part).start()
    for part in range(2):
        leave(part).wait()


def inverse_kernel(par_ref, t_ref, line_ref, base_ref, o_ref):
    par = par_ref[1]
    folds = fold_rows(line_ref, par)
    me = par_ref[3]
    sign = (1 - 2 * par).astype(F32)
    re = t_ref[:, 0:16, :].astype(F32)
    im = t_ref[:, 16:32, :].astype(F32)
    edge = t_ref[:, 32:40, :].astype(F32)
    data = [re[:, 0:8], im[:, 0:8], re[:, 8:16], im[:, 8:16], edge]
    data = jnp.concatenate([d.reshape(256, 128).astype(BF) for d in data], axis=1)
    wave = dot(data, line_ref[0, 0:256], FIRST) + dot(data, line_ref[1, 0:256], FIRST)

    def joined(a, b):
        return jnp.concatenate([a[:, 0:256] - b[:, 256:512], a[:, 256:512] + b[:, 0:256]], axis=1)

    h = joined(wave[512:576], wave[576:640])
    total = [None] * 4
    for chi in range(2):
        u = joined(wave[chi * 256 : chi * 256 + 128], wave[chi * 256 + 128 : chi * 256 + 256])
        for clo in range(2):
            cls = 2 * chi + clo
            e = h[cls * 16 : cls * 16 + 16]
            whole = jnp.concatenate([e[0:8], u[clo * 64 : clo * 64 + 64], e[8:16]], axis=0)
            ur = whole[:, 0:256]
            ui = whole[:, 256:512]
            cos = folds[0][cls * 4 : cls * 4 + 4]
            sin = folds[1][cls * 4 : cls * 4 + 4]
            for f in range(4):
                g = ur * cos[f : f + 1] - ui * sin[f : f + 1]
                total[f] = g if total[f] is None else total[f] + g
    scale = 1.0 / (PIXELS * PIXELS)
    total = [g * scale for g in total]
    total = total + [sign * g for g in total]
    none = jnp.zeros((80, 128), F32)
    lane = lax.broadcasted_iota(jnp.int32, (80, 128), 1)
    for f in range(8):
        before = total[f - 1][:, 128:256] if f > 0 else none
        after = total[f + 1][:, 0:128] if f < 7 else none
        line = jnp.concatenate([before, total[f], after], axis=1)
        line = pltpu.roll(line, 512 - 120, 1)
        pack = jnp.where(f == me - 1, base_ref[0, :, 256:384], 0.0)
        pack = pack + jnp.where(f == me + 1, base_ref[1, :, 256:384], 0.0)
        o_ref[f, :, 0:256] = line[:, 0:256].astype(BF)
        o_ref[f, :, 256:384] = jnp.where(lane < 16, line[:, 256:384], pack).astype(BF)


def tiles_kernel(where_ref, slots_ref, count_ref, tiles_ref, table_ref, o_ref):
    channel = where_ref[0]
    left = lax.broadcasted_iota(jnp.int32, (32, 128), 0)
    right = lax.broadcasted_iota(jnp.int32, (32, 128), 1)
    tile = jnp.full((32, 128), -1, jnp.int32)
    for k in range(SLOTS):
        slot = jnp.where(k < count_ref[channel, 0], slots_ref[channel, 0, k], -1)
        tile = jnp.where(left // 4 == k, slot, tile)
    pick = (tile == right // 4) & (left % 4 == right % 4)
    pick = jnp.where(pick, 1.0, 0.0).astype(BF)
    o_ref[...] = jnp.zeros_like(o_ref)
    for k in range(0, SLOTS, 2):
        pair = [tiles_ref[channel, 0, k + n].astype(F32).T for n in range(2)]
        o_ref[256:320, k * 64 : k * 64 + 128] = jnp.concatenate(pair, axis=1).astype(BF)
    o_ref[256:320, 384:1152] = table_ref[256:320, :]
    o_ref[256:320, 1152:1536] = table_ref[320:384, 0:384]
    for t in range(2):
        row = dot(pick, table_ref[t * 128 : t * 128 + 128, :]).astype(BF)
        for j in range(2):
            for chi in range(2):
                p = 2 * j + chi
                rows = slice(t * 128 + p * 32, t * 128 + p * 32 + 32)
                o_ref[rows, p * 256 : p * 256 + 256] = row[:, 0:256]
                for comp in range(2):
                    at = 256 + chi * 256 + comp * 128
                    to = 1024 + comp * 256 + j * 128
                    o_ref[rows, to : to + 128] = row[:, at : at + 128]


def gram_kernel(d_hbm, e_ref, o_ref, taken, rows, rhs, mid, edge, out, in_sem, sem):
    fetch = [
        pltpu.make_async_copy(d_hbm.at[pl.ds(n * 8, 8)], taken.at[n], in_sem.at[n]) for n in range(4)
    ]
    for move in fetch:
        move.start()
    for n in range(4):
        fetch[n].wait()
        rows[n * 256 : n * 256 + 256, :] = taken[n].reshape(256, 128).astype(F32)
    for p in range(16):
        lanes = slice(p * 128, p * 128 + 128)
        at = (p % 2) * 8 + p // 2
        rhs[0:32, lanes] = rows[pl.ds(at, 32, stride=32), :].astype(BF)
        rhs[32:64, lanes] = rows[pl.ds(16 + at, 32, stride=32), :].astype(BF)
    fixed = e_ref[256:320, :]
    block = [fixed[:, 384:448], fixed[:, 448:512]]
    turns = fixed[:, 512:1024].astype(F32) + fixed[:, 1024:1536].astype(F32)
    tc, ts, ec, es = (turns[:, n * 128 : n * 128 + 128] for n in range(4))
    first = dot(jnp.concatenate(block, axis=0), rhs[...])
    first = first[0:64] + first[64:128]
    for p in range(16):
        g = first[:, p * 128 : p * 128 + 128]
        gr = jnp.concatenate([g[0:32], g[0:32]], axis=0)
        gi = jnp.concatenate([g[32:64], g[32:64]], axis=0)
        down = slice(p // 4 * 64, p // 4 * 64 + 64)
        at = p % 4 * 256
        mid[down, at : at + 128] = (gr * tc + gi * ts).astype(BF)
        mid[down, at + 128 : at + 256] = (gi * tc - gr * ts).astype(BF)
    spec = dot(mid[...], e_ref[0:256, 0:1024], LAST)
    spec = (spec[:, 0:128] + spec[:, 128:256]).astype(BF)
    spec = jnp.concatenate([spec[g * 64 : g * 64 + 64] for g in range(4)], axis=1)
    tiles = [fixed[:, k * 64 : k * 64 + 64] for k in range(SLOTS)]
    mixed = dot(jnp.concatenate(tiles, axis=0), spec)
    lane_slot = (lax.broadcasted_iota(jnp.int32, (64, 512), 1) % 32) // 4
    weighted = jnp.where(lane_slot == 0, mixed[0:64], 0.0)
    for k in range(1, SLOTS):
        weighted = jnp.where(lane_slot == k, mixed[k * 64 : k * 64 + 64], weighted)
    weighted = weighted.astype(BF)
    w = jnp.concatenate([weighted[:, g * 128 : g * 128 + 128] for g in range(4)], axis=0)
    spreads = dot(jnp.concatenate([w, w], axis=1), e_ref[0:256, :])
    for g in range(4):
        z = spreads[g * 64 : g * 64 + 64]
        for v in range(4):
            p = g * 4 + v
            zr = z[:, v * 256 : v * 256 + 128]
            zi = z[:, v * 256 + 128 : v * 256 + 256]
            hr = zr * tc - zi * ts
            hi = zi * tc + zr * ts
            rhs[0:32, p * 128 : p * 128 + 128] = (hr[0:32] + hr[32:64]).astype(BF)
            rhs[32:64, p * 128 : p * 128 + 128] = (hi[0:32] + hi[32:64]).astype(BF)
        for j in range(2):
            zr = z[:, 1024 + j * 128 : 1152 + j * 128]
            zi = z[:, 1280 + j * 128 : 1408 + j * 128]
            hr = zr * ec - zi * es
            hi = zi * ec + zr * es
            lanes = slice((2 * g + j) * 128, (2 * g + j) * 128 + 128)
            edge[0:32, lanes] = (hr[0:32] + hr[32:64]).astype(BF)
            edge[32:64, lanes] = (hi[0:32] + hi[32:64]).astype(BF)
    block = jnp.concatenate(block, axis=1)
    last = dot(block, rhs[...], FIRST)
    last = last[0:64] + last[64:128]
    outer = dot(block, edge[...], FIRST)
    outer = outer[0:32] + outer[64:96]
    for p in range(16):
        lanes = slice(p * 128, p * 128 + 128)
        at = (p % 2) * 8 + p // 2
        rows[pl.ds(at, 32, stride=40), :] = last[0:32, lanes]
        rows[pl.ds(16 + at, 32, stride=40), :] = last[32:64, lanes]
    for v in range(8):
        rows[pl.ds(32 + v, 32, stride=40), :] = outer[:, v * 128 : v * 128 + 128]
    leave = []
    for n in range(2):
        half = rows[n * 640 : n * 640 + 640, :]
        out[n] = half.reshape(16, 40, 128).astype(BF)
        to = o_ref.at[pl.ds(n * 16, 16)]
        leave.append(pltpu.make_async_copy(out.at[n], to, sem.at[n]))
        leave[n].start()
    for n in range(2):
        leave[n].wait()


def bands_kernel(taps_ref, o_ref):
    lane = lax.broadcasted_iota(jnp.int32, (64, 256), 1)
    for k in range(FRAMES):
        wide = jnp.broadcast_to(taps_ref[k : k + 1, :], (128, 256))
        band = pltpu.roll(wide, 0, 1, stride=1, stride_axis=0)
        high = band.astype(BF)
        low = band - high.astype(F32)
        o_ref[k * 128 : k * 128 + 128, :] = high
        o_ref[1024 + k * 128 : 1152 + k * 128, :] = low.astype(BF)
        low = jnp.where(lane < 80, low[0:64], 0.0)
        high = jnp.where(lane < 80, high[0:64].astype(F32), 0.0)
        row = high + pltpu.roll(high, 80, 1) + pltpu.roll(low, 160, 1)
        o_ref[2048 + k * 64 : 2112 + k * 64, :] = row.astype(BF)


def synth_kernel(
    where_ref,
    live_ref,
    dual_ref,
    sky_hbm,
    dirty_hbm,
    bands_ref,
    o_ref,
    head_ref,
    tail_ref,
    sky_ref,
    dirty_ref,
    across,
    sky_sem,
    dirty_sem,
):
    channels = sky_ref.shape[0]
    sky_copy = pltpu.make_async_copy(sky_hbm, sky_ref, sky_sem)
    sky_copy.start()
    dirty_copy = pltpu.make_async_copy(dirty_hbm, dirty_ref, dirty_sem)
    dirty_copy.start()
    row = lax.broadcasted_iota(jnp.int32, (80, WIDE), 0) + where_ref[2] * ROWS - RADIUS
    lane = lax.broadcasted_iota(jnp.int32, (80, WIDE), 1)
    col = lane + where_ref[3] * COLS - RADIUS
    inside = (row >= 0) & (row < PIXELS) & (col >= 0) & (col < PIXELS)
    for k in range(FRAMES):
        p = dual_ref[:, k + 1].reshape(channels * ROWS, COLS)
        both = jnp.concatenate([p[:, 0:128], p[:, 128:256]], axis=0)
        both = jnp.concatenate([both, both], axis=1)
        at = k * 128
        band = jnp.concatenate(
            [bands_ref[at : at + 128, :], bands_ref[1024 + at : 1152 + at, :]], axis=0
        )
        a = dot(both, band)
        a0 = a[0 : channels * ROWS]
        a1 = a[channels * ROWS :]
        out = jnp.concatenate([a0[:, 0:128], a0[:, 128:256] + a1[:, 0:128], a1[:, 128:256]], axis=1)
        for c in range(channels):
            across[c, k * ROWS : (k + 1) * ROWS, :] = out[c * ROWS : (c + 1) * ROWS].astype(BF)
    sky_copy.wait()
    dirty_copy.wait()
    live = lax.broadcasted_iota(jnp.int32, (ROWS, COLS), 0) < live_ref[0]
    none = jnp.zeros((ROWS, 128), F32)
    edge = jnp.zeros((8, WIDE), F32)
    for c in range(channels):
        total = dot(bands_ref[2048:2560, :], across[c], FIRST)
        total = total[0:80] + total[160:240]
        sky = sky_ref[c]
        own = sky + STEP_PRIMAL * dirty_ref[c] - STEP_PRIMAL * dual_ref[c, 0].astype(F32)
        own = jnp.where(live, own, OUTSIDE)
        own = pltpu.roll(jnp.concatenate([own, none], axis=1), 8, 1)
        sky = pltpu.roll(jnp.concatenate([sky, none], axis=1), 8, 1)
        total = total * (-STEP_PRIMAL)
        total = total + jnp.concatenate([edge, own, edge], axis=0)
        total = jnp.where(inside, total, OUTSIDE)
        total = jnp.where(lane < COLS + 2 * RADIUS, total, 0.0)
        sky = jnp.concatenate([edge, sky, edge], axis=0)
        for at, cells in ((c, total), (channels + c, sky)):
            o_ref[at] = cells
            head_ref[at] = cells[0:16].astype(BF)
            tail_ref[at] = cells[64:80].astype(BF)


def edge_kernel(base_ref, before_ref, after_ref, o_ref):
    both = base_ref.shape[0]
    lane = lax.broadcasted_iota(jnp.int32, (80, 128), 1)
    head = jnp.zeros((80, 128), F32)
    tail = jnp.zeros((80, 128), F32)
    for c in range(both):
        o_ref[c, 0:16] = base_ref[c, 0:16] + before_ref[c].astype(F32)
        o_ref[c, 16:64] = base_ref[c, 16:64]
        o_ref[c, 64:80] = base_ref[c, 64:80] + after_ref[c].astype(F32)
        first = o_ref[c, :, 0:128]
        final = o_ref[c, :, 256:384]
        if c < both // 2:
            at = 16 + 16 * c
            head = head + pltpu.roll(jnp.where(lane < 16, first, 0.0), at, 1)
            tail = tail + pltpu.roll(jnp.where(lane < 16, final, 0.0), at, 1)
        else:
            at = 80 + 8 * (c - both // 2)
            head = head + pltpu.roll(jnp.where((lane >= 8) & (lane < 16), first, 0.0), at - 8, 1)
            tail = tail + pltpu.roll(jnp.where(lane < 8, final, 0.0), at, 1)
    o_ref[0, :, 256:384] = o_ref[0, :, 256:384] + head
    o_ref[1, :, 256:384] = o_ref[1, :, 256:384] + tail


def frames_kernel(
    bound_ref,
    where_ref,
    half_ref,
    base_ref,
    dual_ref,
    bands_ref,
    image_ref,
    o_ref,
    image_buf,
    dual_buf,
    probes,
    wide,
    down,
    image_sem,
    dual_sem,
):
    channels = image_buf.shape[0]
    rows = channels * ROWS

    def dual_copy(k):
        return pltpu.make_async_copy(dual_buf.at[k], o_ref.at[:, k], dual_sem.at[k])

    def finish(k, analysis):
        bound = bound_ref[k]
        cand = [dual_ref[c, k].astype(F32) + STEP_DUAL * analysis(c) for c in range(channels)]
        square = cand[0] * cand[0]
        for c in range(1, channels):
            square = square + cand[c] * cand[c]
        factor = bound * lax.rsqrt(jnp.maximum(square, bound * bound))
        for c in range(channels):
            dual_buf[k, c] = (cand[c] * factor).astype(BF)
        dual_copy(k).start()

    wide[...] = jnp.zeros_like(wide)
    me = where_ref[3]
    last = half_ref.shape[0] - 1
    lane = lax.broadcasted_iota(jnp.int32, (80, 128), 1)
    left = half_ref[jnp.maximum(me - 1, 0), :, 256:384].astype(F32)
    left = jnp.where(me > 0, left, 0.0)
    right = half_ref[jnp.minimum(me + 1, last), :, 256:384].astype(F32)
    right = jnp.where(me < last, right, 0.0)
    for c in range(channels):
        gram = half_ref[2 * c].astype(F32) + half_ref[2 * c + 1].astype(F32)
        gram = [gram[:, 0:128], gram[:, 128:256], jnp.where(lane < 16, gram[:, 256:384], 0.0)]
        base = [base_ref[c, :, b * 128 : b * 128 + 128] for b in range(3)]
        sky = [base_ref[channels + c, :, b * 128 : b * 128 + 128] for b in range(3)]
        base[2] = jnp.where(lane < 16, base[2], 0.0)
        at = 16 + 16 * c
        base[0] = base[0] + jnp.where(lane < 16, pltpu.roll(left, 128 - at, 1), 0.0)
        base[2] = base[2] + jnp.where(lane < 16, pltpu.roll(right, 128 - at, 1), 0.0)
        at = 80 + 8 * c
        sky[0] = sky[0] + jnp.where(lane < 8, pltpu.roll(left, 128 - at, 1), 0.0)
        shown = (lane >= 8) & (lane < 16)
        sky[2] = sky[2] + jnp.where(shown, pltpu.roll(right, 136 - at, 1), 0.0)
        image = [jnp.maximum(base[b] - STEP_PRIMAL * gram[b], 0.0) for b in range(3)]
        probe = jnp.concatenate([2.0 * image[b] - sky[b] for b in range(3)], axis=1)
        image = pltpu.roll(jnp.concatenate(image, axis=1), WIDE - 8, 1)
        image_buf[c] = image[8:72, 0:256]
        probes[c] = pltpu.roll(probe, WIDE - 8, 1)[8:72, 0:256]
        high = probe.astype(BF)
        low = (probe - high.astype(F32)).astype(BF)
        wide[0:80, :] = high
        wide[80:160, :] = low
        wide[160:240, :] = high
        d = dot(bands_ref[2048:2560, :], wide[...])
        high = d.astype(BF)
        down[0, c] = high
        down[1, c] = (d - high.astype(F32)).astype(BF)
    image_copy = pltpu.make_async_copy(image_buf, image_ref, image_sem)
    image_copy.start()
    finish(0, lambda c: probes[c])
    for k in range(1, FRAMES + 1):
        at = (k - 1) * ROWS
        a = None
        for t in range(2):
            d = jnp.concatenate([down[t, c, at : at + ROWS, :] for c in range(channels)], axis=0)
            both = jnp.concatenate([d[:, 0:256], d[:, 128:384]], axis=0)
            high = bands_ref[(k - 1) * 128 : k * 128, :]
            if t == 0:
                band = jnp.concatenate([high, bands_ref[896 + k * 128 : 1024 + k * 128, :]], axis=0)
                term = dot(both, band, LAST)
                a = term[:, 0:128] + term[:, 128:256]
            else:
                a = a + dot(both, high, LAST)
        finish(
            k,
            lambda c: jnp.concatenate(
                [a[c * ROWS : c * ROWS + ROWS], a[rows + c * ROWS : rows + c * ROWS + ROWS]], axis=1
            ),
        )
    image_copy.wait()
    for k in range(FRAMES + 1):
        dual_copy(k).wait()


VM = pl.BlockSpec(memory_space=pltpu.VMEM)
SM = pl.BlockSpec(memory_space=pltpu.SMEM)
HB = pl.BlockSpec(memory_space=pltpu.HBM)


def call(kernel, out_shape, scratch, flops, moved, *args, scalars=0, sources=0, result=VM):
    return pl.pallas_call(
        kernel,
        out_shape=out_shape,
        in_specs=[SM] * scalars + [HB] * sources + [VM] * (len(args) - scalars - sources),
        out_specs=jax.tree.map(lambda _: result, out_shape),
        scratch_shapes=scratch,
        compiler_params=pltpu.CompilerParams(vmem_limit_bytes=VMEM_LIMIT),
        cost_estimate=pl.CostEstimate(flops=flops, bytes_accessed=moved, transcendentals=0),
    )(*args)


def frames_call(thresholds, where, halves, base, dual, bands):
    channels = dual.shape[0]
    block = (channels, ROWS, COLS)
    return pl.pallas_call(
        frames_kernel,
        out_shape=(jax.ShapeDtypeStruct(block, F32), jax.ShapeDtypeStruct(dual.shape, BF)),
        in_specs=[SM, SM, VM, VM, VM, VM],
        out_specs=(pl.BlockSpec(memory_space=pl.ANY), pl.BlockSpec(memory_space=pl.ANY)),
        scratch_shapes=[
            pltpu.VMEM(block, F32),
            pltpu.VMEM((FRAMES + 1, *block), BF),
            pltpu.VMEM(block, F32),
            pltpu.VMEM((256, WIDE), BF),
            pltpu.VMEM((2, channels, FRAMES * ROWS, WIDE), BF),
            pltpu.SemaphoreType.DMA(()),
            pltpu.SemaphoreType.DMA((FRAMES + 1,)),
        ],
        compiler_params=pltpu.CompilerParams(vmem_limit_bytes=VMEM_LIMIT),
        cost_estimate=pl.CostEstimate(flops=1 << 31, bytes_accessed=3 << 20, transcendentals=0),
    )(thresholds, where, halves, base, dual, bands)


def after(values, *events):
    return lax.optimization_barrier((*values, *events))[: len(values)]


def body(
    sky_estimate,
    dual_coeffs,
    dirty_image,
    filters,
    thresholds,
    facet_rows,
    tile_slots,
    tile_count,
    gram_tiles,
):
    channels, tile_rows, tile_cols = sky_estimate.shape
    place = lax.axis_index("fou")
    where = jnp.stack([place >> 1, place & 1, lax.axis_index("img"), place]).astype(jnp.int32)

    sent = pl.pallas_call(
        send_kernel,
        out_shape=jax.ShapeDtypeStruct((2 * channels, tile_rows, tile_cols), BF),
        in_specs=[pl.BlockSpec(memory_space=pltpu.HBM)],
        out_specs=pl.BlockSpec(memory_space=pltpu.HBM),
        scratch_shapes=[
            pltpu.VMEM(sky_estimate.shape, F32),
            pltpu.VMEM(sky_estimate.shape, BF),
            pltpu.SemaphoreType.DMA((channels,)),
            pltpu.SemaphoreType.DMA((channels, 2)),
        ],
        compiler_params=pltpu.CompilerParams(vmem_limit_bytes=VMEM_LIMIT),
    )(pltpu.with_memory_space_constraint(sky_estimate, pltpu.HBM))
    lines = lax.all_to_all(sent, "fou", split_axis=0, concat_axis=0, tiled=True)

    taps = jnp.pad(filters, ((0, 0), (0, 256 - filters.shape[1])))
    bands = call(
        bands_kernel, jax.ShapeDtypeStruct((2560, 256), BF), [], 1 << 20, 1 << 20, taps
    )
    (ready_where,) = after((where,), bands)
    line = wave_table()
    held = call(hold_kernel, jax.ShapeDtypeStruct(line.shape, BF), [], 1 << 10, 1 << 20, line)
    packed = call(
        forward_kernel,
        jax.ShapeDtypeStruct((PEERS_IMG, 32, 128), BF),
        [pltpu.VMEM((2, PEERS_IMG, 16, 128), BF), pltpu.SemaphoreType.DMA((2,))],
        1 << 29,
        1 << 20,
        ready_where,
        lines,
        held,
        scalars=1,
        result=HB,
    )
    received = lax.all_to_all(packed, "img", split_axis=0, concat_axis=0, tiled=True)


    ends = jax.ShapeDtypeStruct((2 * channels, 16, WIDE), BF)
    extended = jax.ShapeDtypeStruct((2 * channels, tile_rows + 16, WIDE), F32)
    (late_where,) = after((where,), packed)
    base, head, tail = pl.pallas_call(
        synth_kernel,
        out_shape=(extended, ends, ends),
        in_specs=[SM, SM, VM, HB, HB, VM],
        out_specs=(VM, VM, VM),
        scratch_shapes=[
            pltpu.VMEM(sky_estimate.shape, F32),
            pltpu.VMEM(sky_estimate.shape, F32),
            pltpu.VMEM((channels, FRAMES * ROWS, WIDE), BF),
            pltpu.SemaphoreType.DMA(()),
            pltpu.SemaphoreType.DMA(()),
        ],
        compiler_params=pltpu.CompilerParams(vmem_limit_bytes=VMEM_LIMIT),
        cost_estimate=pl.CostEstimate(flops=1 << 31, bytes_accessed=4 << 20, transcendentals=0),
    )(
        late_where,
        facet_rows,
        dual_coeffs,
        pltpu.with_memory_space_constraint(sky_estimate, pltpu.HBM),
        pltpu.with_memory_space_constraint(dirty_image, pltpu.HBM),
        bands,
    )
    (tiles_where,) = after((where,), head)
    spread = call(
        tiles_kernel,
        jax.ShapeDtypeStruct((320, 1536), BF),
        [],
        1 << 23,
        1 << 20,
        tiles_where,
        tile_slots,
        tile_count,
        gram_tiles,
        sampled_table(),
        scalars=3,
    )
    steps = [(i, i + 1) for i in range(PEERS_IMG - 1)]
    from_after = lax.ppermute(head, "img", [(j, i) for i, j in steps])
    (received,) = after((received,), from_after)

    scratch = [
        pltpu.VMEM((4, 8, 32, 128), BF),
        pltpu.VMEM((1280, 128), F32),
        pltpu.VMEM((64, 2048), BF),
        pltpu.VMEM((256, 1024), BF),
        pltpu.VMEM((64, 1024), BF),
        pltpu.VMEM((2, 16, 40, 128), BF),
        pltpu.SemaphoreType.DMA((4,)),
        pltpu.SemaphoreType.DMA((2,)),
    ]
    weighted = call(
        gram_kernel,
        jax.ShapeDtypeStruct((PEERS_IMG, 40, 128), BF),
        scratch,
        1 << 29,
        1 << 20,
        pltpu.with_memory_space_constraint(received, pltpu.HBM),
        spread,
        result=HB,
        sources=1,
    )
    returned = lax.all_to_all(weighted, "img", split_axis=0, concat_axis=0, tiled=True)

    (late_taps,) = after((taps,), weighted)
    late_bands = call(
        bands_kernel, jax.ShapeDtypeStruct((2560, 256), BF), [], 1 << 20, 1 << 20, late_taps
    )
    (last_where,) = after((where,), late_bands)
    (tail,) = after((tail,), weighted)
    from_before = lax.ppermute(tail, "img", steps)
    base = call(
        edge_kernel,
        extended,
        [],
        1 << 20,
        4 << 20,
        base,
        from_before,
        from_after,
    )
    blocks = call(
        inverse_kernel,
        jax.ShapeDtypeStruct((8, tile_rows + 16, WIDE), BF),
        [],
        1 << 29,
        1 << 20,
        last_where,
        returned,
        line,
        base,
        scalars=1,
    )
    halves = lax.all_to_all(blocks, "fou", split_axis=0, concat_axis=0, tiled=True)

    return frames_call(thresholds, where, halves, base, dual_coeffs, late_bands)


def solution(mesh):
    in_specs = (
        P(None, "img", "fou"),
        P(None, None, "img", "fou"),
        P(None, "img", "fou"),
        P(),
        P(),
        P("img"),
        P(None, "img", None),
        P(None, "img"),
        P(None, "img", None, None, None),
    )
    out_specs = (P(None, "img", "fou"), P(None, None, "img", "fou"))
    return jax.shard_map(body, mesh=mesh, in_specs=in_specs, out_specs=out_specs, check_vma=False)
```

```python
import math

import jax
import jax.numpy as jnp
import numpy as np
from jax import lax
from jax.experimental import pallas as pl
from jax.experimental.pallas import tpu as pltpu
from jax.sharding import PartitionSpec as P

PIXELS = 2048
RADIUS = 8
SLOTS = 6
ROWS = 64
COLS = 256
FRAMES = 8
PEERS_IMG = 32
STEP_PRIMAL = 0.5
STEP_DUAL = 0.5
BF = jnp.bfloat16
F32 = jnp.float32
VMEM_LIMIT = 20 << 20
WIDE = 384
OUTSIDE = -1.0e30
LAST = ((1,), (1,))
FIRST = ((0,), (0,))


def two_terms_np(table):
    high = table.astype(jnp.bfloat16)
    low = (table - high.astype(np.float64)).astype(jnp.bfloat16)
    return high, low


def two_terms(table):
    high = table.astype(BF)
    return high, (table - high.astype(F32)).astype(BF)


def dot(a, b, dims=((1,), (0,))):
    return lax.dot_general(a, b, (dims, ((), ())), preferred_element_type=F32)


def angle_np(a, b, period):
    return 2.0 * np.pi * ((a[:, None] * b[None, :]) % period) / period


def line_table():
    ang = angle_np(np.arange(256), np.arange(256), 256)
    return two_terms_np(np.concatenate([np.cos(ang), np.sin(ang)], axis=1))


def block_table():
    ang = angle_np(np.arange(32), np.arange(32), 32)
    c, s = np.cos(ang), np.sin(ang)
    return two_terms_np(np.block([[c, s], [-s, c]]))


HALO = np.concatenate([np.arange(-8, 0), np.arange(64, 72)])


def turn_table():
    main = np.tile(np.arange(64), 2)
    halo = np.tile(HALO, 8)
    ang = [angle_np(np.arange(64), r, 2048) for r in (main, halo)]
    return two_terms_np(
        np.concatenate([np.cos(ang[0]), np.sin(ang[0]), np.cos(ang[1]), np.sin(ang[1])])
    )


def fixed_table():
    turns = [np.concatenate(np.split(t, 4), axis=1) for t in turn_table()]
    return np.concatenate([*block_table(), *turns], axis=1)


def sampled_table():
    fixed = fixed_table()
    rest = np.zeros((64, 768), fixed.dtype)
    rest[:, 0:384] = fixed[:, 768:1152]
    return np.concatenate([*tile_table(), fixed[:, 0:768], rest], axis=0)


def tile_table():
    t = np.arange(32)
    ang = angle_np(t, np.arange(64), 32)
    c, s = np.cos(ang), np.sin(ang)
    main = np.zeros((32, 2, 2, 2, 2, 64))
    for p in range(2):
        main[:, p, 0, 0, p] = c
        main[:, p, 1, 0, p] = -s
        main[:, p, 0, 1, p] = s
        main[:, p, 1, 1, p] = c
    ang = angle_np(t, HALO, 32)
    c, s = np.cos(ang), np.sin(ang)
    halo = np.zeros((32, 2, 2, 2, 2, 2, 2, 2, 16))
    for p in range(2):
        for x in range(2):
            halo[:, p, 0, x, 0, 0, x, p] = c
            halo[:, p, 1, x, 0, 0, x, p] = -s
            halo[:, p, 0, x, 1, 0, x, p] = s
            halo[:, p, 1, x, 1, 0, x, p] = c
            halo[:, p, 0, x, 0, 1, x, p] = s
            halo[:, p, 1, x, 0, 1, x, p] = c
            halo[:, p, 0, x, 1, 1, x, p] = -c
            halo[:, p, 1, x, 1, 1, x, p] = s
    table = np.concatenate([main.reshape(128, 256), halo.reshape(128, 512)], axis=1)
    return two_terms_np(table)


def wave_table():
    freq = np.arange(2)[:, None] + 2 * np.arange(4)[None]
    pos = np.arange(4 * COLS).reshape(4, COLS)
    ang = 2.0 * np.pi * ((freq[:, :, None, None] * pos) % PIXELS) / PIXELS
    fold = np.concatenate([np.cos(ang), np.sin(ang)], axis=3).reshape(32, 2 * COLS)
    return np.concatenate([np.stack(line_table()), np.stack(two_terms_np(fold))], axis=1)


def fold_rows(line_ref, par):
    at = pl.multiple_of(256 + 16 * par, 16)
    fold = line_ref[0, pl.ds(at, 16), :].astype(F32) + line_ref[1, pl.ds(at, 16), :].astype(F32)
    return fold[:, 0:256], fold[:, 256:512]


def hold_kernel(table_ref, o_ref):
    o_ref[...] = table_ref[...]


def send_kernel(sky_ref, o_ref, taken, rounded, in_sem, out_sem):
    channels = taken.shape[0]

    def fetch(c):
        return pltpu.make_async_copy(sky_ref.at[c], taken.at[c], in_sem.at[c])

    def place(c, h):
        return pltpu.make_async_copy(rounded.at[c], o_ref.at[2 * c + h], out_sem.at[c, h])

    for c in range(channels):
        fetch(c).start()
    for c in range(channels):
        fetch(c).wait()
        rounded[c] = taken[c].astype(BF)
        for h in range(2):
            place(c, h).start()
    for c in range(channels):
        for h in range(2):
            place(c, h).wait()


def forward_kernel(par_ref, x_ref, line_ref, o_ref, out, sem):
    par = par_ref[1]
    folds = fold_rows(line_ref, par)
    sign = (1 - 2 * par).astype(F32)
    xe = [x_ref[f].astype(F32) + sign * x_ref[f + 4].astype(F32) for f in range(4)]
    rows = [[], []]
    for cls in range(4):
        cos = folds[0][cls * 4 : cls * 4 + 4]
        sin = folds[1][cls * 4 : cls * 4 + 4]
        yr = xe[0] * cos[0:1]
        yi = xe[0] * sin[0:1]
        for f in range(1, 4):
            yr = yr + xe[f] * cos[f : f + 1]
            yi = yi + xe[f] * sin[f : f + 1]
        rows[0].append(jnp.concatenate([yr, -yi], axis=1).astype(BF))
        rows[1].append(jnp.concatenate([-yi, -yr], axis=1).astype(BF))
    def leave(n):
        return pltpu.make_async_copy(out.at[n], o_ref.at[pl.ds(n * 8, 8)], sem.at[n])

    parts = []
    for part in range(2):
        r = jnp.concatenate(rows[part], axis=0)
        wave = dot(line_ref[0, 0:256], r, LAST) + dot(line_ref[1, 0:256], r, LAST)
        both = [wave[:, chi * 128 : chi * 128 + 128].reshape(32, 8, 128) for chi in range(2)]
        parts.append(jnp.concatenate(both, axis=1))
    for n in range(4):
        piece = [part[n * 8 : n * 8 + 8] for part in parts]
        out[n] = jnp.concatenate(piece, axis=1).astype(BF)
        leave(n).start()
    for n in range(4):
        leave(n).wait()


def inverse_kernel(par_ref, t_ref, line_ref, base_ref, o_ref):
    par = par_ref[1]
    folds = fold_rows(line_ref, par)
    me = par_ref[3]
    sign = (1 - 2 * par).astype(F32)
    re = t_ref[:, 0:16, :].astype(F32)
    im = t_ref[:, 16:32, :].astype(F32)
    edge = t_ref[:, 32:40, :].astype(F32)
    data = [re[:, 0:8], im[:, 0:8], re[:, 8:16], im[:, 8:16], edge]
    data = jnp.concatenate([d.reshape(256, 128).astype(BF) for d in data], axis=1)
    wave = dot(data, line_ref[0, 0:256], FIRST) + dot(data, line_ref[1, 0:256], FIRST)

    def joined(a, b):
        return jnp.concatenate([a[:, 0:256] - b[:, 256:512], a[:, 256:512] + b[:, 0:256]], axis=1)

    h = joined(wave[512:576], wave[576:640])
    total = [None] * 4
    for chi in range(2):
        u = joined(wave[chi * 256 : chi * 256 + 128], wave[chi * 256 + 128 : chi * 256 + 256])
        for clo in range(2):
            cls = 2 * chi + clo
            e = h[cls * 16 : cls * 16 + 16]
            whole = jnp.concatenate([e[0:8], u[clo * 64 : clo * 64 + 64], e[8:16]], axis=0)
            ur = whole[:, 0:256]
            ui = whole[:, 256:512]
            cos = folds[0][cls * 4 : cls * 4 + 4]
            sin = folds[1][cls * 4 : cls * 4 + 4]
            for f in range(4):
                g = ur * cos[f : f + 1] - ui * sin[f : f + 1]
                total[f] = g if total[f] is None else total[f] + g
    scale = 1.0 / (PIXELS * PIXELS)
    total = [g * scale for g in total]
    total = total + [sign * g for g in total]
    none = jnp.zeros((80, 128), F32)
    lane = lax.broadcasted_iota(jnp.int32, (80, 128), 1)
    for f in range(8):
        before = total[f - 1][:, 128:256] if f > 0 else none
        after = total[f + 1][:, 0:128] if f < 7 else none
        line = jnp.concatenate([before, total[f], after], axis=1)
        line = pltpu.roll(line, 512 - 120, 1)
        pack = jnp.where(f == me - 1, base_ref[0, :, 256:384], 0.0)
        pack = pack + jnp.where(f == me + 1, base_ref[1, :, 256:384], 0.0)
        o_ref[f, :, 0:256] = line[:, 0:256].astype(BF)
        o_ref[f, :, 256:384] = jnp.where(lane < 16, line[:, 256:384], pack).astype(BF)


def tiles_kernel(where_ref, slots_ref, count_ref, tiles_ref, table_ref, o_ref):
    channel = where_ref[0]
    left = lax.broadcasted_iota(jnp.int32, (32, 128), 0)
    right = lax.broadcasted_iota(jnp.int32, (32, 128), 1)
    tile = jnp.full((32, 128), -1, jnp.int32)
    for k in range(SLOTS):
        slot = jnp.where(k < count_ref[channel, 0], slots_ref[channel, 0, k], -1)
        tile = jnp.where(left // 4 == k, slot, tile)
    pick = (tile == right // 4) & (left % 4 == right % 4)
    pick = jnp.where(pick, 1.0, 0.0).astype(BF)
    o_ref[...] = jnp.zeros_like(o_ref)
    for k in range(0, SLOTS, 2):
        pair = [tiles_ref[channel, 0, k + n].astype(F32).T for n in range(2)]
        o_ref[256:320, k * 64 : k * 64 + 128] = jnp.concatenate(pair, axis=1).astype(BF)
    o_ref[256:320, 384:1152] = table_ref[256:320, :]
    o_ref[256:320, 1152:1536] = table_ref[320:384, 0:384]
    for t in range(2):
        row = dot(pick, table_ref[t * 128 : t * 128 + 128, :]).astype(BF)
        for j in range(2):
            for chi in range(2):
                p = 2 * j + chi
                rows = slice(t * 128 + p * 32, t * 128 + p * 32 + 32)
                o_ref[rows, p * 256 : p * 256 + 256] = row[:, 0:256]
                for comp in range(2):
                    at = 256 + chi * 256 + comp * 128
                    to = 1024 + comp * 256 + j * 128
                    o_ref[rows, to : to + 128] = row[:, at : at + 128]


def gram_kernel(d_ref, e_ref, o_ref, rows, rhs, mid, edge, out, sem):
    rows[0:1024, :] = d_ref[...].reshape(1024, 128).astype(F32)
    for p in range(16):
        lanes = slice(p * 128, p * 128 + 128)
        at = (p % 2) * 8 + p // 2
        rhs[0:32, lanes] = rows[pl.ds(at, 32, stride=32), :].astype(BF)
        rhs[32:64, lanes] = rows[pl.ds(16 + at, 32, stride=32), :].astype(BF)
    fixed = e_ref[256:320, :]
    block = [fixed[:, 384:448], fixed[:, 448:512]]
    turns = fixed[:, 512:1024].astype(F32) + fixed[:, 1024:1536].astype(F32)
    tc, ts, ec, es = (turns[:, n * 128 : n * 128 + 128] for n in range(4))
    first = dot(jnp.concatenate(block, axis=0), rhs[...])
    first = first[0:64] + first[64:128]
    for p in range(16):
        g = first[:, p * 128 : p * 128 + 128]
        gr = jnp.concatenate([g[0:32], g[0:32]], axis=0)
        gi = jnp.concatenate([g[32:64], g[32:64]], axis=0)
        down = slice(p // 4 * 64, p // 4 * 64 + 64)
        at = p % 4 * 256
        mid[down, at : at + 128] = (gr * tc + gi * ts).astype(BF)
        mid[down, at + 128 : at + 256] = (gi * tc - gr * ts).astype(BF)
    spec = dot(mid[...], e_ref[0:256, 0:1024], LAST)
    spec = (spec[:, 0:128] + spec[:, 128:256]).astype(BF)
    spec = jnp.concatenate([spec[g * 64 : g * 64 + 64] for g in range(4)], axis=1)
    tiles = [fixed[:, k * 64 : k * 64 + 64] for k in range(SLOTS)]
    mixed = dot(jnp.concatenate(tiles, axis=0), spec)
    lane_slot = (lax.broadcasted_iota(jnp.int32, (64, 512), 1) % 32) // 4
    weighted = jnp.where(lane_slot == 0, mixed[0:64], 0.0)
    for k in range(1, SLOTS):
        weighted = jnp.where(lane_slot == k, mixed[k * 64 : k * 64 + 64], weighted)
    weighted = weighted.astype(BF)
    w = jnp.concatenate([weighted[:, g * 128 : g * 128 + 128] for g in range(4)], axis=0)
    spreads = dot(jnp.concatenate([w, w], axis=1), e_ref[0:256, :])
    for g in range(4):
        z = spreads[g * 64 : g * 64 + 64]
        for v in range(4):
            p = g * 4 + v
            zr = z[:, v * 256 : v * 256 + 128]
            zi = z[:, v * 256 + 128 : v * 256 + 256]
            hr = zr * tc - zi * ts
            hi = zi * tc + zr * ts
            rhs[0:32, p * 128 : p * 128 + 128] = (hr[0:32] + hr[32:64]).astype(BF)
            rhs[32:64, p * 128 : p * 128 + 128] = (hi[0:32] + hi[32:64]).astype(BF)
        for j in range(2):
            zr = z[:, 1024 + j * 128 : 1152 + j * 128]
            zi = z[:, 1280 + j * 128 : 1408 + j * 128]
            hr = zr * ec - zi * es
            hi = zi * ec + zr * es
            lanes = slice((2 * g + j) * 128, (2 * g + j) * 128 + 128)
            edge[0:32, lanes] = (hr[0:32] + hr[32:64]).astype(BF)
            edge[32:64, lanes] = (hi[0:32] + hi[32:64]).astype(BF)
    block = jnp.concatenate(block, axis=1)
    last = dot(block, rhs[...], FIRST)
    last = last[0:64] + last[64:128]
    outer = dot(block, edge[...], FIRST)
    outer = outer[0:32] + outer[64:96]
    for p in range(16):
        lanes = slice(p * 128, p * 128 + 128)
        at = (p % 2) * 8 + p // 2
        rows[pl.ds(at, 32, stride=40), :] = last[0:32, lanes]
        rows[pl.ds(16 + at, 32, stride=40), :] = last[32:64, lanes]
    for v in range(8):
        rows[pl.ds(32 + v, 32, stride=40), :] = outer[:, v * 128 : v * 128 + 128]
    leave = []
    for n in range(2):
        half = rows[n * 640 : n * 640 + 640, :]
        out[n] = half.reshape(16, 40, 128).astype(BF)
        to = o_ref.at[pl.ds(n * 16, 16)]
        leave.append(pltpu.make_async_copy(out.at[n], to, sem.at[n]))
        leave[n].start()
    for n in range(2):
        leave[n].wait()


def bands_kernel(taps_ref, o_ref):
    lane = lax.broadcasted_iota(jnp.int32, (64, 256), 1)
    for k in range(FRAMES):
        wide = jnp.broadcast_to(taps_ref[k : k + 1, :], (128, 256))
        band = pltpu.roll(wide, 0, 1, stride=1, stride_axis=0)
        high = band.astype(BF)
        low = band - high.astype(F32)
        o_ref[k * 128 : k * 128 + 128, :] = high
        o_ref[1024 + k * 128 : 1152 + k * 128, :] = low.astype(BF)
        low = jnp.where(lane < 80, low[0:64], 0.0)
        high = jnp.where(lane < 80, high[0:64].astype(F32), 0.0)
        row = high + pltpu.roll(high, 80, 1) + pltpu.roll(low, 160, 1)
        o_ref[2048 + k * 64 : 2112 + k * 64, :] = row.astype(BF)


def synth_kernel(
    where_ref,
    live_ref,
    dual_ref,
    sky_hbm,
    dirty_hbm,
    bands_ref,
    o_ref,
    head_ref,
    tail_ref,
    sky_ref,
    dirty_ref,
    across,
    sky_sem,
    dirty_sem,
):
    channels = sky_ref.shape[0]
    sky_copy = pltpu.make_async_copy(sky_hbm, sky_ref, sky_sem)
    sky_copy.start()
    dirty_copy = pltpu.make_async_copy(dirty_hbm, dirty_ref, dirty_sem)
    dirty_copy.start()
    row = lax.broadcasted_iota(jnp.int32, (80, WIDE), 0) + where_ref[2] * ROWS - RADIUS
    lane = lax.broadcasted_iota(jnp.int32, (80, WIDE), 1)
    col = lane + where_ref[3] * COLS - RADIUS
    inside = (row >= 0) & (row < PIXELS) & (col >= 0) & (col < PIXELS)
    for k in range(FRAMES):
        p = dual_ref[:, k + 1].reshape(channels * ROWS, COLS)
        both = jnp.concatenate([p[:, 0:128], p[:, 128:256]], axis=0)
        both = jnp.concatenate([both, both], axis=1)
        at = k * 128
        band = jnp.concatenate(
            [bands_ref[at : at + 128, :], bands_ref[1024 + at : 1152 + at, :]], axis=0
        )
        a = dot(both, band)
        a0 = a[0 : channels * ROWS]
        a1 = a[channels * ROWS :]
        out = jnp.concatenate([a0[:, 0:128], a0[:, 128:256] + a1[:, 0:128], a1[:, 128:256]], axis=1)
        for c in range(channels):
            across[c, k * ROWS : (k + 1) * ROWS, :] = out[c * ROWS : (c + 1) * ROWS].astype(BF)
    sky_copy.wait()
    dirty_copy.wait()
    live = lax.broadcasted_iota(jnp.int32, (ROWS, COLS), 0) < live_ref[0]
    none = jnp.zeros((ROWS, 128), F32)
    edge = jnp.zeros((8, WIDE), F32)
    for c in range(channels):
        total = dot(bands_ref[2048:2560, :], across[c], FIRST)
        total = total[0:80] + total[160:240]
        sky = sky_ref[c]
        own = sky + STEP_PRIMAL * dirty_ref[c] - STEP_PRIMAL * dual_ref[c, 0].astype(F32)
        own = jnp.where(live, own, OUTSIDE)
        own = pltpu.roll(jnp.concatenate([own, none], axis=1), 8, 1)
        sky = pltpu.roll(jnp.concatenate([sky, none], axis=1), 8, 1)
        total = total * (-STEP_PRIMAL)
        total = total + jnp.concatenate([edge, own, edge], axis=0)
        total = jnp.where(inside, total, OUTSIDE)
        total = jnp.where(lane < COLS + 2 * RADIUS, total, 0.0)
        sky = jnp.concatenate([edge, sky, edge], axis=0)
        for at, cells in ((c, total), (channels + c, sky)):
            o_ref[at] = cells
            head_ref[at] = cells[0:16].astype(BF)
            tail_ref[at] = cells[64:80].astype(BF)


def edge_kernel(base_ref, before_ref, after_ref, o_ref):
    both = base_ref.shape[0]
    lane = lax.broadcasted_iota(jnp.int32, (80, 128), 1)
    head = jnp.zeros((80, 128), F32)
    tail = jnp.zeros((80, 128), F32)
    for c in range(both):
        o_ref[c, 0:16] = base_ref[c, 0:16] + before_ref[c].astype(F32)
        o_ref[c, 16:64] = base_ref[c, 16:64]
        o_ref[c, 64:80] = base_ref[c, 64:80] + after_ref[c].astype(F32)
        first = o_ref[c, :, 0:128]
        final = o_ref[c, :, 256:384]
        if c < both // 2:
            at = 16 + 16 * c
            head = head + pltpu.roll(jnp.where(lane < 16, first, 0.0), at, 1)
            tail = tail + pltpu.roll(jnp.where(lane < 16, final, 0.0), at, 1)
        else:
            at = 80 + 8 * (c - both // 2)
            head = head + pltpu.roll(jnp.where((lane >= 8) & (lane < 16), first, 0.0), at - 8, 1)
            tail = tail + pltpu.roll(jnp.where(lane < 8, final, 0.0), at, 1)
    o_ref[0, :, 256:384] = o_ref[0, :, 256:384] + head
    o_ref[1, :, 256:384] = o_ref[1, :, 256:384] + tail


def frames_kernel(
    bound_ref,
    where_ref,
    half_ref,
    base_ref,
    dual_ref,
    bands_ref,
    image_ref,
    o_ref,
    image_buf,
    dual_buf,
    probes,
    wide,
    down,
    image_sem,
    dual_sem,
):
    channels = image_buf.shape[0]
    rows = channels * ROWS

    def dual_copy(k):
        return pltpu.make_async_copy(dual_buf.at[k], o_ref.at[:, k], dual_sem.at[k])

    def finish(k, analysis):
        bound = bound_ref[k]
        cand = [dual_ref[c, k].astype(F32) + STEP_DUAL * analysis(c) for c in range(channels)]
        square = cand[0] * cand[0]
        for c in range(1, channels):
            square = square + cand[c] * cand[c]
        factor = bound * lax.rsqrt(jnp.maximum(square, bound * bound))
        for c in range(channels):
            dual_buf[k, c] = (cand[c] * factor).astype(BF)
        dual_copy(k).start()

    wide[...] = jnp.zeros_like(wide)
    me = where_ref[3]
    last = half_ref.shape[0] - 1
    lane = lax.broadcasted_iota(jnp.int32, (80, 128), 1)
    left = half_ref[jnp.maximum(me - 1, 0), :, 256:384].astype(F32)
    left = jnp.where(me > 0, left, 0.0)
    right = half_ref[jnp.minimum(me + 1, last), :, 256:384].astype(F32)
    right = jnp.where(me < last, right, 0.0)
    for c in range(channels):
        gram = half_ref[2 * c].astype(F32) + half_ref[2 * c + 1].astype(F32)
        gram = [gram[:, 0:128], gram[:, 128:256], jnp.where(lane < 16, gram[:, 256:384], 0.0)]
        base = [base_ref[c, :, b * 128 : b * 128 + 128] for b in range(3)]
        sky = [base_ref[channels + c, :, b * 128 : b * 128 + 128] for b in range(3)]
        base[2] = jnp.where(lane < 16, base[2], 0.0)
        at = 16 + 16 * c
        base[0] = base[0] + jnp.where(lane < 16, pltpu.roll(left, 128 - at, 1), 0.0)
        base[2] = base[2] + jnp.where(lane < 16, pltpu.roll(right, 128 - at, 1), 0.0)
        at = 80 + 8 * c
        sky[0] = sky[0] + jnp.where(lane < 8, pltpu.roll(left, 128 - at, 1), 0.0)
        shown = (lane >= 8) & (lane < 16)
        sky[2] = sky[2] + jnp.where(shown, pltpu.roll(right, 136 - at, 1), 0.0)
        image = [jnp.maximum(base[b] - STEP_PRIMAL * gram[b], 0.0) for b in range(3)]
        probe = jnp.concatenate([2.0 * image[b] - sky[b] for b in range(3)], axis=1)
        image = pltpu.roll(jnp.concatenate(image, axis=1), WIDE - 8, 1)
        image_buf[c] = image[8:72, 0:256]
        probes[c] = pltpu.roll(probe, WIDE - 8, 1)[8:72, 0:256]
        high = probe.astype(BF)
        low = (probe - high.astype(F32)).astype(BF)
        wide[0:80, :] = high
        wide[80:160, :] = low
        wide[160:240, :] = high
        d = dot(bands_ref[2048:2560, :], wide[...])
        high = d.astype(BF)
        down[0, c] = high
        down[1, c] = (d - high.astype(F32)).astype(BF)
    image_copy = pltpu.make_async_copy(image_buf, image_ref, image_sem)
    image_copy.start()
    finish(0, lambda c: probes[c])
    for k in range(1, FRAMES + 1):
        at = (k - 1) * ROWS
        a = None
        for t in range(2):
            d = jnp.concatenate([down[t, c, at : at + ROWS, :] for c in range(channels)], axis=0)
            both = jnp.concatenate([d[:, 0:256], d[:, 128:384]], axis=0)
            high = bands_ref[(k - 1) * 128 : k * 128, :]
            if t == 0:
                band = jnp.concatenate([high, bands_ref[896 + k * 128 : 1024 + k * 128, :]], axis=0)
                term = dot(both, band, LAST)
                a = term[:, 0:128] + term[:, 128:256]
            else:
                a = a + dot(both, high, LAST)
        finish(
            k,
            lambda c: jnp.concatenate(
                [a[c * ROWS : c * ROWS + ROWS], a[rows + c * ROWS : rows + c * ROWS + ROWS]], axis=1
            ),
        )
    image_copy.wait()
    for k in range(FRAMES + 1):
        dual_copy(k).wait()


VM = pl.BlockSpec(memory_space=pltpu.VMEM)
SM = pl.BlockSpec(memory_space=pltpu.SMEM)
HB = pl.BlockSpec(memory_space=pltpu.HBM)


def call(kernel, out_shape, scratch, flops, moved, *args, scalars=0, result=VM):
    return pl.pallas_call(
        kernel,
        out_shape=out_shape,
        in_specs=[SM] * scalars + [VM] * (len(args) - scalars),
        out_specs=jax.tree.map(lambda _: result, out_shape),
        scratch_shapes=scratch,
        compiler_params=pltpu.CompilerParams(vmem_limit_bytes=VMEM_LIMIT),
        cost_estimate=pl.CostEstimate(flops=flops, bytes_accessed=moved, transcendentals=0),
    )(*args)


def frames_call(thresholds, where, halves, base, dual, bands):
    channels = dual.shape[0]
    block = (channels, ROWS, COLS)
    return pl.pallas_call(
        frames_kernel,
        out_shape=(jax.ShapeDtypeStruct(block, F32), jax.ShapeDtypeStruct(dual.shape, BF)),
        in_specs=[SM, SM, VM, VM, VM, VM],
        out_specs=(pl.BlockSpec(memory_space=pl.ANY), pl.BlockSpec(memory_space=pl.ANY)),
        scratch_shapes=[
            pltpu.VMEM(block, F32),
            pltpu.VMEM((FRAMES + 1, *block), BF),
            pltpu.VMEM(block, F32),
            pltpu.VMEM((256, WIDE), BF),
            pltpu.VMEM((2, channels, FRAMES * ROWS, WIDE), BF),
            pltpu.SemaphoreType.DMA(()),
            pltpu.SemaphoreType.DMA((FRAMES + 1,)),
        ],
        compiler_params=pltpu.CompilerParams(vmem_limit_bytes=VMEM_LIMIT),
        cost_estimate=pl.CostEstimate(flops=1 << 31, bytes_accessed=3 << 20, transcendentals=0),
    )(thresholds, where, halves, base, dual, bands)


def after(values, *events):
    return lax.optimization_barrier((*values, *events))[: len(values)]


def body(
    sky_estimate,
    dual_coeffs,
    dirty_image,
    filters,
    thresholds,
    facet_rows,
    tile_slots,
    tile_count,
    gram_tiles,
):
    channels, tile_rows, tile_cols = sky_estimate.shape
    place = lax.axis_index("fou")
    where = jnp.stack([place >> 1, place & 1, lax.axis_index("img"), place]).astype(jnp.int32)

    sent = pl.pallas_call(
        send_kernel,
        out_shape=jax.ShapeDtypeStruct((2 * channels, tile_rows, tile_cols), BF),
        in_specs=[pl.BlockSpec(memory_space=pltpu.HBM)],
        out_specs=pl.BlockSpec(memory_space=pltpu.HBM),
        scratch_shapes=[
            pltpu.VMEM(sky_estimate.shape, F32),
            pltpu.VMEM(sky_estimate.shape, BF),
            pltpu.SemaphoreType.DMA((channels,)),
            pltpu.SemaphoreType.DMA((channels, 2)),
        ],
        compiler_params=pltpu.CompilerParams(vmem_limit_bytes=VMEM_LIMIT),
    )(pltpu.with_memory_space_constraint(sky_estimate, pltpu.HBM))
    lines = lax.all_to_all(sent, "fou", split_axis=0, concat_axis=0, tiled=True)

    taps = jnp.pad(filters, ((0, 0), (0, 256 - filters.shape[1])))
    bands = call(
        bands_kernel, jax.ShapeDtypeStruct((2560, 256), BF), [], 1 << 20, 1 << 20, taps
    )
    (ready_where,) = after((where,), bands)
    line = wave_table()
    held = call(hold_kernel, jax.ShapeDtypeStruct(line.shape, BF), [], 1 << 10, 1 << 20, line)
    packed = call(
        forward_kernel,
        jax.ShapeDtypeStruct((PEERS_IMG, 32, 128), BF),
        [pltpu.VMEM((4, 8, 32, 128), BF), pltpu.SemaphoreType.DMA((4,))],
        1 << 29,
        1 << 20,
        ready_where,
        lines,
        held,
        scalars=1,
        result=HB,
    )
    received = lax.all_to_all(packed, "img", split_axis=0, concat_axis=0, tiled=True)


    ends = jax.ShapeDtypeStruct((2 * channels, 16, WIDE), BF)
    extended = jax.ShapeDtypeStruct((2 * channels, tile_rows + 16, WIDE), F32)
    (late_where,) = after((where,), packed)
    base, head, tail = pl.pallas_call(
        synth_kernel,
        out_shape=(extended, ends, ends),
        in_specs=[SM, SM, VM, HB, HB, VM],
        out_specs=(VM, VM, VM),
        scratch_shapes=[
            pltpu.VMEM(sky_estimate.shape, F32),
            pltpu.VMEM(sky_estimate.shape, F32),
            pltpu.VMEM((channels, FRAMES * ROWS, WIDE), BF),
            pltpu.SemaphoreType.DMA(()),
            pltpu.SemaphoreType.DMA(()),
        ],
        compiler_params=pltpu.CompilerParams(vmem_limit_bytes=VMEM_LIMIT),
        cost_estimate=pl.CostEstimate(flops=1 << 31, bytes_accessed=4 << 20, transcendentals=0),
    )(
        late_where,
        facet_rows,
        dual_coeffs,
        pltpu.with_memory_space_constraint(sky_estimate, pltpu.HBM),
        pltpu.with_memory_space_constraint(dirty_image, pltpu.HBM),
        bands,
    )
    (tiles_where,) = after((where,), head)
    spread = call(
        tiles_kernel,
        jax.ShapeDtypeStruct((320, 1536), BF),
        [],
        1 << 23,
        1 << 20,
        tiles_where,
        tile_slots,
        tile_count,
        gram_tiles,
        sampled_table(),
        scalars=3,
    )
    (received,) = after((received,), head)

    scratch = [
        pltpu.VMEM((1280, 128), F32),
        pltpu.VMEM((64, 2048), BF),
        pltpu.VMEM((256, 1024), BF),
        pltpu.VMEM((64, 1024), BF),
        pltpu.VMEM((2, 16, 40, 128), BF),
        pltpu.SemaphoreType.DMA((2,)),
    ]
    weighted = call(
        gram_kernel,
        jax.ShapeDtypeStruct((PEERS_IMG, 40, 128), BF),
        scratch,
        1 << 29,
        1 << 20,
        received,
        spread,
        result=HB,
    )
    returned = lax.all_to_all(weighted, "img", split_axis=0, concat_axis=0, tiled=True)

    (late_taps,) = after((taps,), weighted)
    late_bands = call(
        bands_kernel, jax.ShapeDtypeStruct((2560, 256), BF), [], 1 << 20, 1 << 20, late_taps
    )
    (last_where,) = after((where,), late_bands)
    (tail,) = after((tail,), weighted)
    steps = [(i, i + 1) for i in range(PEERS_IMG - 1)]
    from_before = lax.ppermute(tail, "img", steps)
    from_after = lax.ppermute(head, "img", [(j, i) for i, j in steps])
    base = call(
        edge_kernel,
        extended,
        [],
        1 << 20,
        4 << 20,
        base,
        from_before,
        from_after,
    )
    blocks = call(
        inverse_kernel,
        jax.ShapeDtypeStruct((8, tile_rows + 16, WIDE), BF),
        [],
        1 << 29,
        1 << 20,
        last_where,
        returned,
        line,
        base,
        scalars=1,
    )
    halves = lax.all_to_all(blocks, "fou", split_axis=0, concat_axis=0, tiled=True)

    return frames_call(thresholds, where, halves, base, dual_coeffs, late_bands)


def solution(mesh):
    in_specs = (
        P(None, "img", "fou"),
        P(None, None, "img", "fou"),
        P(None, "img", "fou"),
        P(),
        P(),
        P("img"),
        P(None, "img", None),
        P(None, "img"),
        P(None, "img", None, None, None),
    )
    out_specs = (P(None, "img", "fou"), P(None, None, "img", "fou"))
    return jax.shard_map(body, mesh=mesh, in_specs=in_specs, out_specs=out_specs, check_vma=False)
```
